32 devices in a mesh: dp: 8 (over z, y), tensor: 4 (over x, core).
Axes of the slice: x: 2, y: 2, z: 4, core: 2. Of those that a mesh axis runs over, the one named last changes fastest.
Arguments:
- tokens: bfloat16 [8192, 768], P(('dp', 'tensor')), may hold values from -6 to 6
- qkv_weight: bfloat16 [2, 768, 3, 768], P(None, None, None, 'tensor'), may hold values from -0.21875 to 0.21875
- qv_bias: bfloat16 [2, 2, 768], P(None, None, 'tensor'), may hold values from -3 to 3
- out_weight: bfloat16 [2, 768, 768], P(None, 'tensor'), may hold values from -0.625 to 0.625
- up_weight: bfloat16 [2, 768, 3072], P(None, None, 'tensor'), may hold values from -0.21875 to 0.21875
- up_bias: bfloat16 [2, 3072], P(None, 'tensor'), may hold values from -3 to 3
- down_weight: bfloat16 [2, 3072, 768], P(None, 'tensor'), may hold values from -0.109375 to 0.109375
- out_bias: bfloat16 [2, 4, 768], replicated, may hold values from -2.5 to 2.5
- norm_gain: bfloat16 [2, 2, 768], replicated, may hold values from 0.25 to 1.75
- doc_start: int32 [32], P('dp'), may hold values from 0 to 3, as said below
- picture: int32 [32], P('dp'), may hold values 0 or 1
- cotangent: bfloat16 [8192, 768], P(('dp', 'tensor')), may hold values from -6 to 6
Outputs:
- result: float32 [8192, 768], P(('dp', 'tensor'))
- tokens_grad: float32 [8192, 768], P(('dp', 'tensor'))
- qkv_weight_grad: float32 [2, 768, 3, 768], P(None, 'dp', None, 'tensor')
- qv_bias_grad: float32 [2, 2, 768], P(None, None, ('tensor', 'dp'))
- out_weight_grad: float32 [2, 768, 768], P(None, 'tensor', 'dp')
- up_weight_grad: float32 [2, 768, 3072], P(None, 'dp', 'tensor')
- up_bias_grad: float32 [2, 3072], P(None, ('tensor', 'dp'))
- down_weight_grad: float32 [2, 3072, 768], P(None, 'tensor', 'dp')
- out_bias_grad: float32 [2, 4, 768], P(None, None, ('dp', 'tensor'))
- norm_gain_grad: float32 [2, 2, 768], P(None, None, ('dp', 'tensor'))
The draws below stay inside these ranges and needn't reach their ends.
Inputs may be any that keep to these rules, and one draw needn't show every extreme that they name: `doc_start`: A block's 1024 tokens (one index of dp) are whole documents made of whole 256-token spans; entry b is the first span of span b's document counted from the start of its block, so it never exceeds b and stays constant inside a document; every block holds one document of exactly 768 tokens and none longer.
All inputs are finite; a program needn't handle non-finite values. No bound on the sum of `picture` on one device may be relied on, other than what follows from the above.
Results may differ from the reference program's by a relative error of at most 0.03.
Values may be sent and summed in bfloat16 or wider, within the bound.
A program may use at most 192 MiB of HBM per device.

```python
import jax
import jax.numpy as jnp
from jax import lax

D = 768
HEADS = 12
HEAD_DIM = 64
FF = 3072
LAYERS = 2
TOK_DEV = 1024
SPAN = 256
LONGEST = 768
TOKENS = 8192


def draw_doc_start(key, part):
    groups = TOKENS // TOK_DEV
    blocks = TOK_DEV // SPAN
    longest = LONGEST // SPAN
    place_key, bit_key = jax.random.split(jax.random.fold_in(key, 17))
    anchor = jax.random.randint(place_key, (groups, 1), 0, blocks - longest + 1)
    random_bits = jax.random.randint(bit_key, (groups, blocks), 0, 2)
    block_index = jnp.arange(blocks)[None, :]
    offset = block_index - anchor
    forced = offset % longest == 0
    inside = (offset > 0) & (offset < longest)
    starts = jnp.where(forced | (block_index == 0), 1, jnp.where(inside, 0, random_bits))
    marked = jnp.where(starts == 1, block_index, 0)
    return lax.cummax(marked, axis=1).reshape(groups * blocks).astype(jnp.int32)


def place_ends(values, rng, low, largest):
    dims = values.shape
    index_at = [jax.random.randint(jax.random.fold_in(rng, axis), (), 0, dims[axis]) for axis in range(len(dims))]
    values = values.at[tuple(index_at)].set(low)
    longest = dims.index(max(dims))
    index_at[longest] = (index_at[longest] + 1) % dims[longest]
    return values.at[tuple(index_at)].set(largest)


def raised(values, rng, source, target, blocks, factor):
    owner, partner = [(jnp.arange(values.shape[dim]) // (values.shape[dim] // blocks)).reshape([-1 if axis == dim else 1 for axis in range(values.ndim)]) for dim in (source, target)]
    chosen = jax.random.permutation(rng, blocks)[partner]
    strong = (owner == chosen) | (owner == (partner + blocks // 2) % blocks)
    return jnp.where(strong, factor * values, values)


def levels(stream_key, shape, cuts, smallest, top_value):
    level, own = 1.0, jax.random.fold_in(stream_key, 6)
    for axis_at, shards_of in cuts:
        draws = jnp.exp(jax.random.uniform(jax.random.fold_in(own, axis_at), (shards_of,), jnp.float32, smallest / len(cuts), top_value / len(cuts)))
        level = level * jnp.repeat(draws, shape[axis_at] // shards_of).reshape([-1 if axis == axis_at else 1 for axis in range(len(shape))])
    return level


def noise(rng, extent, scale, reach, cuts=(), dtype=jnp.bfloat16):
    drawn = scale * jax.random.normal(rng, extent, jnp.float32)
    if cuts:
        drawn = drawn * levels(rng, extent, cuts, -0.22, 0.18)
    return jnp.clip(drawn, -reach, reach).astype(dtype)


def heavy_noise(key, dims, deviation, limit, shards, heavy, held_as=jnp.bfloat16):
    array = deviation * jax.random.normal(key, dims, jnp.float32)
    if shards:
        array = array * levels(key, dims, shards, -0.22, 0.18)
    return jnp.clip(raised(array, jax.random.fold_in(key, 3), *heavy), -limit, limit).astype(held_as)


def setup_inputs(seed: int = 0) -> dict:
    keys = jax.random.split(jax.random.key(seed), 13)
    return {
        "tokens": heavy_noise(keys[0], (TOKENS, D), 1.0, 6.0, ((0, 32),), (0, 1, 32, 2.75)),
        "qkv_weight": noise(keys[1], (LAYERS, D, 3, D), D ** -0.5, 0.21875, ((3, 4),)),
        "qv_bias": noise(keys[2], (LAYERS, 2, D), 0.5, 3.0, ((2, 4),)),
        "out_weight": noise(keys[3], (LAYERS, D, D), (D // 8) ** -0.5, 0.625, ((1, 4),)),
        "up_weight": noise(keys[4], (LAYERS, D, FF), D ** -0.5, 0.21875, ((2, 4),)),
        "up_bias": noise(keys[5], (LAYERS, FF), 0.5, 3.0, ((1, 4),)),
        "down_weight": noise(keys[6], (LAYERS, FF, D), FF ** -0.5, 0.109375, ((1, 4),)),
        "out_bias": noise(keys[7], (LAYERS, 4, D), 0.4, 2.5),
        "norm_gain": jnp.clip(1.0 + 0.15 * jax.random.normal(keys[8], (LAYERS, 2, D), jnp.float32), 0.25, 1.75).astype(jnp.bfloat16),
        "doc_start": draw_doc_start(jax.random.fold_in(keys[12], 71), 0),
        "picture": place_ends((jax.random.randint(keys[10], (TOKENS // SPAN,), 0, 3) < 1).astype(jnp.int32), jax.random.fold_in(keys[10], 1), 0, 1),
        "cotangent": noise(keys[11], (TOKENS, D), 1.0, 6.0, ((0, 32),)),
    }


@jax.custom_vjp
def low(v):
    return lax.optimization_barrier(v.astype(jnp.bfloat16)).astype(jnp.float32)

@jax.custom_vjp
def low_back(v):
    return v

def low_keep(v):
    return (low(v), None)

def low_pass(kept, grad):
    return (grad,)

def back_keep(v):
    return (v, None)

def back_low(kept, grad):
    return (low(grad),)
low.defvjp(low_keep, low_pass)
low_back.defvjp(back_keep, back_low)
HIGHEST = lax.Precision.HIGHEST
epsilon = 1e-05

def matmul(left, right):
    return jnp.dot(left, right, precision=HIGHEST, preferred_element_type=jnp.float32)

def layer_norm(inputs, gain, shift):
    average = lax.optimization_barrier(jnp.mean(inputs, axis=-1, keepdims=True))
    centered = inputs - average
    variance = lax.optimization_barrier(jnp.mean(centered * centered, axis=-1, keepdims=True))
    return centered * lax.rsqrt(variance + epsilon) * gain + shift

def attend_block(operands):
    query_rows, key_rows, value_rows, doc_tokens, picture_tokens = operands
    positions = jnp.arange(TOK_DEV)
    span_ids = positions // SPAN
    same_doc = doc_tokens[:, None] == doc_tokens[None, :]
    earlier = positions[None, :] <= positions[:, None]
    inside = (span_ids[:, None] == span_ids[None, :]) & (picture_tokens[:, None] == 1)
    allowed = same_doc & (earlier | inside)
    scores = jnp.einsum('qhd,khd->hqk', query_rows, key_rows, precision=HIGHEST) * 0.125
    scores = low_back(scores)
    scores = jnp.where(allowed[None], scores, -1e+30)
    row_max = lax.optimization_barrier(jnp.max(scores, axis=-1, keepdims=True))
    exponent = jnp.exp(scores - row_max)
    probability = low(exponent / lax.optimization_barrier(jnp.sum(exponent, axis=-1, keepdims=True)))
    return jnp.einsum('hqk,khd->qhd', probability, value_rows, precision=HIGHEST)

def forward(tokens, qkv_weight, qv_bias, out_weight, up_weight, up_bias, down_weight, out_bias, norm_gain, doc_tokens, picture_tokens):
    stream = tokens
    groups = TOKENS // TOK_DEV
    doc_groups = doc_tokens.reshape(groups, TOK_DEV)
    picture_groups = picture_tokens.reshape(groups, TOK_DEV)
    for layer_idx in range(LAYERS):
        rounded_in = low(stream)
        projected = jnp.einsum('td,dcf->tcf', rounded_in, qkv_weight[layer_idx], precision=HIGHEST)
        query_rows = low(low_back(projected[:, 0] + qv_bias[layer_idx, 0]))
        key_rows = low(low_back(projected[:, 1]))
        value_rows = low(low_back(projected[:, 2] + qv_bias[layer_idx, 1]))
        shaped = (groups, TOK_DEV, HEADS, HEAD_DIM)
        attended = lax.map(jax.checkpoint(attend_block), (query_rows.reshape(shaped), key_rows.reshape(shaped), value_rows.reshape(shaped), doc_groups, picture_groups))
        attended = low(low_back(attended.reshape(TOKENS, D)))
        branch = low_back(matmul(attended, out_weight[layer_idx]))
        normed = layer_norm(stream + branch + out_bias[layer_idx, 0], norm_gain[layer_idx, 0], out_bias[layer_idx, 1])
        rounded_normed = low(normed)
        pre_act = low_back(matmul(rounded_normed, up_weight[layer_idx]) + up_bias[layer_idx])
        activation = low(jax.nn.gelu(pre_act, approximate=False))
        branch_two = low_back(matmul(activation, down_weight[layer_idx]))
        stream = layer_norm(normed + branch_two + out_bias[layer_idx, 2], norm_gain[layer_idx, 1], out_bias[layer_idx, 3])
    return stream

def reference(tokens, qkv_weight, qv_bias, out_weight, up_weight, up_bias, down_weight, out_bias, norm_gain, doc_start, picture, cotangent):
    doc_tokens = jnp.repeat(doc_start, SPAN)
    picture_tokens = jnp.repeat(picture, SPAN)
    as_float = tuple((item.astype(jnp.float32) for item in (tokens, qkv_weight, qv_bias, out_weight, up_weight, up_bias, down_weight, out_bias, norm_gain)))

    def wrapped(*floats):
        return forward(*floats, doc_tokens, picture_tokens)
    result, pullback = jax.vjp(wrapped, *as_float)
    gradients = pullback(cotangent.astype(jnp.float32))
    return (result, gradients[0], gradients[1], gradients[2], gradients[3], gradients[4], gradients[5], gradients[6], gradients[7], gradients[8])
```

```python
from functools import partial

import jax
import jax.numpy as jnp
from jax import lax
from jax.sharding import PartitionSpec as P

HEAD_DIM = 64
SPAN = 256


epsilon = 1e-05


def layer_norm(inputs, gain, shift):
    average = jnp.mean(inputs, axis=-1, keepdims=True)
    centered = inputs - average
    variance = jnp.mean(centered * centered, axis=-1, keepdims=True)
    return centered * lax.rsqrt(variance + epsilon) * gain + shift


def block_mask(doc_tokens, picture_tokens, begin_row, end_row):
    query_pos = jnp.arange(begin_row, end_row)
    key_pos = jnp.arange(end_row)
    same_doc = doc_tokens[begin_row:end_row, None] == doc_tokens[None, :end_row]
    earlier = key_pos[None, :] <= query_pos[:, None]
    same_span = query_pos[:, None] // SPAN == key_pos[None, :] // SPAN
    picture_row = picture_tokens[begin_row:end_row, None] == 1
    return same_doc & (earlier | same_span & picture_row)


def block_scores(query_rows, key_rows, doc_tokens, picture_tokens, begin_row, end_row):
    heads_here = query_rows.shape[1] // HEAD_DIM
    query_block = query_rows[begin_row:end_row].reshape(end_row - begin_row, heads_here, HEAD_DIM)
    key_part = key_rows[:end_row].reshape(end_row, heads_here, HEAD_DIM)
    scores = (
        jnp.einsum("qhd,khd->hqk", query_block, key_part, preferred_element_type=jnp.float32)
        * 0.125
    )
    allowed = block_mask(doc_tokens, picture_tokens, begin_row, end_row)
    return (jnp.where(allowed[None], scores, -1e30), query_block, key_part)


def attention_forward(query_rows, key_rows, value_rows, doc_tokens, picture_tokens, block_rows):
    seq_rows, local_width = query_rows.shape
    heads_here = local_width // HEAD_DIM
    outputs = []
    log_totals = []
    for begin_row in range(0, seq_rows, block_rows):
        end_row = begin_row + block_rows
        scores, query_block, key_part = block_scores(
            query_rows, key_rows, doc_tokens, picture_tokens, begin_row, end_row
        )
        row_max = jnp.max(scores, axis=-1, keepdims=True)
        exponent = jnp.exp(scores - row_max)
        row_total = jnp.sum(exponent, axis=-1, keepdims=True)
        probability = (exponent / row_total).astype(jnp.bfloat16)
        value_part = value_rows[:end_row].reshape(end_row, heads_here, HEAD_DIM)
        attended = jnp.einsum(
            "hqk,khd->qhd", probability, value_part, preferred_element_type=jnp.float32
        )
        outputs.append(attended.reshape(block_rows, local_width).astype(jnp.bfloat16))
        log_totals.append(row_max + jnp.log(row_total))
    return (jnp.concatenate(outputs, axis=0), log_totals)


def attention_backward(
    query_rows,
    key_rows,
    value_rows,
    grad_attended,
    log_totals,
    doc_tokens,
    picture_tokens,
    block_rows,
):
    seq_rows, local_width = query_rows.shape
    heads_here = local_width // HEAD_DIM
    grad_query_blocks = []
    grad_keys = jnp.zeros((seq_rows, heads_here, HEAD_DIM), jnp.float32)
    grad_values = jnp.zeros((seq_rows, heads_here, HEAD_DIM), jnp.float32)
    for block_idx, begin_row in enumerate(range(0, seq_rows, block_rows)):
        end_row = begin_row + block_rows
        scores, query_block, key_part = block_scores(
            query_rows, key_rows, doc_tokens, picture_tokens, begin_row, end_row
        )
        probability = jnp.exp(scores - log_totals[block_idx])
        prob_low = probability.astype(jnp.bfloat16)
        value_part = value_rows[:end_row].reshape(end_row, heads_here, HEAD_DIM)
        grad_block = grad_attended[begin_row:end_row].reshape(block_rows, heads_here, HEAD_DIM)
        grad_prob = jnp.einsum(
            "qhd,khd->hqk", grad_block, value_part, preferred_element_type=jnp.float32
        )
        row_inner = jnp.sum(probability * grad_prob, axis=-1, keepdims=True)
        grad_scores = (probability * (grad_prob - row_inner)).astype(jnp.bfloat16)
        grad_query = (
            jnp.einsum("hqk,khd->qhd", grad_scores, key_part, preferred_element_type=jnp.float32)
            * 0.125
        )
        grad_query_blocks.append(grad_query.reshape(block_rows, local_width).astype(jnp.bfloat16))
        grad_keys = grad_keys.at[:end_row].add(
            jnp.einsum("hqk,qhd->khd", grad_scores, query_block, preferred_element_type=jnp.float32)
            * 0.125
        )
        grad_values = grad_values.at[:end_row].add(
            jnp.einsum("hqk,qhd->khd", prob_low, grad_block, preferred_element_type=jnp.float32)
        )
    grad_query_all = jnp.concatenate(grad_query_blocks, axis=0)
    return (
        grad_query_all,
        grad_keys.reshape(seq_rows, local_width).astype(jnp.bfloat16),
        grad_values.reshape(seq_rows, local_width).astype(jnp.bfloat16),
    )


def body(
    tokens,
    qkv_weight,
    qv_bias,
    out_weight,
    up_weight,
    up_bias,
    down_weight,
    out_bias,
    norm_gain,
    doc_start,
    picture,
    cotangent,
):
    layers = qkv_weight.shape[0]
    rows_here = tokens.shape[0]
    doc_tokens = jnp.repeat(doc_start, SPAN)
    picture_tokens = jnp.repeat(picture, SPAN)
    seq_rows = doc_tokens.shape[0]
    block_rows = min(512, seq_rows)
    exact_gelu = partial(jax.nn.gelu, approximate=False)
    stream = tokens.astype(jnp.float32)
    stored = []
    for layer_idx in range(layers):
        rows_in = lax.all_gather(stream.astype(jnp.bfloat16), "tensor", axis=0, tiled=True)
        projected = jnp.einsum(
            "td,dcf->tcf", rows_in, qkv_weight[layer_idx], preferred_element_type=jnp.float32
        )
        query_rows = (projected[:, 0] + qv_bias[layer_idx, 0]).astype(jnp.bfloat16)
        key_rows = projected[:, 1].astype(jnp.bfloat16)
        value_rows = (projected[:, 2] + qv_bias[layer_idx, 1]).astype(jnp.bfloat16)
        attended, log_totals = attention_forward(
            query_rows, key_rows, value_rows, doc_tokens, picture_tokens, block_rows
        )
        attn_weight = out_weight[layer_idx]

        def attn_rows(begin_row, row_count, source=attended, weight_rows=attn_weight):
            return jnp.dot(
                lax.dynamic_slice_in_dim(source, begin_row, row_count, 0),
                weight_rows,
                preferred_element_type=jnp.float32,
            )

        branch = lax.psum_scatter(
            attn_rows(jnp.int32(0), rows_here * lax.axis_size("tensor")).astype(jnp.bfloat16),
            "tensor",
            scatter_dimension=0,
            tiled=True,
        ).astype(jnp.float32)
        normed, first_pull = jax.vjp(
            layer_norm,
            stream + branch + out_bias[layer_idx, 0].astype(jnp.float32),
            norm_gain[layer_idx, 0].astype(jnp.float32),
            out_bias[layer_idx, 1].astype(jnp.float32),
        )
        normed_rows = lax.all_gather(normed.astype(jnp.bfloat16), "tensor", axis=0, tiled=True)
        pre_act = (
            jnp.dot(normed_rows, up_weight[layer_idx], preferred_element_type=jnp.float32)
            + up_bias[layer_idx]
        )
        activation_f, gelu_pull = jax.vjp(exact_gelu, pre_act)
        activation = activation_f.astype(jnp.bfloat16)
        ffn_weight = down_weight[layer_idx]

        def ffn_rows(begin_row, row_count, source=activation, weight_rows=ffn_weight):
            return jnp.dot(
                lax.dynamic_slice_in_dim(source, begin_row, row_count, 0),
                weight_rows,
                preferred_element_type=jnp.float32,
            )

        branch_two = lax.psum_scatter(
            ffn_rows(jnp.int32(0), rows_here * lax.axis_size("tensor")).astype(jnp.bfloat16),
            "tensor",
            scatter_dimension=0,
            tiled=True,
        ).astype(jnp.float32)
        stream, second_pull = jax.vjp(
            layer_norm,
            normed + branch_two + out_bias[layer_idx, 2].astype(jnp.float32),
            norm_gain[layer_idx, 1].astype(jnp.float32),
            out_bias[layer_idx, 3].astype(jnp.float32),
        )
        stored.append(
            (
                rows_in,
                query_rows,
                key_rows,
                value_rows,
                attended,
                log_totals,
                first_pull,
                normed_rows,
                gelu_pull,
                activation,
                second_pull,
            )
        )
    grad_stream = cotangent.astype(jnp.float32)
    local_terms = [None] * layers
    vector_terms = [None] * layers
    for layer_idx in reversed(range(layers)):
        (
            rows_in,
            query_rows,
            key_rows,
            value_rows,
            attended,
            log_totals,
            first_pull,
            normed_rows,
            gelu_pull,
            activation,
            second_pull,
        ) = stored[layer_idx]
        grad_second, grad_gain_two, grad_shift_two = second_pull(grad_stream)
        grad_ffn_bias = jnp.sum(grad_second, axis=0)
        ffn_grad_rows = lax.all_gather(
            grad_second.astype(jnp.bfloat16), "tensor", axis=0, tiled=True
        )
        down_grad = jnp.einsum(
            "tf,td->fd", activation, ffn_grad_rows, preferred_element_type=jnp.float32
        )
        grad_activation = jnp.einsum(
            "td,fd->tf", ffn_grad_rows, down_weight[layer_idx], preferred_element_type=jnp.float32
        )
        grad_pre = gelu_pull(grad_activation)[0].astype(jnp.bfloat16)
        up_bias_grad = jnp.sum(grad_pre, axis=0, dtype=jnp.float32)
        up_grad = jnp.einsum("td,tf->df", normed_rows, grad_pre, preferred_element_type=jnp.float32)
        up_rows = up_weight[layer_idx]

        def ffn_back_rows(begin_row, row_count, source=grad_pre, weight_rows=up_rows):
            return jnp.einsum(
                "tf,df->td",
                lax.dynamic_slice_in_dim(source, begin_row, row_count, 0),
                weight_rows,
                preferred_element_type=jnp.float32,
            )

        grad_normed = grad_second + lax.psum_scatter(
            ffn_back_rows(jnp.int32(0), rows_here * lax.axis_size("tensor")).astype(jnp.bfloat16),
            "tensor",
            scatter_dimension=0,
            tiled=True,
        ).astype(jnp.float32)
        grad_first, grad_gain_one, grad_shift_one = first_pull(grad_normed)
        grad_attn_bias = jnp.sum(grad_first, axis=0)
        attn_grad_rows = lax.all_gather(
            grad_first.astype(jnp.bfloat16), "tensor", axis=0, tiled=True
        )
        out_grad = jnp.einsum(
            "tf,td->fd", attended, attn_grad_rows, preferred_element_type=jnp.float32
        )
        grad_attended = jnp.einsum(
            "td,fd->tf", attn_grad_rows, out_weight[layer_idx], preferred_element_type=jnp.float32
        ).astype(jnp.bfloat16)
        grad_query, grad_keys, grad_values = attention_backward(
            query_rows,
            key_rows,
            value_rows,
            grad_attended,
            log_totals,
            doc_tokens,
            picture_tokens,
            block_rows,
        )
        grad_stack = jnp.stack((grad_query, grad_keys, grad_values), axis=1)
        qkv_grad = jnp.einsum(
            "td,tcf->dcf", rows_in, grad_stack, preferred_element_type=jnp.float32
        )
        head_bias_grad = jnp.stack(
            (
                jnp.sum(grad_query, axis=0, dtype=jnp.float32),
                jnp.sum(grad_values, axis=0, dtype=jnp.float32),
            )
        )
        proj_rows = qkv_weight[layer_idx]

        def attn_back_rows(begin_row, row_count, source=grad_stack, weight_rows=proj_rows):
            return jnp.einsum(
                "tcf,dcf->td",
                lax.dynamic_slice_in_dim(source, begin_row, row_count, 0),
                weight_rows,
                preferred_element_type=jnp.float32,
            )

        grad_stream = grad_first + lax.psum_scatter(
            attn_back_rows(jnp.int32(0), rows_here * lax.axis_size("tensor")).astype(jnp.bfloat16),
            "tensor",
            scatter_dimension=0,
            tiled=True,
        ).astype(jnp.float32)
        layer_terms = (qkv_grad, head_bias_grad, out_grad, up_grad, up_bias_grad, down_grad)
        vector_terms[layer_idx] = (
            jnp.stack((grad_attn_bias, grad_shift_one, grad_ffn_bias, grad_shift_two)),
            jnp.stack((grad_gain_one, grad_gain_two)),
        )
        local_terms[layer_idx] = layer_terms
    shares = lax.axis_size("dp")
    split = lax.axis_size("tensor")
    width = tokens.shape[1]
    rows_each = width // shares
    head_each = qv_bias.shape[2] // shares
    up_each = up_bias.shape[1] // shares
    packed = []
    for layer_idx in range(layers):
        qkv_grad, head_bias_grad, out_grad, up_grad, up_bias_grad, down_grad = local_terms[layer_idx]
        local_width = qkv_grad.shape[2]
        hidden = up_grad.shape[1]
        total_width = 4 * local_width + 2 * hidden
        vectors = jnp.concatenate(vector_terms[layer_idx], axis=0)
        extra = jnp.concatenate(
            (
                vectors.reshape(6, shares, rows_each).transpose(1, 0, 2).reshape(shares, -1),
                head_bias_grad.reshape(2, shares, head_each).transpose(1, 0, 2).reshape(shares, -1),
                up_bias_grad.reshape(shares, up_each),
            ),
            axis=1,
        )
        extra = jnp.pad(extra, ((0, 0), (0, -extra.shape[1] % total_width)))
        extra = extra.reshape(shares, -1, total_width)
        whole = jnp.concatenate(
            (qkv_grad.reshape(width, -1), out_grad.T, up_grad, down_grad.T), axis=1
        ).reshape(shares, rows_each, total_width)
        whole = jnp.concatenate((whole, extra), axis=1).astype(jnp.bfloat16)
        packed.append(
            lax.psum_scatter(whole, "dp", scatter_dimension=0, tiled=True)[0].astype(jnp.float32)
        )
    qkv_parts, head_parts, out_parts, up_parts, up_bias_parts, down_parts, vector_parts = (
        [],
        [],
        [],
        [],
        [],
        [],
        [],
    )
    for part in packed:
        main, extra = part[:rows_each], part[rows_each:].reshape(-1)
        vector_parts.append(extra[: 6 * rows_each].reshape(6, rows_each))
        extra = extra[6 * rows_each :]
        head_parts.append(extra[: 2 * head_each].reshape(2, head_each))
        up_bias_parts.append(extra[2 * head_each : 2 * head_each + up_each])
        qkv_parts.append(main[:, : 3 * local_width].reshape(rows_each, 3, local_width))
        out_parts.append(main[:, 3 * local_width : 4 * local_width].T)
        up_parts.append(main[:, 4 * local_width : 4 * local_width + hidden])
        down_parts.append(main[:, 4 * local_width + hidden :].T)
    vector_sum = lax.psum_scatter(
        jnp.stack(vector_parts), "tensor", scatter_dimension=2, tiled=True
    )
    return (
        stream,
        grad_stream,
        jnp.stack(qkv_parts),
        jnp.stack(head_parts),
        jnp.stack(out_parts),
        jnp.stack(up_parts),
        jnp.stack(up_bias_parts),
        jnp.stack(down_parts),
        vector_sum[:, :4],
        vector_sum[:, 4:],
    )


def solution(mesh):
    return jax.shard_map(
        body,
        mesh=mesh,
        in_specs=(
            P(("dp", "tensor"), None),
            P(None, None, None, "tensor"),
            P(None, None, "tensor"),
            P(None, "tensor", None),
            P(None, None, "tensor"),
            P(None, "tensor"),
            P(None, "tensor", None),
            P(),
            P(),
            P("dp"),
            P("dp"),
            P(("dp", "tensor"), None),
        ),
        out_specs=(
            P(("dp", "tensor"), None),
            P(("dp", "tensor"), None),
            P(None, "dp", None, "tensor"),
            P(None, None, ("tensor", "dp")),
            P(None, "tensor", "dp"),
            P(None, "dp", "tensor"),
            P(None, ("tensor", "dp")),
            P(None, "tensor", "dp"),
            P(None, None, ("dp", "tensor")),
            P(None, None, ("dp", "tensor")),
        ),
        check_vma=False,
    )
```

```python
from functools import partial

import jax
import jax.numpy as jnp
from jax import lax
from jax.experimental import pallas as pl
from jax.experimental.pallas import tpu as pltpu
from jax.sharding import PartitionSpec as P

HEAD_DIM = 64
SPAN = 256
GROUP = 4
LONGEST = 3
CHUNKS = 2
EPSILON = 1e-05
FAR = 1 << 20
F32 = jnp.float32
BF16 = jnp.bfloat16
MESH = pl.DeviceIdType.MESH
FWD_ATTN, FWD_FFN, BWD_FFN, BWD_ATTN = range(4)


def dot_nn(left, right):
    return lax.dot_general(left, right, (((1,), (0,)), ((), ())), preferred_element_type=F32)


def dot_nt(left, right):
    return lax.dot_general(left, right, (((1,), (1,)), ((), ())), preferred_element_type=F32)


def dot_tn(left, right):
    return lax.dot_general(left, right, (((0,), (0,)), ((), ())), preferred_element_type=F32)


def gelu_parts(value):
    cdf = 0.5 * (1.0 + lax.erf(value * 0.7071067811865476))
    density = jnp.exp(-0.5 * value * value) * 0.3989422804014327
    return value * cdf, cdf + value * density


def step_kernel(
    tokens_ref,
    cot_ref,
    vin_ref,
    doc_ref,
    pic_ref,
    wqkv_hbm,
    wout_hbm,
    wup_hbm,
    wdown_hbm,
    result_ref,
    tgrad_ref,
    vout_ref,
    grads_ref,
    wqkv,
    wout,
    wup,
    wdown,
    xr,
    q_all,
    k_all,
    v_all,
    prob,
    att,
    hr,
    act,
    slope,
    n_one,
    r_one,
    n_two,
    r_two,
    gf,
    ga,
    go,
    gq,
    gk,
    gv,
    gqkv,
    cur,
    mid,
    d0s,
    d0r,
    d1s,
    d1r,
    xsd,
    xrv,
    keep,
    w_sem,
    agx_s,
    agx_r,
    ags_s,
    ags_r,
    agf_s,
    agf_r,
    d0_s,
    d0_r,
    d1_s,
    d1_r,
    x_s,
    x_r,
):
    layers = vin_ref.shape[0]
    shard, width = tokens_ref.shape
    chunk = shard // CHUNKS
    heads_width = att.shape[2]
    window = LONGEST * SPAN
    hidden = wup.shape[2]
    me = lax.axis_index("tensor")
    row, col = me // 2, me % 2
    sib = row * 2 + (1 - col)
    cross = (1 - row) * 2 + col
    diag = (1 - row) * 2 + (1 - col)

    loads = []
    for place, (src, dst) in enumerate(
        ((wqkv_hbm, wqkv), (wout_hbm, wout), (wup_hbm, wup), (wdown_hbm, wdown))
    ):
        load = pltpu.make_async_copy(src, dst, w_sem.at[place])
        load.start()
        loads.append(load)

    barrier = pltpu.get_barrier_semaphore()
    for peer in (sib, cross):
        pl.semaphore_signal(barrier, inc=1, device_id={"tensor": peer}, device_id_type=MESH)
    pl.semaphore_wait(barrier, 2)

    def at_rows(owner, piece):
        return pl.ds(pl.multiple_of(owner * shard + piece * chunk, chunk), chunk)

    def span_rows(owner):
        return pl.ds(pl.multiple_of(owner * shard, shard), shard)

    def part(piece):
        return pl.ds(piece * chunk, chunk)

    def remote(src, dst, send, recv, peer):
        return pltpu.make_async_remote_copy(
            src_ref=src,
            dst_ref=dst,
            send_sem=send,
            recv_sem=recv,
            device_id={"tensor": peer},
            device_id_type=MESH,
        )

    def ag_copy(kind, phase, layer, piece, buf):
        owner, peer, send, recv = {
            "x": (me, cross, agx_s, agx_r),
            "s": (me, sib, ags_s, ags_r),
            "f": (cross, sib, agf_s, agf_r),
        }[kind]
        view = buf.at[at_rows(owner, piece)]
        return remote(view, view, send.at[phase, layer, piece], recv.at[phase, layer, piece], peer)

    def ag_recv(kind, phase, layer, piece, buf):
        owner, peer, send, recv = {
            "x": (cross, cross, agx_s, agx_r),
            "s": (sib, sib, ags_s, ags_r),
            "f": (diag, sib, agf_s, agf_r),
        }[kind]
        view = buf.at[at_rows(owner, piece)]
        return remote(view, view, send.at[phase, layer, piece], recv.at[phase, layer, piece], peer)

    def ag_send(phase, layer, piece, buf):
        ag_copy("x", phase, layer, piece, buf).start()
        ag_copy("s", phase, layer, piece, buf).start()

    def ag_forward(phase, layer, piece, buf):
        ag_recv("x", phase, layer, piece, buf).wait_recv()
        ag_copy("f", phase, layer, piece, buf).start()

    def ag_done(phase, layer, buf):
        for piece in range(CHUNKS):
            for kind in "xsf":
                ag_copy(kind, phase, layer, piece, buf).wait_send()

    def rs_copy(kind, phase, layer, piece):
        src, dst, send, recv, peer = {
            "d0": (d0s, d0r, d0_s, d0_r, sib),
            "d1": (d1s, d1r, d1_s, d1_r, sib),
            "x": (xsd, xrv, x_s, x_r, cross),
        }[kind]
        return remote(
            src.at[piece],
            dst.at[piece],
            send.at[phase, layer, piece],
            recv.at[phase, layer, piece],
            peer,
        )

    def rs_diag(phase, layer, piece, value):
        d0s[piece] = value.astype(BF16)
        rs_copy("d0", phase, layer, piece).start()

    def rs_cross(phase, layer, piece, value):
        rs_copy("d0", phase, layer, piece).wait_recv()
        xsd[piece] = (value + d0r[piece].astype(F32)).astype(BF16)
        rs_copy("x", phase, layer, piece).start()

    def rs_sib(phase, layer, piece, value):
        d1s[piece] = value.astype(BF16)
        rs_copy("d1", phase, layer, piece).start()

    def rs_final(phase, layer, piece):
        rs_copy("d1", phase, layer, piece).wait_recv()
        rs_copy("x", phase, layer, piece).wait_recv()
        total = keep[piece] + d1r[piece].astype(F32) + xrv[piece].astype(F32)
        for kind in ("d0", "d1", "x"):
            rs_copy(kind, phase, layer, piece).wait_send()
        return total

    def vec(layer, place):
        return vin_ref[layer, pl.ds(place, 1), :]

    def norm_forward(layer, piece, value, gain, shift, normed, inverse):
        centered = value - jnp.mean(value, axis=-1, keepdims=True)
        scale = lax.rsqrt(jnp.mean(centered * centered, axis=-1, keepdims=True) + EPSILON)
        unit = centered * scale
        normed[layer, part(piece), :] = unit
        inverse[layer, part(piece), :] = scale
        return unit * vec(layer, gain) + vec(layer, shift)

    def norm_backward(layer, piece, grad, gain, normed, inverse, rows):
        unit = normed[layer, part(piece), :]
        scale = inverse[layer, part(piece), :]
        scaled = grad * vec(layer, gain)
        out = scale * (
            scaled
            - jnp.mean(scaled, axis=-1, keepdims=True)
            - unit * jnp.mean(scaled * unit, axis=-1, keepdims=True)
        )
        gain_row, shift_row, bias_row = rows
        for place, term in ((gain_row, grad * unit), (shift_row, grad), (bias_row, out)):
            vout_ref[layer, pl.ds(place, 1), :] += jnp.sum(term, axis=0, keepdims=True)
        return out

    groups = []
    for begin in range(0, heads_width, 128):
        wide = min(128, heads_width - begin)
        groups.append((begin, wide, range(begin // HEAD_DIM, (begin + wide) // HEAD_DIM)))

    def only_head(value, begin, head):
        if value.shape[1] == HEAD_DIM:
            return value
        lane = lax.broadcasted_iota(jnp.int32, value.shape, 1)
        low = head * HEAD_DIM - begin
        return jnp.where((lane >= low) & (lane < low + HEAD_DIM), value, jnp.zeros_like(value))

    def window_of(span):
        return pl.ds(pl.multiple_of((span // LONGEST) * SPAN, SPAN), window)

    def attend(layer, span):
        rows = span_rows(span)
        keys = window_of(span)
        query_pos = span * SPAN + lax.broadcasted_iota(jnp.int32, (SPAN, 1), 0)
        picture = jnp.full((SPAN, 1), pic_ref[span], jnp.int32) == 1
        limit = jnp.where(picture, span * SPAN + SPAN - 1, query_pos)
        key_pos = (span // LONGEST) * SPAN + lax.broadcasted_iota(jnp.int32, (1, window), 1)
        first = jnp.full((1, window), doc_ref[span] * SPAN, jnp.int32)
        key_pos = jnp.where(key_pos >= first, key_pos, FAR)
        allowed = key_pos <= limit
        for begin, wide, heads in groups:
            cols = pl.ds(begin, wide)
            q_here = q_all[layer, rows, cols]
            k_here = k_all[layer, keys, cols]
            v_here = v_all[layer, keys, cols]
            total = jnp.zeros((SPAN, wide), F32)
            for head in heads:
                scores = dot_nt(only_head(q_here, begin, head), k_here)
                scores = jnp.where(allowed, scores, -1e30)
                raised = jnp.exp(scores - jnp.max(scores, axis=-1, keepdims=True))
                share = raised * (1.0 / jnp.sum(raised, axis=-1, keepdims=True))
                share = share.astype(BF16)
                prob[layer, span, head] = share
                total = total + dot_nn(share, only_head(v_here, begin, head))
            att[layer, rows, cols] = total.astype(BF16)

    def attend_back(layer, span):
        rows = span_rows(span)
        keys = window_of(span)
        for begin, wide, heads in groups:
            cols = pl.ds(begin, wide)
            q_here = q_all[layer, rows, cols]
            k_here = k_all[layer, keys, cols]
            v_here = v_all[layer, keys, cols]
            go_here = go[rows, cols]
            mixed = go_here.astype(F32) * att[layer, rows, cols].astype(F32)
            total = jnp.zeros((SPAN, wide), F32)
            key_total = gk[keys, cols]
            value_total = gv[keys, cols]
            for head in heads:
                go_head = only_head(go_here, begin, head)
                inner = jnp.sum(only_head(mixed, begin, head), axis=-1, keepdims=True)
                gp = dot_nt(go_head, v_here)
                share = prob[layer, span, head]
                gs = (share.astype(F32) * (gp - inner)).astype(BF16)
                total = total + dot_nn(gs, only_head(k_here, begin, head))
                key_total = key_total + dot_tn(gs, only_head(q_here, begin, head))
                value_total = value_total + dot_tn(share, go_head)
            gk[keys, cols] = key_total
            gv[keys, cols] = value_total
            gq[rows, cols] = total * 0.125

    def project(layer, owner):
        rows = span_rows(owner)
        out = dot_nn(xr[layer, rows, :], wqkv[layer])
        bias = vec(layer, 7)
        q_all[layer, rows, :] = (
            (out[:, :heads_width] + bias[:, :heads_width]) * 0.125
        ).astype(BF16)
        k_all[layer, rows, :] = out[:, heads_width : 2 * heads_width].astype(BF16)
        v_all[layer, rows, :] = (
            out[:, 2 * heads_width :] + bias[:, heads_width : 2 * heads_width]
        ).astype(BF16)

    def two(buf, first, second, piece):
        return jnp.concatenate(
            (buf[at_rows(first, piece), :], buf[at_rows(second, piece), :]), axis=0
        )

    def ffn_rows(layer, first, second, piece):
        pre = dot_nn(two(hr.at[layer], first, second, piece), wup[layer]) + vec(layer, 6)
        value, grad = gelu_parts(pre)
        value, grad = value.astype(BF16), grad.astype(BF16)
        for place, owner in enumerate((first, second)):
            rows = at_rows(owner, piece)
            act[layer, rows, :] = value[place * chunk : (place + 1) * chunk]
            slope[layer, rows, :] = grad[place * chunk : (place + 1) * chunk]
        out = dot_nn(value, wdown[layer])
        return out[:chunk], out[chunk:]

    def ffn_back_rows(layer, first, second, piece):
        gu = dot_nt(two(gf, first, second, piece), wdown[layer])
        gpre = (gu * two(slope.at[layer], first, second, piece).astype(F32)).astype(BF16)
        for place, owner in enumerate((first, second)):
            slope[layer, at_rows(owner, piece), :] = gpre[place * chunk : (place + 1) * chunk]
        out = dot_nt(gpre, wup[layer])
        return out[:chunk], out[chunk:]

    def ffn_phase(phase, layer, buf, rows_of):
        for piece in range(CHUNKS):
            ag_recv("s", phase, layer, piece, buf).wait_recv()
            own_part, sib_part = rows_of(layer, me, sib, piece)
            rs_sib(phase, layer, piece, sib_part)
            keep[piece] = own_part
        for piece in range(CHUNKS):
            ag_forward(phase, layer, piece, buf)
            ag_recv("f", phase, layer, piece, buf).wait_recv()
            cross_part, diag_part = rows_of(layer, cross, diag, piece)
            rs_diag(phase, layer, piece, diag_part)
            rs_cross(phase, layer, piece, cross_part)
        ag_done(phase, layer, buf)

    def weight_grad(layer, left, right, begin, wide):
        def block(place, carry):
            cols = pl.ds(pl.multiple_of(place * 256, 256), 256)
            grads_ref[layer, cols, pl.ds(begin, wide)] = dot_tn(left[:, cols], right[...]).astype(
                BF16
            )
            return carry

        lax.fori_loop(0, width // 256, block, 0)

    vout_ref[...] = jnp.zeros_like(vout_ref)
    cur[...] = tokens_ref[...].astype(F32)

    def forward(layer, carry):
        here = xr.at[layer]
        for piece in range(CHUNKS):
            xr[layer, at_rows(me, piece), :] = cur[part(piece), :].astype(BF16)
            ag_send(FWD_ATTN, layer, piece, here)

        @pl.when(layer == 0)
        def _():
            loads[0].wait()
            loads[1].wait()

        project(layer, me)
        for piece in range(CHUNKS):
            ag_recv("s", FWD_ATTN, layer, piece, here).wait_recv()
        project(layer, sib)

        @pl.when(layer == 0)
        def _():
            loads[2].wait()
            loads[3].wait()

        for piece in range(CHUNKS):
            ag_forward(FWD_ATTN, layer, piece, here)
        project(layer, cross)
        for piece in range(CHUNKS):
            ag_recv("f", FWD_ATTN, layer, piece, here).wait_recv()
        project(layer, diag)
        for owner, send in ((diag, rs_diag), (cross, rs_cross), (sib, rs_sib), (me, None)):
            attend(layer, owner)
            out = dot_nn(att[layer, span_rows(owner), :], wout[layer])
            for piece in range(CHUNKS):
                value = out[piece * chunk : (piece + 1) * chunk]
                if send is None:
                    keep[piece] = value
                else:
                    send(FWD_ATTN, layer, piece, value)
        ag_done(FWD_ATTN, layer, here)
        there = hr.at[layer]
        for piece in range(CHUNKS):
            value = cur[part(piece), :] + rs_final(FWD_ATTN, layer, piece) + vec(layer, 0)
            value = norm_forward(layer, piece, value, 4, 1, n_one, r_one)
            mid[part(piece), :] = value
            hr[layer, at_rows(me, piece), :] = value.astype(BF16)
            ag_send(FWD_FFN, layer, piece, there)
        ffn_phase(FWD_FFN, layer, there, ffn_rows)
        for piece in range(CHUNKS):
            value = mid[part(piece), :] + rs_final(FWD_FFN, layer, piece) + vec(layer, 2)
            cur[part(piece), :] = norm_forward(layer, piece, value, 5, 3, n_two, r_two)
        return carry

    lax.fori_loop(0, layers, forward, 0)
    result_ref[...] = cur[...]

    cur[...] = cot_ref[...].astype(F32)

    def backward(step, carry):
        layer = layers - 1 - step
        for piece in range(CHUNKS):
            grad = norm_backward(layer, piece, cur[part(piece), :], 5, n_two, r_two, (5, 3, 2))
            mid[part(piece), :] = grad
            gf[at_rows(me, piece), :] = grad.astype(BF16)
            ag_send(BWD_FFN, layer, piece, gf)
        ffn_phase(BWD_FFN, layer, gf, ffn_back_rows)
        weight_grad(layer, gf, act.at[layer], hidden, hidden)
        for piece in range(CHUNKS):
            grad = mid[part(piece), :] + rs_final(BWD_FFN, layer, piece)
            grad = norm_backward(layer, piece, grad, 4, n_one, r_one, (4, 1, 0))
            cur[part(piece), :] = grad
            ga[at_rows(me, piece), :] = grad.astype(BF16)
            ag_send(BWD_ATTN, layer, piece, ga)
        weight_grad(layer, hr.at[layer], slope.at[layer], 0, hidden)
        vout_ref[layer, pl.ds(6, 1), :] = jnp.sum(
            slope[layer].astype(F32), axis=0, keepdims=True
        )
        gk[...] = jnp.zeros_like(gk)
        gv[...] = jnp.zeros_like(gv)

        def heads_grad(owner):
            rows = span_rows(owner)
            go[rows, :] = dot_nt(ga[rows, :], wout[layer]).astype(BF16)
            attend_back(layer, owner)

        heads_grad(me)
        for piece in range(CHUNKS):
            ag_recv("s", BWD_ATTN, layer, piece, ga).wait_recv()
        heads_grad(sib)
        for piece in range(CHUNKS):
            ag_forward(BWD_ATTN, layer, piece, ga)
        heads_grad(cross)
        for piece in range(CHUNKS):
            ag_recv("f", BWD_ATTN, layer, piece, ga).wait_recv()
        heads_grad(diag)
        for owner, send in ((diag, rs_diag), (cross, rs_cross), (sib, rs_sib), (me, None)):
            rows = span_rows(owner)
            joined = jnp.concatenate((gq[rows, :], gk[rows, :], gv[rows, :]), axis=1).astype(BF16)
            gqkv[rows, :] = joined
            out = dot_nt(joined, wqkv[layer])
            for piece in range(CHUNKS):
                value = out[piece * chunk : (piece + 1) * chunk]
                if send is None:
                    keep[piece] = value
                else:
                    send(BWD_ATTN, layer, piece, value)
        ag_done(BWD_ATTN, layer, ga)
        weight_grad(layer, xr.at[layer], gqkv, 2 * hidden, 3 * heads_width)
        weight_grad(layer, ga, att.at[layer], 2 * hidden + 3 * heads_width, heads_width)
        sums = jnp.sum(gqkv[...].astype(F32), axis=0, keepdims=True)
        vout_ref[layer, pl.ds(7, 1), pl.ds(0, heads_width)] = sums[:, :heads_width]
        vout_ref[layer, pl.ds(7, 1), pl.ds(heads_width, heads_width)] = sums[:, 2 * heads_width :]
        for piece in range(CHUNKS):
            cur[part(piece), :] = cur[part(piece), :] + rs_final(BWD_ATTN, layer, piece)
        return carry

    lax.fori_loop(0, layers, backward, 0)
    tgrad_ref[...] = cur[...]


def body(
    tokens,
    qkv_weight,
    qv_bias,
    out_weight,
    up_weight,
    up_bias,
    down_weight,
    out_bias,
    norm_gain,
    doc_start,
    picture,
    cotangent,
):
    layers, width, _, heads_width = qkv_weight.shape
    shard = tokens.shape[0]
    seq = shard * GROUP
    hidden = up_weight.shape[2]
    spans = seq // SPAN
    heads = heads_width // HEAD_DIM
    total_width = 4 * heads_width + 2 * hidden
    chunk = shard // CHUNKS
    wide = max(hidden, width)
    vin = jnp.concatenate(
        (
            out_bias,
            norm_gain,
            up_bias[:, None, :],
            jnp.pad(
                qv_bias.reshape(layers, 1, 2 * heads_width),
                ((0, 0), (0, 0), (0, wide - 2 * heads_width)),
            ),
        ),
        axis=1,
    ).astype(F32)
    vmem = partial(pl.BlockSpec, memory_space=pltpu.VMEM)
    smem = partial(pl.BlockSpec, memory_space=pltpu.SMEM)
    anywhere = partial(pl.BlockSpec, memory_space=pl.ANY)
    sems = pltpu.SemaphoreType.DMA((4, layers, CHUNKS))
    result, tokens_grad, vout, grads = pl.pallas_call(
        step_kernel,
        name="encoder_step",
        out_shape=(
            jax.ShapeDtypeStruct((shard, width), F32),
            jax.ShapeDtypeStruct((shard, width), F32),
            jax.ShapeDtypeStruct((layers, 8, wide), F32),
            jax.ShapeDtypeStruct((layers, width, total_width), BF16),
        ),
        in_specs=[vmem(), vmem(), vmem(), smem(), smem()] + [anywhere()] * 4,
        out_specs=(vmem(), vmem(), vmem(), vmem()),
        scratch_shapes=[
            pltpu.VMEM((layers, width, 3 * heads_width), BF16),
            pltpu.VMEM(out_weight.shape, BF16),
            pltpu.VMEM(up_weight.shape, BF16),
            pltpu.VMEM(down_weight.shape, BF16),
            pltpu.VMEM((layers, seq, width), BF16),
            pltpu.VMEM((layers, seq, heads_width), BF16),
            pltpu.VMEM((layers, seq, heads_width), BF16),
            pltpu.VMEM((layers, seq, heads_width), BF16),
            pltpu.VMEM((layers, spans, heads, SPAN, LONGEST * SPAN), BF16),
            pltpu.VMEM((layers, seq, heads_width), BF16),
            pltpu.VMEM((layers, seq, width), BF16),
            pltpu.VMEM((layers, seq, hidden), BF16),
            pltpu.VMEM((layers, seq, hidden), BF16),
            pltpu.VMEM((layers, shard, width), F32),
            pltpu.VMEM((layers, shard, 1), F32),
            pltpu.VMEM((layers, shard, width), F32),
            pltpu.VMEM((layers, shard, 1), F32),
            pltpu.VMEM((seq, width), BF16),
            pltpu.VMEM((seq, width), BF16),
            pltpu.VMEM((seq, heads_width), BF16),
            pltpu.VMEM((seq, heads_width), F32),
            pltpu.VMEM((seq, heads_width), F32),
            pltpu.VMEM((seq, heads_width), F32),
            pltpu.VMEM((seq, 3 * heads_width), BF16),
            pltpu.VMEM((shard, width), F32),
            pltpu.VMEM((shard, width), F32),
        ]
        + [pltpu.VMEM((CHUNKS, chunk, width), BF16)] * 6
        + [pltpu.VMEM((CHUNKS, chunk, width), F32), pltpu.SemaphoreType.DMA((4,))]
        + [sems] * 12,
        compiler_params=pltpu.CompilerParams(
            collective_id=0, has_side_effects=True, vmem_limit_bytes=67043328
        ),
    )(
        tokens,
        cotangent,
        vin,
        doc_start,
        picture,
        qkv_weight.reshape(layers, width, 3 * heads_width),
        out_weight,
        up_weight,
        down_weight,
    )
    shares = lax.axis_size("dp")
    rows_each = width // shares
    head_each = heads_width // shares
    up_each = hidden // shares
    place = lax.axis_index("dp")
    summed = [
        lax.psum_scatter(grads[layer], "dp", scatter_dimension=0, tiled=True).astype(F32)
        for layer in range(layers)
    ]
    main = jnp.stack(summed)
    qkv_part = main[:, :, 2 * hidden : 2 * hidden + 3 * heads_width].reshape(
        layers, rows_each, 3, heads_width
    )
    out_part = main[:, :, 2 * hidden + 3 * heads_width :].transpose(0, 2, 1)
    up_part = main[:, :, :hidden]
    down_part = main[:, :, hidden : 2 * hidden].transpose(0, 2, 1)
    vector_sum = lax.psum(vout[:, :6], ("dp", "tensor"))
    bias_sum = lax.psum(vout[:, 6:], "dp")
    fine = width // (shares * GROUP)
    vector_sum = lax.dynamic_slice_in_dim(
        vector_sum, place * rows_each + lax.axis_index("tensor") * fine, fine, 2
    )
    head_sum = bias_sum[:, 1, : 2 * heads_width].reshape(layers, 2, heads_width)
    return (
        result,
        tokens_grad,
        qkv_part,
        lax.dynamic_slice_in_dim(head_sum, place * head_each, head_each, 2),
        out_part,
        up_part,
        lax.dynamic_slice_in_dim(bias_sum[:, 0, :hidden], place * up_each, up_each, 1),
        down_part,
        vector_sum[:, :4],
        vector_sum[:, 4:],
    )


def solution(mesh):
    return jax.shard_map(
        body,
        mesh=mesh,
        in_specs=(
            P(("dp", "tensor"), None),
            P(None, None, None, "tensor"),
            P(None, None, "tensor"),
            P(None, "tensor", None),
            P(None, None, "tensor"),
            P(None, "tensor"),
            P(None, "tensor", None),
            P(),
            P(),
            P("dp"),
            P("dp"),
            P(("dp", "tensor"), None),
        ),
        out_specs=(
            P(("dp", "tensor"), None),
            P(("dp", "tensor"), None),
            P(None, "dp", None, "tensor"),
            P(None, None, ("tensor", "dp")),
            P(None, "tensor", "dp"),
            P(None, "dp", "tensor"),
            P(None, ("tensor", "dp")),
            P(None, "tensor", "dp"),
            P(None, None, ("dp", "tensor")),
            P(None, None, ("dp", "tensor")),
        ),
        check_vma=False,
    )
```

```python
from functools import partial

import jax
import jax.numpy as jnp
from jax import lax
from jax.experimental import pallas as pl
from jax.experimental.pallas import tpu as pltpu
from jax.sharding import PartitionSpec as P

HEAD_DIM = 64
SPAN = 256
GROUP = 4
LONGEST = 3
CHUNKS = 2
EPSILON = 1e-05
BEYOND = 1 << 20
NEAR, FAR_SIDE = 2, 4
NEAR_ORDER = (1, 0, 2, None)
F32 = jnp.float32
BF16 = jnp.bfloat16
MESH = pl.DeviceIdType.MESH
FWD_ATTN, FWD_FFN, BWD_FFN, BWD_ATTN = range(4)


def dot_nn(left, right):
    return lax.dot_general(left, right, (((1,), (0,)), ((), ())), preferred_element_type=F32)


def dot_nt(left, right):
    return lax.dot_general(left, right, (((1,), (1,)), ((), ())), preferred_element_type=F32)


def dot_tn(left, right):
    return lax.dot_general(left, right, (((0,), (0,)), ((), ())), preferred_element_type=F32)


def gelu_parts(value):
    cdf = 0.5 * (1.0 + lax.erf(value * 0.7071067811865476))
    density = jnp.exp(-0.5 * value * value) * 0.3989422804014327
    return value * cdf, cdf + value * density


def step_kernel(inside, *refs):
    (
        tokens_hbm,
        cot_hbm,
        obias_ref,
        gain_ref,
        ubias_ref,
        hbias_ref,
        doc_ref,
        pic_ref,
        wqkv_hbm,
        wout_hbm,
        wup_hbm,
        wdown_hbm,
        result_hbm,
        tgrad_hbm,
        vout_ref,
        *refs,
    ) = refs
    *refs, vin_ref = refs
    if inside:
        final_hbm, *refs = refs
        *refs, stage, f_sem, vsend, vrecv, y_buf, z_buf, y_s, y_r, z_s, z_r, v_s, v_r = refs
    (
        grads_ref,
        wqkv,
        wout,
        wup,
        wdown,
        xr,
        q_all,
        k_all,
        v_all,
        prob,
        att,
        hr,
        act,
        slope,
        n_one,
        r_one,
        n_two,
        r_two,
        gf,
        ga,
        go,
        gq,
        gk,
        gv,
        gqkv,
        cur,
        mid,
        d0s,
        d0r,
        d1s,
        d1r,
        xsd,
        xrv,
        keep,
        w_sem,
        agx_s,
        agx_r,
        ags_s,
        ags_r,
        agf_s,
        agf_r,
        d0_s,
        d0_r,
        d1_s,
        d1_r,
        x_s,
        x_r,
    ) = refs
    layers = obias_ref.shape[0]
    shard, width = tokens_hbm.shape
    chunk = shard // CHUNKS
    heads_width = att.shape[2]
    window = LONGEST * SPAN
    hidden = wup.shape[2]
    me = lax.axis_index("tensor")
    row, col = me // 2, me % 2
    sib = row * 2 + (1 - col)
    cross = (1 - row) * 2 + col
    diag = (1 - row) * 2 + (1 - col)

    own = pl.ds(pl.multiple_of(me * shard, shard), shard)
    loads = []
    for place, (src, dst) in enumerate(
        (
            (tokens_hbm, xr.at[0, own]),
            (wqkv_hbm, wqkv),
            (wout_hbm, wout),
            (wup_hbm, wup),
            (wdown_hbm, wdown),
            (cot_hbm, gf.at[own]),
        )
    ):
        load = pltpu.make_async_copy(src, dst, w_sem.at[place])
        load.start()
        loads.append(load)

    barrier = pltpu.get_barrier_semaphore()
    for peer in (sib, cross):
        pl.semaphore_signal(barrier, inc=1, device_id={"tensor": peer}, device_id_type=MESH)
    if inside:
        share = lax.axis_index("dp")
        far, near = share // NEAR, share % NEAR
        across = far * NEAR + (1 - near)
        distant = [((far + hop) % FAR_SIDE) * NEAR + near for hop in range(1, FAR_SIDE)]
        for peer in (across, *distant):
            pl.semaphore_signal(barrier, inc=1, device_id={"dp": peer}, device_id_type=MESH)
        pl.semaphore_wait(barrier, 3 + len(distant))
    else:
        pl.semaphore_wait(barrier, 2)

    def at_rows(owner, piece):
        return pl.ds(pl.multiple_of(owner * shard + piece * chunk, chunk), chunk)

    def span_rows(owner):
        return pl.ds(pl.multiple_of(owner * shard, shard), shard)

    def part(piece):
        return pl.ds(piece * chunk, chunk)

    def remote(src, dst, send, recv, peer, axis="tensor"):
        return pltpu.make_async_remote_copy(
            src_ref=src,
            dst_ref=dst,
            send_sem=send,
            recv_sem=recv,
            device_id={axis: peer},
            device_id_type=MESH,
        )

    def ag_copy(kind, phase, layer, piece, buf):
        owner, peer, send, recv = {
            "x": (me, cross, agx_s, agx_r),
            "s": (me, sib, ags_s, ags_r),
            "f": (cross, sib, agf_s, agf_r),
        }[kind]
        view = buf.at[at_rows(owner, piece)]
        return remote(view, view, send.at[phase, layer, piece], recv.at[phase, layer, piece], peer)

    def ag_recv(kind, phase, layer, piece, buf):
        owner, peer, send, recv = {
            "x": (cross, cross, agx_s, agx_r),
            "s": (sib, sib, ags_s, ags_r),
            "f": (diag, sib, agf_s, agf_r),
        }[kind]
        view = buf.at[at_rows(owner, piece)]
        return remote(view, view, send.at[phase, layer, piece], recv.at[phase, layer, piece], peer)

    def ag_send(phase, layer, piece, buf):
        ag_copy("x", phase, layer, piece, buf).start()
        ag_copy("s", phase, layer, piece, buf).start()

    def ag_forward(phase, layer, piece, buf):
        ag_recv("x", phase, layer, piece, buf).wait_recv()
        ag_copy("f", phase, layer, piece, buf).start()

    def ag_done(phase, layer, buf):
        for piece in range(CHUNKS):
            for kind in "xsf":
                ag_copy(kind, phase, layer, piece, buf).wait_send()

    def rs_copy(kind, phase, layer, piece):
        src, dst, send, recv, peer = {
            "d0": (d0s, d0r, d0_s, d0_r, sib),
            "d1": (d1s, d1r, d1_s, d1_r, sib),
            "x": (xsd, xrv, x_s, x_r, cross),
        }[kind]
        return remote(
            src.at[piece],
            dst.at[piece],
            send.at[phase, layer, piece],
            recv.at[phase, layer, piece],
            peer,
        )

    def rs_diag(phase, layer, piece, value):
        d0s[piece] = value.astype(BF16)
        rs_copy("d0", phase, layer, piece).start()

    def rs_cross(phase, layer, piece, value):
        rs_copy("d0", phase, layer, piece).wait_recv()
        xsd[piece] = (value + d0r[piece].astype(F32)).astype(BF16)
        rs_copy("x", phase, layer, piece).start()

    def rs_sib(phase, layer, piece, value):
        d1s[piece] = value.astype(BF16)
        rs_copy("d1", phase, layer, piece).start()

    def rs_final(phase, layer, piece):
        rs_copy("d1", phase, layer, piece).wait_recv()
        rs_copy("x", phase, layer, piece).wait_recv()
        total = keep[piece] + d1r[piece].astype(F32) + xrv[piece].astype(F32)
        for kind in ("d0", "d1", "x"):
            rs_copy(kind, phase, layer, piece).wait_send()
        return total

    def vec(layer, place):
        return vin_ref[layer, pl.ds(place, 1), :]

    def norm_forward(layer, piece, value, gain, shift, normed, inverse):
        centered = value - jnp.mean(value, axis=-1, keepdims=True)
        scale = lax.rsqrt(jnp.mean(centered * centered, axis=-1, keepdims=True) + EPSILON)
        unit = centered * scale
        normed[layer, part(piece), :] = unit.astype(BF16)
        inverse[layer, part(piece), :] = scale
        return unit * vec(layer, gain) + vec(layer, shift)

    def norm_backward(layer, piece, grad, gain, normed, inverse, rows):
        unit = normed[layer, part(piece), :].astype(F32)
        scale = inverse[layer, part(piece), :]
        scaled = grad * vec(layer, gain)
        out = scale * (
            scaled
            - jnp.mean(scaled, axis=-1, keepdims=True)
            - unit * jnp.mean(scaled * unit, axis=-1, keepdims=True)
        )
        gain_row, shift_row, bias_row = rows
        for place, term in ((gain_row, grad * unit), (shift_row, grad), (bias_row, out)):
            vout_ref[layer, pl.ds(place, 1), :] += jnp.sum(term, axis=0, keepdims=True)
        return out

    groups = []
    for begin in range(0, heads_width, 128):
        wide = min(128, heads_width - begin)
        groups.append((begin, wide, range(begin // HEAD_DIM, (begin + wide) // HEAD_DIM)))

    def only_head(value, begin, head):
        if value.shape[1] == HEAD_DIM:
            return value
        lane = lax.broadcasted_iota(jnp.int32, value.shape, 1)
        low = head * HEAD_DIM - begin
        return jnp.where((lane >= low) & (lane < low + HEAD_DIM), value, jnp.zeros_like(value))

    def window_of(span):
        return pl.ds(pl.multiple_of((span // LONGEST) * SPAN, SPAN), window)

    def attend(layer, span):
        rows = span_rows(span)
        keys = window_of(span)
        query_pos = span * SPAN + lax.broadcasted_iota(jnp.int32, (SPAN, 1), 0)
        picture = jnp.full((SPAN, 1), pic_ref[span], jnp.int32) == 1
        limit = jnp.where(picture, span * SPAN + SPAN - 1, query_pos)
        key_pos = (span // LONGEST) * SPAN + lax.broadcasted_iota(jnp.int32, (1, window), 1)
        first = jnp.full((1, window), doc_ref[span] * SPAN, jnp.int32)
        key_pos = jnp.where(key_pos >= first, key_pos, BEYOND)
        allowed = key_pos <= limit
        for begin, wide, heads in groups:
            cols = pl.ds(begin, wide)
            q_here = q_all[layer, rows, cols]
            k_here = k_all[layer, keys, cols]
            v_here = v_all[layer, keys, cols]
            total = jnp.zeros((SPAN, wide), F32)
            for head in heads:
                scores = dot_nt(only_head(q_here, begin, head), k_here)
                scores = jnp.where(allowed, scores, -1e30)
                raised = jnp.exp(scores - jnp.max(scores, axis=-1, keepdims=True))
                share = raised * (1.0 / jnp.sum(raised, axis=-1, keepdims=True))
                share = share.astype(BF16)
                prob[layer, span, head] = share
                total = total + dot_nn(share, only_head(v_here, begin, head))
            att[layer, rows, cols] = total.astype(BF16)

    def attend_back(layer, span):
        rows = span_rows(span)
        keys = window_of(span)
        for begin, wide, heads in groups:
            cols = pl.ds(begin, wide)
            q_here = q_all[layer, rows, cols]
            k_here = k_all[layer, keys, cols]
            v_here = v_all[layer, keys, cols]
            go_here = go[rows, cols]
            mixed = go_here.astype(F32) * att[layer, rows, cols].astype(F32)
            total = jnp.zeros((SPAN, wide), F32)
            key_total = gk[keys, cols]
            value_total = gv[keys, cols]
            for head in heads:
                go_head = only_head(go_here, begin, head)
                inner = jnp.sum(only_head(mixed, begin, head), axis=-1, keepdims=True)
                gp = dot_nt(go_head, v_here)
                share = prob[layer, span, head]
                gs = (share.astype(F32) * (gp - inner)).astype(BF16)
                total = total + dot_nn(gs, only_head(k_here, begin, head))
                key_total = key_total + dot_tn(gs, only_head(q_here, begin, head))
                value_total = value_total + dot_tn(share, go_head)
            gk[keys, cols] = key_total
            gv[keys, cols] = value_total
            gq[rows, cols] = (total * 0.125).astype(BF16)

    def project(layer, owner):
        rows = span_rows(owner)
        out = dot_nn(xr[layer, rows, :], wqkv[layer])
        query_bias = vin_ref[layer, pl.ds(7, 1), pl.ds(0, heads_width)]
        value_bias = vin_ref[layer, pl.ds(7, 1), pl.ds(256, heads_width)]
        q_all[layer, rows, :] = (
            (out[:, :heads_width] + query_bias) * 0.125
        ).astype(BF16)
        k_all[layer, rows, :] = out[:, heads_width : 2 * heads_width].astype(BF16)
        v_all[layer, rows, :] = (
            out[:, 2 * heads_width :] + value_bias
        ).astype(BF16)

    def two(buf, first, second, piece):
        return jnp.concatenate(
            (buf[at_rows(first, piece), :], buf[at_rows(second, piece), :]), axis=0
        )

    def ffn_rows(layer, first, second, piece):
        pre = dot_nn(two(hr.at[layer], first, second, piece), wup[layer]) + vec(layer, 6)
        value, grad = gelu_parts(pre)
        value, grad = value.astype(BF16), grad.astype(BF16)
        for place, owner in enumerate((first, second)):
            rows = at_rows(owner, piece)
            act[layer, rows, :] = value[place * chunk : (place + 1) * chunk]
            slope[layer, rows, :] = grad[place * chunk : (place + 1) * chunk]
        out = dot_nn(value, wdown[layer])
        return out[:chunk], out[chunk:]

    def ffn_back_rows(layer, first, second, piece):
        gu = dot_nt(two(gf, first, second, piece), wdown[layer])
        gpre = (gu * two(slope.at[layer], first, second, piece).astype(F32)).astype(BF16)
        for place, owner in enumerate((first, second)):
            slope[layer, at_rows(owner, piece), :] = gpre[place * chunk : (place + 1) * chunk]
        out = dot_nt(gpre, wup[layer])
        return out[:chunk], out[chunk:]

    def ffn_phase(phase, layer, buf, rows_of):
        for piece in range(CHUNKS):
            ag_recv("s", phase, layer, piece, buf).wait_recv()
            own_part, sib_part = rows_of(layer, me, sib, piece)
            rs_sib(phase, layer, piece, sib_part)
            keep[piece] = own_part
        for piece in range(CHUNKS):
            ag_forward(phase, layer, piece, buf)
            ag_recv("f", phase, layer, piece, buf).wait_recv()
            cross_part, diag_part = rows_of(layer, cross, diag, piece)
            rs_diag(phase, layer, piece, diag_part)
            rs_cross(phase, layer, piece, cross_part)
        ag_done(phase, layer, buf)

    def weight_grad(layer, left, right, begin, wide):
        def block(place, carry):
            cols = pl.ds(pl.multiple_of(place * 256, 256), 256)
            grads_ref[layer, cols, pl.ds(begin, wide)] = dot_tn(left[:, cols], right[...]).astype(
                BF16
            )
            return carry

        lax.fori_loop(0, width // 256, block, 0)

    each = width // (NEAR * FAR_SIDE)
    blocks = ((0, hidden), (hidden, hidden), (2 * hidden, 4 * heads_width))

    def slice_rows(owner):
        return pl.ds(pl.multiple_of(owner * each, each), each)

    def near_copy(layer, block, place):
        begin, wide = blocks[block]
        return remote(
            grads_ref.at[layer, slice_rows(place * NEAR + 1 - near), pl.ds(begin, wide)],
            y_buf.at[layer, place, :, pl.ds(begin, wide)],
            y_s.at[layer, block, place],
            y_r.at[layer, block, place],
            across,
            "dp",
        )

    def far_copy(layer, block, hop):
        begin, wide = blocks[block]
        return remote(
            grads_ref.at[layer, slice_rows(distant[hop]), pl.ds(begin, wide)],
            z_buf.at[layer, hop, :, pl.ds(begin, wide)],
            z_s.at[layer, block, hop],
            z_r.at[layer, block, hop],
            distant[hop],
            "dp",
        )

    def near_send(layer, block):
        if inside:
            for hop in NEAR_ORDER:
                near_copy(layer, block, far if hop is None else distant[hop] // NEAR).start()

    def near_part(layer, block, hop):
        begin, wide = blocks[block]
        cols = pl.ds(begin, wide)
        place = far if hop is None else distant[hop] // NEAR
        near_copy(layer, block, place).wait_recv()
        rows = slice_rows(place * NEAR + near)
        grads_ref[layer, rows, cols] = (
            grads_ref[layer, rows, cols].astype(F32) + y_buf[layer, place, :, cols].astype(F32)
        ).astype(BF16)
        if hop is not None:
            far_copy(layer, block, hop).start()

    def near_add(layer, block):
        if inside:
            for hop in NEAR_ORDER:
                near_part(layer, block, hop)

    staged = []

    def far_add(layer, block):
        begin, wide = blocks[block]
        cols = pl.ds(begin, wide)
        total = grads_ref[layer, slice_rows(share), cols].astype(F32)
        for hop in range(FAR_SIDE - 1):
            far_copy(layer, block, hop).wait_recv()
            total = total + z_buf[layer, hop, :, cols].astype(F32)
        slot = len(staged) % 2
        if len(staged) > 1:
            staged[-2].wait()
        stage[slot] = total
        staged.append(
            pltpu.make_async_copy(stage.at[slot], final_hbm.at[layer, :, cols], f_sem.at[slot])
        )
        staged[-1].start()
        for place in range(FAR_SIDE):
            near_copy(layer, block, place).wait_send()
        for hop in range(FAR_SIDE - 1):
            far_copy(layer, block, hop).wait_send()

    def vec_send(place, peers, axis):
        vsend[place] = vout_ref[...]
        copies = []
        for order, peer in enumerate(peers):
            slot = place + order
            copies.append(
                remote(vsend.at[place], vrecv.at[slot], v_s.at[slot], v_r.at[slot], peer, axis)
            )
        for copy in copies:
            copy.start()
        return copies, place

    def vec_add(pending, whole):
        copies, place = pending
        for order, copy in enumerate(copies):
            copy.wait_recv()
            term = vrecv[place + order]
            if not whole:
                line = lax.broadcasted_iota(jnp.int32, term.shape, 1)
                term = jnp.where(line < 6, term, 0.0)
            vout_ref[...] += term
        for copy in copies:
            copy.wait_send()

    for layer in range(layers):
        vin_ref[layer, 0:4, :] = obias_ref[layer].astype(F32)
        vin_ref[layer, 4:6, :] = gain_ref[layer].astype(F32)
        vin_ref[layer, 6:7, :] = ubias_ref[layer : layer + 1, :].astype(F32)
        for place in range(2):
            vin_ref[layer, 7:8, place * 256 : place * 256 + heads_width] = hbias_ref[
                layer, place : place + 1, :
            ].astype(F32)
    vout_ref[...] = jnp.zeros_like(vout_ref)
    loads[0].wait()
    for piece in range(CHUNKS):
        ag_send(FWD_ATTN, 0, piece, xr.at[0])
    cur[...] = xr[0, own, :].astype(F32)

    def forward(layer, carry):
        here = xr.at[layer]

        @pl.when(layer == 0)
        def _():
            loads[1].wait()

        project(layer, me)
        for piece in range(CHUNKS):
            ag_recv("s", FWD_ATTN, layer, piece, here).wait_recv()
        project(layer, sib)

        @pl.when(layer == 0)
        def _():
            for load in loads[2:]:
                load.wait()

        for piece in range(CHUNKS):
            ag_forward(FWD_ATTN, layer, piece, here)
        project(layer, cross)
        for piece in range(CHUNKS):
            ag_recv("f", FWD_ATTN, layer, piece, here).wait_recv()
        project(layer, diag)
        for owner, send in ((diag, rs_diag), (cross, rs_cross), (sib, rs_sib), (me, None)):
            attend(layer, owner)
            out = dot_nn(att[layer, span_rows(owner), :], wout[layer])
            for piece in range(CHUNKS):
                value = out[piece * chunk : (piece + 1) * chunk]
                if send is None:
                    keep[piece] = value
                else:
                    send(FWD_ATTN, layer, piece, value)
        ag_done(FWD_ATTN, layer, here)
        there = hr.at[layer]
        for piece in range(CHUNKS):
            value = cur[part(piece), :] + rs_final(FWD_ATTN, layer, piece) + vec(layer, 0)
            value = norm_forward(layer, piece, value, 4, 1, n_one, r_one)
            mid[part(piece), :] = value
            hr[layer, at_rows(me, piece), :] = value.astype(BF16)
            ag_send(FWD_FFN, layer, piece, there)
        ffn_phase(FWD_FFN, layer, there, ffn_rows)
        for piece in range(CHUNKS):
            value = mid[part(piece), :] + rs_final(FWD_FFN, layer, piece) + vec(layer, 2)
            value = norm_forward(layer, piece, value, 5, 3, n_two, r_two)
            cur[part(piece), :] = value

            @pl.when(layer + 1 < layers)
            def _():
                xr[layer + 1, at_rows(me, piece), :] = value.astype(BF16)
                ag_send(FWD_ATTN, layer + 1, piece, xr.at[layer + 1])

        return carry

    lax.fori_loop(0, layers, forward, 0)
    store = pltpu.make_async_copy(cur, result_hbm, w_sem.at[6])
    store.start()
    store.wait()

    cur[...] = gf[own, :].astype(F32)

    def backward(step, carry):
        layer = layers - 1 - step
        for piece in range(CHUNKS):
            grad = norm_backward(layer, piece, cur[part(piece), :], 5, n_two, r_two, (5, 3, 2))
            mid[part(piece), :] = grad
            gf[at_rows(me, piece), :] = grad.astype(BF16)
            ag_send(BWD_FFN, layer, piece, gf)

        @pl.when(step > 0)
        def _():
            near_add(layer + 1, 2)

        ffn_phase(BWD_FFN, layer, gf, ffn_back_rows)
        weight_grad(layer, gf, act.at[layer], hidden, hidden)
        near_send(layer, 1)
        for piece in range(CHUNKS):
            grad = mid[part(piece), :] + rs_final(BWD_FFN, layer, piece)
            grad = norm_backward(layer, piece, grad, 4, n_one, r_one, (4, 1, 0))
            cur[part(piece), :] = grad
            ga[at_rows(me, piece), :] = grad.astype(BF16)
            ag_send(BWD_ATTN, layer, piece, ga)
        weight_grad(layer, hr.at[layer], slope.at[layer], 0, hidden)
        near_send(layer, 0)
        vout_ref[layer, pl.ds(6, 1), :] = jnp.sum(
            slope[layer].astype(F32), axis=0, keepdims=True
        )
        gk[...] = jnp.zeros_like(gk)
        gv[...] = jnp.zeros_like(gv)

        def heads_grad(owner):
            rows = span_rows(owner)
            go[rows, :] = dot_nt(ga[rows, :], wout[layer]).astype(BF16)
            attend_back(layer, owner)

        heads_grad(me)
        for piece in range(CHUNKS):
            ag_recv("s", BWD_ATTN, layer, piece, ga).wait_recv()
        heads_grad(sib)
        near_add(layer, 1)
        for piece in range(CHUNKS):
            ag_forward(BWD_ATTN, layer, piece, ga)
        heads_grad(cross)
        for piece in range(CHUNKS):
            ag_recv("f", BWD_ATTN, layer, piece, ga).wait_recv()
        heads_grad(diag)
        for owner, send in ((diag, rs_diag), (cross, rs_cross), (sib, rs_sib), (me, None)):
            rows = span_rows(owner)
            joined = jnp.concatenate(
                (gq[rows, :], gk[rows, :].astype(BF16), gv[rows, :].astype(BF16)), axis=1
            )
            gqkv[rows, :] = joined
            out = dot_nt(joined, wqkv[layer])
            for piece in range(CHUNKS):
                value = out[piece * chunk : (piece + 1) * chunk]
                if send is None:
                    keep[piece] = value
                else:
                    send(BWD_ATTN, layer, piece, value)
        ag_done(BWD_ATTN, layer, ga)
        weight_grad(layer, xr.at[layer], gqkv, 2 * hidden, 3 * heads_width)
        weight_grad(layer, ga, att.at[layer], 2 * hidden + 3 * heads_width, heads_width)
        near_send(layer, 2)
        near_add(layer, 0)
        sums = jnp.sum(gqkv[...].astype(F32), axis=0, keepdims=True)
        vout_ref[layer, pl.ds(7, 1), pl.ds(0, heads_width)] = sums[:, :heads_width]
        vout_ref[layer, pl.ds(7, 1), pl.ds(256, heads_width)] = sums[:, 2 * heads_width :]
        for piece in range(CHUNKS):
            cur[part(piece), :] = cur[part(piece), :] + rs_final(BWD_ATTN, layer, piece)
        return carry

    lax.fori_loop(0, layers, backward, 0)
    store = pltpu.make_async_copy(cur, tgrad_hbm, w_sem.at[7])
    store.start()
    if inside:
        pending = vec_send(0, (sib,), "tensor")
        for layer in range(layers - 1, 0, -1):
            far_add(layer, 1)
            far_add(layer, 0)
        near_part(0, 2, NEAR_ORDER[0])
        vec_add(pending, False)
        pending = vec_send(1, (cross,), "tensor")
        for layer in range(layers - 1, 0, -1):
            far_add(layer, 2)
        near_part(0, 2, NEAR_ORDER[1])
        vec_add(pending, False)
        pending = vec_send(2, (across,), "dp")
        near_part(0, 2, NEAR_ORDER[2])
        vec_add(pending, True)
        pending = vec_send(3, distant, "dp")
        near_part(0, 2, NEAR_ORDER[3])
        far_add(0, 1)
        far_add(0, 0)
        vec_add(pending, True)
        far_add(0, 2)
        for copy in staged[-2:]:
            copy.wait()
    store.wait()


def finish_kernel(hidden, heads_width, result, tgrad, vout, main, *outs):
    layers, each, _ = main.shape
    fine = each // GROUP
    head_each = heads_width // (NEAR * FAR_SIDE)
    place, mine = lax.axis_index("dp"), lax.axis_index("tensor")
    res_o, tg_o, qkv_o, head_o, out_o, up_o, ubias_o, down_o, obias_o, gain_o = outs
    res_o[...] = result[...]
    tg_o[...] = tgrad[...]

    def shifted(value, begin):
        return pltpu.roll(value, value.shape[1] - begin, 1)

    for layer in range(layers):
        up_o[layer] = main[layer, :, :hidden]
        down_o[layer] = main[layer, :, hidden : 2 * hidden].T
        qkv_o[layer] = main[layer, :, 2 * hidden : 2 * hidden + 3 * heads_width]
        out_o[layer] = main[layer, :, 2 * hidden + 3 * heads_width :].T
        whole = vout[layer]
        picked = shifted(whole, place * each + mine * fine)
        obias_o[layer] = picked[0:4, :fine]
        gain_o[layer] = picked[4:6, :fine]
        ubias_o[layer : layer + 1, :] = shifted(whole, place * each)[6:7, :each]
        picked = shifted(whole, place * head_each)
        head_o[layer, 0:1, :] = picked[7:8, :head_each]
        head_o[layer, 1:2, :] = picked[7:8, 256 : 256 + head_each]


def finish(result, tokens_grad, vout, main, hidden, heads_width):
    layers, each, _ = main.shape
    fine = each // GROUP
    head_each = heads_width // (NEAR * FAR_SIDE)
    shapes = (
        result.shape,
        tokens_grad.shape,
        (layers, each, 3 * heads_width),
        (layers, 2, head_each),
        (layers, heads_width, each),
        (layers, each, hidden),
        (layers, each),
        (layers, hidden, each),
        (layers, 4, fine),
        (layers, 2, fine),
    )
    outs = pl.pallas_call(
        partial(finish_kernel, hidden, heads_width),
        name="finish",
        out_shape=tuple(jax.ShapeDtypeStruct(shape, F32) for shape in shapes),
        in_specs=[pl.BlockSpec(memory_space=pltpu.VMEM)] * 4,
        out_specs=tuple(pl.BlockSpec(memory_space=pltpu.VMEM) for _ in shapes),
    )(result, tokens_grad, vout, main)
    return (
        *outs[:2],
        outs[2].reshape(layers, each, 3, heads_width),
        *outs[3:],
    )


def body(
    tokens,
    qkv_weight,
    qv_bias,
    out_weight,
    up_weight,
    up_bias,
    down_weight,
    out_bias,
    norm_gain,
    doc_start,
    picture,
    cotangent,
):
    layers, width, _, heads_width = qkv_weight.shape
    shard = tokens.shape[0]
    seq = shard * GROUP
    hidden = up_weight.shape[2]
    spans = seq // SPAN
    heads = heads_width // HEAD_DIM
    total_width = 4 * heads_width + 2 * hidden
    chunk = shard // CHUNKS
    wide = max(hidden, width)
    vmem = partial(pl.BlockSpec, memory_space=pltpu.VMEM)
    smem = partial(pl.BlockSpec, memory_space=pltpu.SMEM)
    anywhere = partial(pl.BlockSpec, memory_space=pl.ANY)
    sems = pltpu.SemaphoreType.DMA((4, layers, CHUNKS))
    shares = lax.axis_size("dp")
    inside = shares == NEAR * FAR_SIDE
    rows_each = width // shares
    outputs = [
        jax.ShapeDtypeStruct((shard, width), F32),
        jax.ShapeDtypeStruct((shard, width), F32),
        jax.ShapeDtypeStruct((layers, 8, wide), F32),
    ]
    dma = pltpu.SemaphoreType.DMA
    first, last = [], []
    if inside:
        outputs.append(jax.ShapeDtypeStruct((layers, rows_each, total_width), F32))
        first = [pltpu.VMEM((layers, width, total_width), BF16)]
        last = [
            pltpu.VMEM((2, rows_each, hidden), F32),
            dma((2,)),
            pltpu.VMEM((4, layers, 8, wide), F32),
            pltpu.VMEM((2 + FAR_SIDE, layers, 8, wide), F32),
            pltpu.VMEM((layers, FAR_SIDE, rows_each, total_width), BF16),
            pltpu.VMEM((layers, FAR_SIDE - 1, rows_each, total_width), BF16),
            dma((layers, 3, FAR_SIDE)),
            dma((layers, 3, FAR_SIDE)),
            dma((layers, 3, FAR_SIDE - 1)),
            dma((layers, 3, FAR_SIDE - 1)),
            dma((2 + FAR_SIDE,)),
            dma((2 + FAR_SIDE,)),
        ]
    else:
        outputs.append(jax.ShapeDtypeStruct((layers, width, total_width), BF16))
    result, tokens_grad, vout, grads = pl.pallas_call(
        partial(step_kernel, inside),
        name="encoder_step",
        out_shape=tuple(outputs),
        in_specs=[anywhere()] * 2 + [vmem()] * 4 + [smem()] * 2 + [anywhere()] * 4,
        out_specs=(anywhere(), anywhere(), vmem(), anywhere() if inside else vmem()),
        scratch_shapes=first
        + [
            pltpu.VMEM((layers, width, 3 * heads_width), BF16),
            pltpu.VMEM(out_weight.shape, BF16),
            pltpu.VMEM(up_weight.shape, BF16),
            pltpu.VMEM(down_weight.shape, BF16),
            pltpu.VMEM((layers, seq, width), BF16),
            pltpu.VMEM((layers, seq, heads_width), BF16),
            pltpu.VMEM((layers, seq, heads_width), BF16),
            pltpu.VMEM((layers, seq, heads_width), BF16),
            pltpu.VMEM((layers, spans, heads, SPAN, LONGEST * SPAN), BF16),
            pltpu.VMEM((layers, seq, heads_width), BF16),
            pltpu.VMEM((layers, seq, width), BF16),
            pltpu.VMEM((layers, seq, hidden), BF16),
            pltpu.VMEM((layers, seq, hidden), BF16),
            pltpu.VMEM((layers, shard, width), BF16),
            pltpu.VMEM((layers, shard, 1), F32),
            pltpu.VMEM((layers, shard, width), BF16),
            pltpu.VMEM((layers, shard, 1), F32),
            pltpu.VMEM((seq, width), BF16),
            pltpu.VMEM((seq, width), BF16),
            pltpu.VMEM((seq, heads_width), BF16),
            pltpu.VMEM((seq, heads_width), BF16),
            pltpu.VMEM((seq, heads_width), F32),
            pltpu.VMEM((seq, heads_width), F32),
            pltpu.VMEM((seq, 3 * heads_width), BF16),
            pltpu.VMEM((shard, width), F32),
            pltpu.VMEM((shard, width), F32),
        ]
        + [pltpu.VMEM((CHUNKS, chunk, width), BF16)] * 6
        + [pltpu.VMEM((CHUNKS, chunk, width), F32), pltpu.SemaphoreType.DMA((8,))]
        + [sems] * 12
        + last
        + [pltpu.VMEM((layers, 8, wide), F32)],
        compiler_params=pltpu.CompilerParams(
            collective_id=0, has_side_effects=True, vmem_limit_bytes=67043328
        ),
    )(
        tokens,
        cotangent,
        out_bias,
        norm_gain,
        up_bias,
        qv_bias,
        doc_start,
        picture,
        qkv_weight.reshape(layers, width, 3 * heads_width),
        out_weight,
        up_weight,
        down_weight,
    )
    head_each = heads_width // shares
    up_each = hidden // shares
    place = lax.axis_index("dp")
    if inside:
        return finish(result, tokens_grad, vout, grads, hidden, heads_width)
    else:
        main = jnp.stack(
            [
                lax.psum_scatter(grads[layer], "dp", scatter_dimension=0, tiled=True).astype(F32)
                for layer in range(layers)
            ]
        )
        vector_sum = lax.psum(vout[:, :6], ("dp", "tensor"))
        bias_sum = lax.psum(vout[:, 6:], "dp")
    qkv_part = main[:, :, 2 * hidden : 2 * hidden + 3 * heads_width].reshape(
        layers, rows_each, 3, heads_width
    )
    out_part = main[:, :, 2 * hidden + 3 * heads_width :].transpose(0, 2, 1)
    up_part = main[:, :, :hidden]
    down_part = main[:, :, hidden : 2 * hidden].transpose(0, 2, 1)
    fine = width // (shares * GROUP)
    vector_sum = lax.dynamic_slice_in_dim(
        vector_sum, place * rows_each + lax.axis_index("tensor") * fine, fine, 2
    )
    head_sum = jnp.stack(
        (bias_sum[:, 1, :heads_width], bias_sum[:, 1, 256 : 256 + heads_width]), axis=1
    )
    return (
        result,
        tokens_grad,
        qkv_part,
        lax.dynamic_slice_in_dim(head_sum, place * head_each, head_each, 2),
        out_part,
        up_part,
        lax.dynamic_slice_in_dim(bias_sum[:, 0, :hidden], place * up_each, up_each, 1),
        down_part,
        vector_sum[:, :4],
        vector_sum[:, 4:],
    )


def solution(mesh):
    return jax.shard_map(
        body,
        mesh=mesh,
        in_specs=(
            P(("dp", "tensor"), None),
            P(None, None, None, "tensor"),
            P(None, None, "tensor"),
            P(None, "tensor", None),
            P(None, None, "tensor"),
            P(None, "tensor"),
            P(None, "tensor", None),
            P(),
            P(),
            P("dp"),
            P("dp"),
            P(("dp", "tensor"), None),
        ),
        out_specs=(
            P(("dp", "tensor"), None),
            P(("dp", "tensor"), None),
            P(None, "dp", None, "tensor"),
            P(None, None, ("tensor", "dp")),
            P(None, "tensor", "dp"),
            P(None, "dp", "tensor"),
            P(None, ("tensor", "dp")),
            P(None, "tensor", "dp"),
            P(None, None, ("dp", "tensor")),
            P(None, None, ("dp", "tensor")),
        ),
        check_vma=False,
    )
```

```python
from functools import partial

import jax
import jax.numpy as jnp
from jax import lax
from jax.experimental import pallas as pl
from jax.experimental.pallas import tpu as pltpu
from jax.sharding import PartitionSpec as P

HEAD_DIM = 64
SPAN = 256
GROUP = 4
LONGEST = 3
CHUNKS = 2
HALVES = 2
EPSILON = 1e-05
BEYOND = 1 << 20
NEAR, FAR_SIDE = 2, 4
NEAR_ORDER = (1, 0, 2, None)
OUT_WIDE, QKV_WIDE = 256, 640
UP, DOWN, OUT, QKV = range(4)
F32 = jnp.float32
BF16 = jnp.bfloat16
MESH = pl.DeviceIdType.MESH
FWD_ATTN, FWD_FFN, BWD_FFN, BWD_ATTN = range(4)


def dot_nn(left, right):
    return lax.dot_general(left, right, (((1,), (0,)), ((), ())), preferred_element_type=F32)


def dot_nt(left, right):
    return lax.dot_general(left, right, (((1,), (1,)), ((), ())), preferred_element_type=F32)


def dot_tn(left, right):
    return lax.dot_general(left, right, (((0,), (0,)), ((), ())), preferred_element_type=F32)


def gelu_parts(value):
    cdf = 0.5 * (1.0 + lax.erf(value * 0.7071067811865476))
    density = jnp.exp(-0.5 * value * value) * 0.3989422804014327
    return value * cdf, cdf + value * density


def step_kernel(inside, *refs):
    (
        tokens_hbm,
        cot_hbm,
        obias_ref,
        gain_ref,
        ubias_ref,
        hbias_ref,
        doc_ref,
        pic_ref,
        wqkv_hbm,
        wout_hbm,
        wup_hbm,
        wdown_hbm,
        result_hbm,
        tgrad_hbm,
        vout_ref,
        *refs,
    ) = refs
    *refs, vin_ref = refs
    if inside:
        final_hbm, *refs = refs
        *refs, stage, f_sem, vsend, vrecv, y_buf, z_buf, y_s, y_r, z_s, z_r, v_s, v_r = refs
    (
        grads_ref,
        wqkv,
        wout,
        wup,
        wdown,
        xr,
        q_all,
        k_all,
        v_all,
        prob,
        att,
        hr,
        act,
        slope,
        n_one,
        r_one,
        n_two,
        r_two,
        gf,
        ga,
        go,
        gq,
        gk,
        gv,
        gqkv,
        cur,
        mid,
        d0s,
        d0r,
        d1s,
        d1r,
        xsd,
        xrv,
        keep,
        w_sem,
        agx_s,
        agx_r,
        ags_s,
        ags_r,
        agf_s,
        agf_r,
        d0_s,
        d0_r,
        d1_s,
        d1_r,
        x_s,
        x_r,
    ) = refs
    layers = obias_ref.shape[0]
    shard, width = tokens_hbm.shape
    chunk = shard // CHUNKS
    part_rows = shard // HALVES
    heads_width = att.shape[2]
    hidden = wup.shape[2]
    me = lax.axis_index("tensor")
    row, col = me // 2, me % 2
    sib = row * 2 + (1 - col)
    cross = (1 - row) * 2 + col
    diag = (1 - row) * 2 + (1 - col)

    own = pl.ds(pl.multiple_of(me * shard, shard), shard)
    loads = []
    for place, (src, dst) in enumerate(
        (
            (tokens_hbm, xr.at[0, own]),
            (wqkv_hbm, wqkv),
            (wout_hbm, wout),
            (wup_hbm, wup),
            (wdown_hbm, wdown),
            (cot_hbm, gf.at[own]),
        )
    ):
        load = pltpu.make_async_copy(src, dst, w_sem.at[place])
        load.start()
        loads.append(load)

    barrier = pltpu.get_barrier_semaphore()
    for peer in (sib, cross):
        pl.semaphore_signal(barrier, inc=1, device_id={"tensor": peer}, device_id_type=MESH)
    if inside:
        share = lax.axis_index("dp")
        far, near = share // NEAR, share % NEAR
        across = far * NEAR + (1 - near)
        distant = [((far + hop) % FAR_SIDE) * NEAR + near for hop in range(1, FAR_SIDE)]
        for peer in (across, *distant):
            pl.semaphore_signal(barrier, inc=1, device_id={"dp": peer}, device_id_type=MESH)
        pl.semaphore_wait(barrier, 3 + len(distant))
    else:
        pl.semaphore_wait(barrier, 2)

    def at_rows(owner, piece):
        return pl.ds(pl.multiple_of(owner * shard + piece * chunk, chunk), chunk)

    def half_rows(owner, half):
        return pl.ds(pl.multiple_of(owner * shard + half * part_rows, part_rows), part_rows)

    def span_rows(owner):
        return pl.ds(pl.multiple_of(owner * shard, shard), shard)

    def part(piece):
        return pl.ds(piece * chunk, chunk)

    def remote(src, dst, send, recv, peer, axis="tensor"):
        return pltpu.make_async_remote_copy(
            src_ref=src,
            dst_ref=dst,
            send_sem=send,
            recv_sem=recv,
            device_id={axis: peer},
            device_id_type=MESH,
        )

    def ag_copy(kind, phase, layer, piece, buf):
        owner, peer, send, recv = {
            "x": (me, cross, agx_s, agx_r),
            "s": (me, sib, ags_s, ags_r),
            "f": (cross, sib, agf_s, agf_r),
        }[kind]
        view = buf.at[at_rows(owner, piece)]
        return remote(view, view, send.at[phase, layer, piece], recv.at[phase, layer, piece], peer)

    def ag_recv(kind, phase, layer, piece, buf):
        owner, peer, send, recv = {
            "x": (cross, cross, agx_s, agx_r),
            "s": (sib, sib, ags_s, ags_r),
            "f": (diag, sib, agf_s, agf_r),
        }[kind]
        view = buf.at[at_rows(owner, piece)]
        return remote(view, view, send.at[phase, layer, piece], recv.at[phase, layer, piece], peer)

    def ag_send(phase, layer, piece, buf):
        ag_copy("x", phase, layer, piece, buf).start()
        ag_copy("s", phase, layer, piece, buf).start()

    def ag_forward(phase, layer, piece, buf):
        ag_recv("x", phase, layer, piece, buf).wait_recv()
        ag_copy("f", phase, layer, piece, buf).start()

    def ag_done(phase, layer, buf):
        for piece in range(CHUNKS):
            for kind in "xsf":
                ag_copy(kind, phase, layer, piece, buf).wait_send()

    def rs_copy(kind, phase, layer, piece):
        src, dst, send, recv, peer = {
            "d0": (d0s, d0r, d0_s, d0_r, sib),
            "d1": (d1s, d1r, d1_s, d1_r, sib),
            "x": (xsd, xrv, x_s, x_r, cross),
        }[kind]
        return remote(
            src.at[piece],
            dst.at[piece],
            send.at[phase, layer, piece],
            recv.at[phase, layer, piece],
            peer,
        )

    def rs_diag(phase, layer, piece, value):
        d0s[piece] = value.astype(BF16)
        rs_copy("d0", phase, layer, piece).start()

    def rs_cross(phase, layer, piece, value):
        rs_copy("d0", phase, layer, piece).wait_recv()
        xsd[piece] = (value + d0r[piece].astype(F32)).astype(BF16)
        rs_copy("x", phase, layer, piece).start()

    def rs_sib(phase, layer, piece, value):
        d1s[piece] = value.astype(BF16)
        rs_copy("d1", phase, layer, piece).start()

    def place_part(phase, layer, pair, which, piece, value):
        @pl.when((pair == 0) & (which == 0))
        def _():
            rs_diag(phase, layer, piece, value)

        @pl.when((pair == 0) & (which == 1))
        def _():
            rs_cross(phase, layer, piece, value)

        @pl.when((pair == 1) & (which == 0))
        def _():
            rs_sib(phase, layer, piece, value)

        @pl.when((pair == 1) & (which == 1))
        def _():
            keep[piece] = value

    def rs_final(phase, layer, piece):
        rs_copy("d1", phase, layer, piece).wait_recv()
        rs_copy("x", phase, layer, piece).wait_recv()
        total = keep[piece] + d1r[piece].astype(F32) + xrv[piece].astype(F32)
        for kind in ("d0", "d1", "x"):
            rs_copy(kind, phase, layer, piece).wait_send()
        return total

    def vec(layer, place):
        return vin_ref[layer, pl.ds(place, 1), :]

    def norm_forward(layer, piece, value, gain, shift, normed, inverse):
        centered = value - jnp.mean(value, axis=-1, keepdims=True)
        scale = lax.rsqrt(jnp.mean(centered * centered, axis=-1, keepdims=True) + EPSILON)
        unit = centered * scale
        normed[layer, part(piece), :] = unit.astype(BF16)
        inverse[layer, part(piece), :] = scale
        return unit * vec(layer, gain) + vec(layer, shift)

    def norm_backward(layer, piece, grad, gain, normed, inverse, rows):
        unit = normed[layer, part(piece), :].astype(F32)
        scale = inverse[layer, part(piece), :]
        scaled = grad * vec(layer, gain)
        out = scale * (
            scaled
            - jnp.mean(scaled, axis=-1, keepdims=True)
            - unit * jnp.mean(scaled * unit, axis=-1, keepdims=True)
        )
        gain_row, shift_row, bias_row = rows
        for place, term in ((gain_row, grad * unit), (shift_row, grad), (bias_row, out)):
            vout_ref[layer, pl.ds(place, 1), :] += jnp.sum(term, axis=0, keepdims=True)
        return out

    groups = []
    for begin in range(0, heads_width, 128):
        wide = min(128, heads_width - begin)
        groups.append((begin, wide, range(begin // HEAD_DIM, (begin + wide) // HEAD_DIM)))

    def only_head(value, begin, head):
        if value.shape[1] == HEAD_DIM:
            return value
        lane = lax.broadcasted_iota(jnp.int32, value.shape, 1)
        low = head * HEAD_DIM - begin
        return jnp.where((lane >= low) & (lane < low + HEAD_DIM), value, jnp.zeros_like(value))

    def by_keys(span, run):
        for count in range(1, LONGEST + 1):

            @pl.when((span == count - 1) if count < LONGEST else (span >= count - 1))
            def _():
                run(count)

    def keys_of(span, count):
        if count < LONGEST:
            return 0, pl.ds(0, count * SPAN), (count * (count - 1)) // 2
        begin = span - (LONGEST - 1)
        rows = pl.ds(pl.multiple_of(begin * SPAN, SPAN), LONGEST * SPAN)
        return begin * SPAN, rows, LONGEST * (span - 1)

    def attend(layer, span, half, count):
        rows = half_rows(span, half)
        first_key, keys, base = keys_of(span, count)
        query_pos = (
            span * SPAN + half * part_rows + lax.broadcasted_iota(jnp.int32, (part_rows, 1), 0)
        )
        picture = jnp.full((part_rows, 1), pic_ref[span], jnp.int32) == 1
        limit = jnp.where(picture, span * SPAN + SPAN - 1, query_pos)
        key_pos = first_key + lax.broadcasted_iota(jnp.int32, (1, count * SPAN), 1)
        first = jnp.full((1, count * SPAN), doc_ref[span] * SPAN, jnp.int32)
        key_pos = jnp.where(key_pos >= first, key_pos, BEYOND)
        allowed = key_pos <= limit
        for begin, wide, heads in groups:
            cols = pl.ds(begin, wide)
            q_here = q_all[layer, rows, cols]
            k_here = k_all[layer, keys, cols]
            v_here = v_all[layer, keys, cols]
            total = jnp.zeros((part_rows, wide), F32)
            for head in heads:
                scores = dot_nt(only_head(q_here, begin, head), k_here)
                scores = jnp.where(allowed, scores, -1e30)
                raised = jnp.exp(scores - jnp.max(scores, axis=-1, keepdims=True))
                share = raised * (1.0 / jnp.sum(raised, axis=-1, keepdims=True))
                share = share.astype(BF16)
                for block in range(count):
                    prob[layer, head, base + block, pl.ds(half * part_rows, part_rows), :] = share[
                        :, block * SPAN : (block + 1) * SPAN
                    ]
                total = total + dot_nn(share, only_head(v_here, begin, head))
            att[layer, rows, cols] = total.astype(BF16)

    def attend_back(layer, span, count):
        rows = span_rows(span)
        _, keys, base = keys_of(span, count)
        for begin, wide, heads in groups:
            cols = pl.ds(begin, wide)
            q_here = q_all[layer, rows, cols]
            k_here = k_all[layer, keys, cols]
            v_here = v_all[layer, keys, cols]
            go_here = go[rows, cols]
            mixed = go_here.astype(F32) * att[layer, rows, cols].astype(F32)
            total = jnp.zeros((SPAN, wide), F32)
            key_total = gk[keys, cols]
            value_total = gv[keys, cols]
            for head in heads:
                go_head = only_head(go_here, begin, head)
                inner = jnp.sum(only_head(mixed, begin, head), axis=-1, keepdims=True)
                gp = dot_nt(go_head, v_here)
                share = jnp.concatenate(
                    [prob[layer, head, base + block] for block in range(count)], axis=1
                )
                gs = (share.astype(F32) * (gp - inner)).astype(BF16)
                total = total + dot_nn(gs, only_head(k_here, begin, head))
                key_total = key_total + dot_tn(gs, only_head(q_here, begin, head))
                value_total = value_total + dot_tn(share, go_head)
            gk[keys, cols] = key_total
            gv[keys, cols] = value_total
            gq[rows, cols] = (total * 0.125).astype(BF16)

    def member(pair, which):
        line = (1 - pair) * (1 - row) + pair * row
        return line * 2 + (1 - which) * (1 - col) + which * col

    def project(layer, owner):
        rows = span_rows(owner)
        out = dot_nt(xr[layer, rows, :], wqkv[layer])
        query_bias = vin_ref[layer, pl.ds(7, 1), pl.ds(0, heads_width)]
        value_bias = vin_ref[layer, pl.ds(7, 1), pl.ds(256, heads_width)]
        q_all[layer, rows, :] = (
            (out[:, :heads_width] + query_bias) * 0.125
        ).astype(BF16)
        k_all[layer, rows, :] = out[:, heads_width : 2 * heads_width].astype(BF16)
        v_all[layer, rows, :] = (
            out[:, 2 * heads_width :] + value_bias
        ).astype(BF16)

    def two(buf, first, second, piece):
        return jnp.concatenate(
            (buf[at_rows(first, piece), :], buf[at_rows(second, piece), :]), axis=0
        )

    def ffn_rows(layer, first, second, piece):
        pre = dot_nn(two(hr.at[layer], first, second, piece), wup[layer]) + vec(layer, 6)
        value, grad = gelu_parts(pre)
        value, grad = value.astype(BF16), grad.astype(BF16)
        for place, owner in enumerate((first, second)):
            rows = at_rows(owner, piece)
            act[layer, rows, :] = value[place * chunk : (place + 1) * chunk]
            slope[layer, rows, :] = grad[place * chunk : (place + 1) * chunk]
        out = dot_nn(value, wdown[layer])
        return out[:chunk], out[chunk:]

    def ffn_back_rows(layer, first, second, piece):
        gu = dot_nt(two(gf, first, second, piece), wdown[layer])
        gpre = (gu * two(slope.at[layer], first, second, piece).astype(F32)).astype(BF16)
        for place, owner in enumerate((first, second)):
            slope[layer, at_rows(owner, piece), :] = gpre[place * chunk : (place + 1) * chunk]
        out = dot_nt(gpre, wup[layer])
        return out[:chunk], out[chunk:]

    def ffn_phase(phase, layer, buf, rows_of):
        for piece in range(CHUNKS):
            ag_recv("s", phase, layer, piece, buf).wait_recv()
            own_part, sib_part = rows_of(layer, me, sib, piece)
            rs_sib(phase, layer, piece, sib_part)
            keep[piece] = own_part
        for piece in range(CHUNKS):
            ag_forward(phase, layer, piece, buf)
            ag_recv("f", phase, layer, piece, buf).wait_recv()
            cross_part, diag_part = rows_of(layer, cross, diag, piece)
            rs_diag(phase, layer, piece, diag_part)
            rs_cross(phase, layer, piece, cross_part)
        ag_done(phase, layer, buf)

    def weight_grad(layer, left, right, begin, wide):
        def block(place, carry):
            cols = pl.ds(pl.multiple_of(place * 256, 256), 256)
            grads_ref[layer, cols, pl.ds(begin, wide)] = dot_tn(left[:, cols], right[...]).astype(
                BF16
            )
            return carry

        lax.fori_loop(0, width // 256, block, 0)

    each = width // (NEAR * FAR_SIDE)
    blocks = (
        (0, hidden),
        (hidden, hidden),
        (2 * hidden, OUT_WIDE),
        (2 * hidden + OUT_WIDE, QKV_WIDE),
    )

    def slice_rows(owner):
        return pl.ds(pl.multiple_of(owner * each, each), each)

    def near_copy(layer, block, place):
        begin, wide = blocks[block]
        return remote(
            grads_ref.at[layer, slice_rows(place * NEAR + 1 - near), pl.ds(begin, wide)],
            y_buf.at[layer, place, :, pl.ds(begin, wide)],
            y_s.at[layer, block, place],
            y_r.at[layer, block, place],
            across,
            "dp",
        )

    def far_copy(layer, block, hop):
        begin, wide = blocks[block]
        return remote(
            grads_ref.at[layer, slice_rows(distant[hop]), pl.ds(begin, wide)],
            z_buf.at[layer, hop, :, pl.ds(begin, wide)],
            z_s.at[layer, block, hop],
            z_r.at[layer, block, hop],
            distant[hop],
            "dp",
        )

    def near_send(layer, block):
        if inside:
            for hop in NEAR_ORDER:
                near_copy(layer, block, far if hop is None else distant[hop] // NEAR).start()

    def near_part(layer, block, hop):
        begin, wide = blocks[block]
        cols = pl.ds(begin, wide)
        place = far if hop is None else distant[hop] // NEAR
        near_copy(layer, block, place).wait_recv()
        rows = slice_rows(place * NEAR + near)
        grads_ref[layer, rows, cols] = (
            grads_ref[layer, rows, cols].astype(F32) + y_buf[layer, place, :, cols].astype(F32)
        ).astype(BF16)
        if hop is not None:
            far_copy(layer, block, hop).start()

    def near_add(layer, block):
        if inside:
            for hop in NEAR_ORDER:
                near_part(layer, block, hop)

    staged = []

    def far_add(layer, block):
        begin, wide = blocks[block]
        cols = pl.ds(begin, wide)
        total = grads_ref[layer, slice_rows(share), cols].astype(F32)
        for hop in range(FAR_SIDE - 1):
            far_copy(layer, block, hop).wait_recv()
            total = total + z_buf[layer, hop, :, cols].astype(F32)
        slot = len(staged) % 2
        if len(staged) > 1:
            staged[-2].wait()
        stage[slot, :, pl.ds(0, wide)] = total
        staged.append(
            pltpu.make_async_copy(
                stage.at[slot, :, pl.ds(0, wide)], final_hbm.at[layer, :, cols], f_sem.at[slot]
            )
        )
        staged[-1].start()
        for place in range(FAR_SIDE):
            near_copy(layer, block, place).wait_send()
        for hop in range(FAR_SIDE - 1):
            far_copy(layer, block, hop).wait_send()

    def vec_copies(place, peers, axis):
        copies = []
        for order, peer in enumerate(peers):
            slot = place + order
            copies.append(
                remote(vsend.at[place], vrecv.at[slot], v_s.at[slot], v_r.at[slot], peer, axis)
            )
        return copies, place

    def vec_send(place, peers, axis):
        vsend[place] = vout_ref[...]
        for copy in vec_copies(place, peers, axis)[0]:
            copy.start()

    def vec_add(pending, whole):
        copies, place = pending
        for order, copy in enumerate(copies):
            copy.wait_recv()
            term = vrecv[place + order]
            if not whole:
                line = lax.broadcasted_iota(jnp.int32, term.shape, 1)
                term = jnp.where(line < 6, term, 0.0)
            vout_ref[...] += term
        for copy in copies:
            copy.wait_send()

    for layer in range(layers):
        vin_ref[layer, 0:4, :] = obias_ref[layer].astype(F32)
        vin_ref[layer, 4:6, :] = gain_ref[layer].astype(F32)
        vin_ref[layer, 6:7, :] = ubias_ref[layer : layer + 1, :].astype(F32)
        for place in range(2):
            vin_ref[layer, 7:8, place * 256 : place * 256 + heads_width] = hbias_ref[
                layer, place : place + 1, :
            ].astype(F32)
    vout_ref[...] = jnp.zeros_like(vout_ref)
    for begin, wide, room in (
        (2 * hidden, heads_width, OUT_WIDE),
        (2 * hidden + OUT_WIDE, 3 * heads_width, QKV_WIDE),
    ):
        blank = (layers, width, room - wide)
        grads_ref[:, :, begin + wide : begin + room] = jnp.zeros(blank, BF16)
    loads[0].wait()
    for piece in range(CHUNKS):
        ag_send(FWD_ATTN, 0, piece, xr.at[0])
    cur[...] = xr[0, own, :].astype(F32)

    def forward(layer, carry):
        here = xr.at[layer]

        @pl.when(layer == 0)
        def _():
            loads[1].wait()

        project(layer, me)
        for piece in range(CHUNKS):
            ag_recv("s", FWD_ATTN, layer, piece, here).wait_recv()
        project(layer, sib)

        @pl.when(layer == 0)
        def _():
            for load in loads[2:]:
                load.wait()

        for piece in range(CHUNKS):
            ag_forward(FWD_ATTN, layer, piece, here)
        project(layer, cross)
        for piece in range(CHUNKS):
            ag_recv("f", FWD_ATTN, layer, piece, here).wait_recv()
        project(layer, diag)

        def heads_out(turn, inner):
            pair, half, which = turn // (2 * HALVES), (turn % (2 * HALVES)) // 2, turn % 2
            owner = member(pair, which)
            by_keys(owner, partial(attend, layer, owner, half))
            out = dot_nn(att[layer, half_rows(owner, half), :], wout[layer])
            for piece in range(CHUNKS // HALVES):
                place_part(
                    FWD_ATTN,
                    layer,
                    pair,
                    which,
                    half * (CHUNKS // HALVES) + piece,
                    out[piece * chunk : (piece + 1) * chunk],
                )
            return inner

        lax.fori_loop(0, 4 * HALVES, heads_out, 0)
        ag_done(FWD_ATTN, layer, here)
        there = hr.at[layer]
        for piece in range(CHUNKS):
            value = cur[part(piece), :] + rs_final(FWD_ATTN, layer, piece) + vec(layer, 0)
            value = norm_forward(layer, piece, value, 4, 1, n_one, r_one)
            mid[part(piece), :] = value
            hr[layer, at_rows(me, piece), :] = value.astype(BF16)
            ag_send(FWD_FFN, layer, piece, there)
        ffn_phase(FWD_FFN, layer, there, ffn_rows)
        for piece in range(CHUNKS):
            value = mid[part(piece), :] + rs_final(FWD_FFN, layer, piece) + vec(layer, 2)
            value = norm_forward(layer, piece, value, 5, 3, n_two, r_two)
            cur[part(piece), :] = value

            @pl.when(layer + 1 < layers)
            def _():
                xr[layer + 1, at_rows(me, piece), :] = value.astype(BF16)
                ag_send(FWD_ATTN, layer + 1, piece, xr.at[layer + 1])

        return carry

    lax.fori_loop(0, layers, forward, 0)
    store = pltpu.make_async_copy(cur, result_hbm, w_sem.at[6])
    store.start()
    store.wait()

    cur[...] = gf[own, :].astype(F32)

    def backward(step, carry):
        layer = layers - 1 - step
        for piece in range(CHUNKS):
            grad = norm_backward(layer, piece, cur[part(piece), :], 5, n_two, r_two, (5, 3, 2))
            mid[part(piece), :] = grad
            gf[at_rows(me, piece), :] = grad.astype(BF16)
            ag_send(BWD_FFN, layer, piece, gf)

        ffn_phase(BWD_FFN, layer, gf, ffn_back_rows)
        weight_grad(layer, gf, act.at[layer], hidden, hidden)
        near_send(layer, DOWN)

        @pl.when(step > 0)
        def _():
            near_add(layer + 1, OUT)
            near_add(layer + 1, QKV)

        for piece in range(CHUNKS):
            grad = mid[part(piece), :] + rs_final(BWD_FFN, layer, piece)
            grad = norm_backward(layer, piece, grad, 4, n_one, r_one, (4, 1, 0))
            cur[part(piece), :] = grad
            ga[at_rows(me, piece), :] = grad.astype(BF16)
            ag_send(BWD_ATTN, layer, piece, ga)
        weight_grad(layer, hr.at[layer], slope.at[layer], 0, hidden)
        near_send(layer, UP)
        vout_ref[layer, pl.ds(6, 1), :] = jnp.sum(
            slope[layer].astype(F32), axis=0, keepdims=True
        )
        gk[...] = jnp.zeros_like(gk)
        gv[...] = jnp.zeros_like(gv)

        def heads_grad(turn, inner):
            @pl.when(turn == 1)
            def _():
                for piece in range(CHUNKS):
                    ag_recv("s", BWD_ATTN, layer, piece, ga).wait_recv()

            @pl.when(turn == 2)
            def _():
                for piece in range(CHUNKS):
                    ag_forward(BWD_ATTN, layer, piece, ga)
                    if piece == 0:
                        near_add(layer, DOWN)

            @pl.when(turn == 3)
            def _():
                for piece in range(CHUNKS):
                    ag_recv("f", BWD_ATTN, layer, piece, ga).wait_recv()

            owner = member(1 - turn // 2, 1 - turn % 2)
            rows = span_rows(owner)
            go[rows, :] = dot_nt(ga[rows, :], wout[layer]).astype(BF16)
            by_keys(owner, partial(attend_back, layer, owner))
            return inner

        lax.fori_loop(0, GROUP, heads_grad, 0)

        def rows_back(turn, inner):
            @pl.when(turn == 2)
            def _():
                weight_grad(layer, ga, att.at[layer], 2 * hidden, heads_width)
                near_send(layer, OUT)

            pair, which = turn // 2, turn % 2
            rows = span_rows(member(pair, which))
            joined = jnp.concatenate(
                (gq[rows, :], gk[rows, :].astype(BF16), gv[rows, :].astype(BF16)), axis=1
            )
            gqkv[rows, :] = joined
            out = dot_nn(joined, wqkv[layer])
            for piece in range(CHUNKS):
                place_part(
                    BWD_ATTN, layer, pair, which, piece, out[piece * chunk : (piece + 1) * chunk]
                )
            return inner

        lax.fori_loop(0, GROUP, rows_back, 0)
        ag_done(BWD_ATTN, layer, ga)
        weight_grad(layer, xr.at[layer], gqkv, 2 * hidden + OUT_WIDE, 3 * heads_width)
        near_send(layer, QKV)
        sums = jnp.sum(gqkv[...].astype(F32), axis=0, keepdims=True)
        vout_ref[layer, pl.ds(7, 1), pl.ds(0, heads_width)] = sums[:, :heads_width]
        vout_ref[layer, pl.ds(7, 1), pl.ds(256, heads_width)] = sums[:, 2 * heads_width :]
        if inside:

            @pl.when(step == layers - 1)
            def _():
                vec_send(0, (sib,), "tensor")
                near_add(layer, UP)
                vec_add(vec_copies(0, (sib,), "tensor"), False)
                vec_send(1, (cross,), "tensor")
                near_add(layer, OUT)

            @pl.when(step < layers - 1)
            def _():
                near_add(layer, UP)

        for piece in range(CHUNKS):
            cur[part(piece), :] = cur[part(piece), :] + rs_final(BWD_ATTN, layer, piece)
        if inside:

            @pl.when(step == layers - 1)
            def _():
                vec_add(vec_copies(1, (cross,), "tensor"), False)
                vec_send(2, (across,), "dp")

        return carry

    lax.fori_loop(0, layers, backward, 0)
    store = pltpu.make_async_copy(cur, tgrad_hbm, w_sem.at[7])
    store.start()
    if inside:
        older = [
            (layer, block)
            for layer in range(layers - 1, 0, -1)
            for block in (DOWN, UP, OUT, QKV)
        ]
        near_part(0, QKV, NEAR_ORDER[0])
        vec_add(vec_copies(2, (across,), "dp"), True)
        vec_send(3, distant, "dp")
        for place, hop in enumerate(NEAR_ORDER[1:]):
            for layer, block in older[place :: FAR_SIDE - 1]:
                far_add(layer, block)
            near_part(0, QKV, hop)
        for block in (DOWN, UP, OUT):
            far_add(0, block)
        vec_add(vec_copies(3, distant, "dp"), True)
        far_add(0, QKV)
        for copy in staged[-2:]:
            copy.wait()
    store.wait()


def finish_kernel(hidden, heads_width, result, tgrad, vout, main, *outs):
    layers, each, _ = main.shape
    fine = each // GROUP
    head_each = heads_width // (NEAR * FAR_SIDE)
    place, mine = lax.axis_index("dp"), lax.axis_index("tensor")
    res_o, tg_o, qkv_o, head_o, out_o, up_o, ubias_o, down_o, obias_o, gain_o = outs
    res_o[...] = result[...]
    tg_o[...] = tgrad[...]

    def shifted(value, begin):
        return pltpu.roll(value, value.shape[1] - begin, 1)

    for layer in range(layers):
        up_o[layer] = main[layer, :, :hidden]
        down_o[layer] = main[layer, :, hidden : 2 * hidden]
        out_o[layer] = main[layer, :, 2 * hidden : 2 * hidden + heads_width].T
        begin = 2 * hidden + OUT_WIDE
        for third in range(3):
            qkv_o[layer, third] = main[
                layer, :, begin + third * heads_width : begin + (third + 1) * heads_width
            ]
        whole = vout[layer]
        picked = shifted(whole, place * each + mine * fine)
        obias_o[layer] = picked[0:4, :fine]
        gain_o[layer] = picked[4:6, :fine]
        ubias_o[layer : layer + 1, :] = shifted(whole, place * each)[6:7, :each]
        picked = shifted(whole, place * head_each)
        head_o[layer, 0:1, :] = picked[7:8, :head_each]
        head_o[layer, 1:2, :] = picked[7:8, 256 : 256 + head_each]


def finish(result, tokens_grad, vout, main, hidden, heads_width):
    layers, each, _ = main.shape
    fine = each // GROUP
    head_each = heads_width // (NEAR * FAR_SIDE)
    shapes = (
        result.shape,
        tokens_grad.shape,
        (layers, 3, each, heads_width),
        (layers, 2, head_each),
        (layers, heads_width, each),
        (layers, each, hidden),
        (layers, each),
        (layers, each, hidden),
        (layers, 4, fine),
        (layers, 2, fine),
    )
    outs = pl.pallas_call(
        partial(finish_kernel, hidden, heads_width),
        name="finish",
        out_shape=tuple(jax.ShapeDtypeStruct(shape, F32) for shape in shapes),
        in_specs=[pl.BlockSpec(memory_space=pltpu.VMEM)] * 4,
        out_specs=tuple(pl.BlockSpec(memory_space=pltpu.VMEM) for _ in shapes),
    )(result, tokens_grad, vout, main)
    return (
        *outs[:2],
        outs[2].transpose(0, 2, 1, 3),
        *outs[3:7],
        outs[7].transpose(0, 2, 1),
        *outs[8:],
    )


def body(
    tokens,
    qkv_weight,
    qv_bias,
    out_weight,
    up_weight,
    up_bias,
    down_weight,
    out_bias,
    norm_gain,
    doc_start,
    picture,
    cotangent,
):
    layers, width, _, heads_width = qkv_weight.shape
    shard = tokens.shape[0]
    seq = shard * GROUP
    hidden = up_weight.shape[2]
    spans = seq // SPAN
    pairs = sum(min(span + 1, LONGEST) for span in range(spans))
    heads = heads_width // HEAD_DIM
    total_width = 2 * hidden + OUT_WIDE + QKV_WIDE
    chunk = shard // CHUNKS
    wide = max(hidden, width)
    vmem = partial(pl.BlockSpec, memory_space=pltpu.VMEM)
    smem = partial(pl.BlockSpec, memory_space=pltpu.SMEM)
    anywhere = partial(pl.BlockSpec, memory_space=pl.ANY)
    sems = pltpu.SemaphoreType.DMA((4, layers, CHUNKS))
    shares = lax.axis_size("dp")
    inside = shares == NEAR * FAR_SIDE
    rows_each = width // shares
    outputs = [
        jax.ShapeDtypeStruct((shard, width), F32),
        jax.ShapeDtypeStruct((shard, width), F32),
        jax.ShapeDtypeStruct((layers, 8, wide), F32),
    ]
    dma = pltpu.SemaphoreType.DMA
    first, last = [], []
    if inside:
        outputs.append(jax.ShapeDtypeStruct((layers, rows_each, total_width), F32))
        first = [pltpu.VMEM((layers, width, total_width), BF16)]
        last = [
            pltpu.VMEM((2, rows_each, hidden), F32),
            dma((2,)),
            pltpu.VMEM((4, layers, 8, wide), F32),
            pltpu.VMEM((2 + FAR_SIDE, layers, 8, wide), F32),
            pltpu.VMEM((layers, FAR_SIDE, rows_each, total_width), BF16),
            pltpu.VMEM((layers, FAR_SIDE - 1, rows_each, total_width), BF16),
            dma((layers, 4, FAR_SIDE)),
            dma((layers, 4, FAR_SIDE)),
            dma((layers, 4, FAR_SIDE - 1)),
            dma((layers, 4, FAR_SIDE - 1)),
            dma((2 + FAR_SIDE,)),
            dma((2 + FAR_SIDE,)),
        ]
    else:
        outputs.append(jax.ShapeDtypeStruct((layers, width, total_width), BF16))
    result, tokens_grad, vout, grads = pl.pallas_call(
        partial(step_kernel, inside),
        name="encoder_step",
        out_shape=tuple(outputs),
        in_specs=[anywhere()] * 2 + [vmem()] * 4 + [smem()] * 2 + [anywhere()] * 4,
        out_specs=(anywhere(), anywhere(), vmem(), anywhere() if inside else vmem()),
        scratch_shapes=first
        + [
            pltpu.VMEM((layers, 3 * heads_width, width), BF16),
            pltpu.VMEM(out_weight.shape, BF16),
            pltpu.VMEM(up_weight.shape, BF16),
            pltpu.VMEM(down_weight.shape, BF16),
            pltpu.VMEM((layers, seq, width), BF16),
            pltpu.VMEM((layers, seq, heads_width), BF16),
            pltpu.VMEM((layers, seq, heads_width), BF16),
            pltpu.VMEM((layers, seq, heads_width), BF16),
            pltpu.VMEM((layers, heads, pairs, SPAN, SPAN), BF16),
            pltpu.VMEM((layers, seq, heads_width), BF16),
            pltpu.VMEM((layers, seq, width), BF16),
            pltpu.VMEM((layers, seq, hidden), BF16),
            pltpu.VMEM((layers, seq, hidden), BF16),
            pltpu.VMEM((layers, shard, width), BF16),
            pltpu.VMEM((layers, shard, 1), F32),
            pltpu.VMEM((layers, shard, width), BF16),
            pltpu.VMEM((layers, shard, 1), F32),
            pltpu.VMEM((seq, width), BF16),
            pltpu.VMEM((seq, width), BF16),
            pltpu.VMEM((seq, heads_width), BF16),
            pltpu.VMEM((seq, heads_width), BF16),
            pltpu.VMEM((seq, heads_width), F32),
            pltpu.VMEM((seq, heads_width), F32),
            pltpu.VMEM((seq, 3 * heads_width), BF16),
            pltpu.VMEM((shard, width), F32),
            pltpu.VMEM((shard, width), F32),
        ]
        + [pltpu.VMEM((CHUNKS, chunk, width), BF16)] * 6
        + [pltpu.VMEM((CHUNKS, chunk, width), F32), pltpu.SemaphoreType.DMA((8,))]
        + [sems] * 12
        + last
        + [pltpu.VMEM((layers, 8, wide), F32)],
        compiler_params=pltpu.CompilerParams(
            collective_id=0, has_side_effects=True, vmem_limit_bytes=67043328
        ),
    )(
        tokens,
        cotangent,
        out_bias,
        norm_gain,
        up_bias,
        qv_bias,
        doc_start,
        picture,
        qkv_weight.transpose(0, 2, 3, 1).reshape(layers, 3 * heads_width, width),
        out_weight,
        up_weight,
        down_weight,
    )
    head_each = heads_width // shares
    up_each = hidden // shares
    place = lax.axis_index("dp")
    if inside:
        return finish(result, tokens_grad, vout, grads, hidden, heads_width)
    else:
        main = jnp.stack(
            [
                lax.psum_scatter(grads[layer], "dp", scatter_dimension=0, tiled=True).astype(F32)
                for layer in range(layers)
            ]
        )
        vector_sum = lax.psum(vout[:, :6], ("dp", "tensor"))
        bias_sum = lax.psum(vout[:, 6:], "dp")
    begin = 2 * hidden + OUT_WIDE
    qkv_part = main[:, :, begin : begin + 3 * heads_width].reshape(
        layers, rows_each, 3, heads_width
    )
    out_part = main[:, :, 2 * hidden : 2 * hidden + heads_width].transpose(0, 2, 1)
    up_part = main[:, :, :hidden]
    down_part = main[:, :, hidden : 2 * hidden].transpose(0, 2, 1)
    fine = width // (shares * GROUP)
    vector_sum = lax.dynamic_slice_in_dim(
        vector_sum, place * rows_each + lax.axis_index("tensor") * fine, fine, 2
    )
    head_sum = jnp.stack(
        (bias_sum[:, 1, :heads_width], bias_sum[:, 1, 256 : 256 + heads_width]), axis=1
    )
    return (
        result,
        tokens_grad,
        qkv_part,
        lax.dynamic_slice_in_dim(head_sum, place * head_each, head_each, 2),
        out_part,
        up_part,
        lax.dynamic_slice_in_dim(bias_sum[:, 0, :hidden], place * up_each, up_each, 1),
        down_part,
        vector_sum[:, :4],
        vector_sum[:, 4:],
    )


def solution(mesh):
    return jax.shard_map(
        body,
        mesh=mesh,
        in_specs=(
            P(("dp", "tensor"), None),
            P(None, None, None, "tensor"),
            P(None, None, "tensor"),
            P(None, "tensor", None),
            P(None, None, "tensor"),
            P(None, "tensor"),
            P(None, "tensor", None),
            P(),
            P(),
            P("dp"),
            P("dp"),
            P(("dp", "tensor"), None),
        ),
        out_specs=(
            P(("dp", "tensor"), None),
            P(("dp", "tensor"), None),
            P(None, "dp", None, "tensor"),
            P(None, None, ("tensor", "dp")),
            P(None, "tensor", "dp"),
            P(None, "dp", "tensor"),
            P(None, ("tensor", "dp")),
            P(None, "tensor", "dp"),
            P(None, None, ("dp", "tensor")),
            P(None, None, ("dp", "tensor")),
        ),
        check_vma=False,
    )
```

```python
from functools import partial

import jax
import jax.numpy as jnp
from jax import lax
from jax.experimental import pallas as pl
from jax.experimental.pallas import tpu as pltpu
from jax.sharding import PartitionSpec as P

HEAD_DIM = 64
SPAN = 256
GROUP = 4
LONGEST = 3
CHUNKS = 2
HALVES = 2
EPSILON = 1e-05
BEYOND = 1 << 20
NEAR, FAR_SIDE = 2, 4
NEAR_ORDER = (1, 0, 2, None)
OUT_WIDE, QKV_WIDE = 256, 640
UP, DOWN, OUT, QKV = range(4)
F32 = jnp.float32
BF16 = jnp.bfloat16
MESH = pl.DeviceIdType.MESH
FWD_ATTN, FWD_FFN, BWD_FFN, BWD_ATTN = range(4)


def dot_nn(left, right):
    return lax.dot_general(left, right, (((1,), (0,)), ((), ())), preferred_element_type=F32)


def dot_nt(left, right):
    return lax.dot_general(left, right, (((1,), (1,)), ((), ())), preferred_element_type=F32)


def dot_tn(left, right):
    return lax.dot_general(left, right, (((0,), (0,)), ((), ())), preferred_element_type=F32)


def gelu_parts(value):
    cdf = 0.5 * (1.0 + lax.erf(value * 0.7071067811865476))
    density = jnp.exp(-0.5 * value * value) * 0.3989422804014327
    return value * cdf, cdf + value * density


def step_kernel(inside, *refs):
    (
        tokens_hbm,
        cot_hbm,
        obias_ref,
        gain_ref,
        ubias_ref,
        hbias_ref,
        doc_ref,
        pic_ref,
        wqkv_hbm,
        wout_hbm,
        wup_hbm,
        wdown_hbm,
        result_hbm,
        tgrad_hbm,
        vout_ref,
        *refs,
    ) = refs
    *refs, vin_ref = refs
    if inside:
        final_hbm, *refs = refs
        *refs, stage, f_sem, vsend, vrecv, y_buf, z_buf, y_s, y_r, z_s, z_r, v_s, v_r = refs
    (
        grads_ref,
        wqkv,
        wout,
        wup,
        wdown,
        xr,
        q_all,
        k_all,
        v_all,
        prob,
        att,
        hr,
        act,
        slope,
        n_one,
        r_one,
        n_two,
        r_two,
        gf,
        ga,
        go,
        gq,
        gk,
        gv,
        gqkv,
        cur,
        mid,
        d0s,
        d0r,
        d1s,
        d1r,
        xsd,
        xrv,
        keep,
        w_sem,
        agx_s,
        agx_r,
        ags_s,
        ags_r,
        agf_s,
        agf_r,
        d0_s,
        d0_r,
        d1_s,
        d1_r,
        x_s,
        x_r,
    ) = refs
    layers = obias_ref.shape[0]
    shard, width = tokens_hbm.shape
    chunk = shard // CHUNKS
    part_rows = shard // HALVES
    heads_width = att.shape[2]
    hidden = wup.shape[2]
    me = lax.axis_index("tensor")
    row, col = me // 2, me % 2
    sib = row * 2 + (1 - col)
    cross = (1 - row) * 2 + col
    diag = (1 - row) * 2 + (1 - col)

    own = pl.ds(pl.multiple_of(me * shard, shard), shard)
    loads = []
    for place, (src, dst) in enumerate(
        (
            (tokens_hbm, xr.at[0, own]),
            (wqkv_hbm, wqkv),
            (wout_hbm, wout),
            (wup_hbm, wup),
            (wdown_hbm, wdown),
            (cot_hbm, gf.at[own]),
        )
    ):
        load = pltpu.make_async_copy(src, dst, w_sem.at[place])
        load.start()
        loads.append(load)

    barrier = pltpu.get_barrier_semaphore()
    for peer in (sib, cross):
        pl.semaphore_signal(barrier, inc=1, device_id={"tensor": peer}, device_id_type=MESH)
    if inside:
        share = lax.axis_index("dp")
        far, near = share // NEAR, share % NEAR
        across = far * NEAR + (1 - near)
        distant = [((far + hop) % FAR_SIDE) * NEAR + near for hop in range(1, FAR_SIDE)]
        for peer in (across, *distant):
            pl.semaphore_signal(barrier, inc=1, device_id={"dp": peer}, device_id_type=MESH)
        pl.semaphore_wait(barrier, 3 + len(distant))
    else:
        pl.semaphore_wait(barrier, 2)

    def at_rows(owner, piece):
        return pl.ds(pl.multiple_of(owner * shard + piece * chunk, chunk), chunk)

    def half_rows(owner, half):
        return pl.ds(pl.multiple_of(owner * shard + half * part_rows, part_rows), part_rows)

    def span_rows(owner):
        return pl.ds(pl.multiple_of(owner * shard, shard), shard)

    def part(piece):
        return pl.ds(piece * chunk, chunk)

    def remote(src, dst, send, recv, peer, axis="tensor"):
        return pltpu.make_async_remote_copy(
            src_ref=src,
            dst_ref=dst,
            send_sem=send,
            recv_sem=recv,
            device_id={axis: peer},
            device_id_type=MESH,
        )

    def ag_copy(kind, phase, layer, piece, buf):
        owner, peer, send, recv = {
            "x": (me, cross, agx_s, agx_r),
            "s": (me, sib, ags_s, ags_r),
            "f": (cross, sib, agf_s, agf_r),
        }[kind]
        view = buf.at[at_rows(owner, piece)]
        return remote(view, view, send.at[phase, layer, piece], recv.at[phase, layer, piece], peer)

    def ag_recv(kind, phase, layer, piece, buf):
        owner, peer, send, recv = {
            "x": (cross, cross, agx_s, agx_r),
            "s": (sib, sib, ags_s, ags_r),
            "f": (diag, sib, agf_s, agf_r),
        }[kind]
        view = buf.at[at_rows(owner, piece)]
        return remote(view, view, send.at[phase, layer, piece], recv.at[phase, layer, piece], peer)

    def ag_send(phase, layer, piece, buf):
        ag_copy("x", phase, layer, piece, buf).start()
        ag_copy("s", phase, layer, piece, buf).start()

    def ag_forward(phase, layer, piece, buf):
        ag_recv("x", phase, layer, piece, buf).wait_recv()
        ag_copy("f", phase, layer, piece, buf).start()

    def ag_done(phase, layer, buf):
        for piece in range(CHUNKS):
            for kind in "xsf":
                ag_copy(kind, phase, layer, piece, buf).wait_send()

    def rs_copy(kind, phase, layer, piece):
        src, dst, send, recv, peer = {
            "d0": (d0s, d0r, d0_s, d0_r, sib),
            "d1": (d1s, d1r, d1_s, d1_r, sib),
            "x": (xsd, xrv, x_s, x_r, cross),
        }[kind]
        return remote(
            src.at[piece],
            dst.at[piece],
            send.at[phase, layer, piece],
            recv.at[phase, layer, piece],
            peer,
        )

    def rs_diag(phase, layer, piece, value):
        d0s[piece] = value.astype(BF16)
        rs_copy("d0", phase, layer, piece).start()

    def rs_cross(phase, layer, piece, value):
        rs_copy("d0", phase, layer, piece).wait_recv()
        xsd[piece] = (value + d0r[piece].astype(F32)).astype(BF16)
        rs_copy("x", phase, layer, piece).start()

    def rs_sib(phase, layer, piece, value):
        d1s[piece] = value.astype(BF16)
        rs_copy("d1", phase, layer, piece).start()

    def place_part(phase, layer, pair, which, piece, value):
        @pl.when((pair == 0) & (which == 0))
        def _():
            rs_diag(phase, layer, piece, value)

        @pl.when((pair == 0) & (which == 1))
        def _():
            rs_cross(phase, layer, piece, value)

        @pl.when((pair == 1) & (which == 0))
        def _():
            rs_sib(phase, layer, piece, value)

        @pl.when((pair == 1) & (which == 1))
        def _():
            keep[piece] = value

    def rs_final(phase, layer, piece):
        rs_copy("d1", phase, layer, piece).wait_recv()
        rs_copy("x", phase, layer, piece).wait_recv()
        total = keep[piece] + d1r[piece].astype(F32) + xrv[piece].astype(F32)
        for kind in ("d0", "d1", "x"):
            rs_copy(kind, phase, layer, piece).wait_send()
        return total

    def vec(layer, place):
        return vin_ref[layer, pl.ds(place, 1), :]

    def norm_forward(layer, piece, value, gain, shift, normed, inverse):
        centered = value - jnp.mean(value, axis=-1, keepdims=True)
        scale = lax.rsqrt(jnp.mean(centered * centered, axis=-1, keepdims=True) + EPSILON)
        unit = centered * scale
        normed[layer, part(piece), :] = unit.astype(BF16)
        inverse[layer, part(piece), :] = scale
        return unit * vec(layer, gain) + vec(layer, shift)

    def norm_backward(layer, piece, grad, gain, normed, inverse, rows):
        unit = normed[layer, part(piece), :].astype(F32)
        scale = inverse[layer, part(piece), :]
        scaled = grad * vec(layer, gain)
        out = scale * (
            scaled
            - jnp.mean(scaled, axis=-1, keepdims=True)
            - unit * jnp.mean(scaled * unit, axis=-1, keepdims=True)
        )
        gain_row, shift_row, bias_row = rows
        for place, term in ((gain_row, grad * unit), (shift_row, grad), (bias_row, out)):
            vout_ref[layer, pl.ds(place, 1), :] += jnp.sum(term, axis=0, keepdims=True)
        return out

    def begin_back(layer, piece, grad):
        grad = norm_backward(layer, piece, grad, 5, n_two, r_two, (5, 3, 2))
        mid[part(piece), :] = grad
        gf[at_rows(me, piece), :] = grad.astype(BF16)
        ag_send(BWD_FFN, layer, piece, gf)

    def result_copy(piece):
        return pltpu.make_async_copy(
            keep.at[piece], result_hbm.at[part(piece)], w_sem.at[6 + piece]
        )

    groups = []
    for begin in range(0, heads_width, 128):
        wide = min(128, heads_width - begin)
        groups.append((begin, wide, range(begin // HEAD_DIM, (begin + wide) // HEAD_DIM)))

    def only_head(value, begin, head):
        if value.shape[1] == HEAD_DIM:
            return value
        lane = lax.broadcasted_iota(jnp.int32, value.shape, 1)
        low = head * HEAD_DIM - begin
        return jnp.where((lane >= low) & (lane < low + HEAD_DIM), value, jnp.zeros_like(value))

    def by_keys(span, run):
        for count in range(1, LONGEST + 1):

            @pl.when((span == count - 1) if count < LONGEST else (span >= count - 1))
            def _():
                run(count)

    def keys_of(span, count):
        if count < LONGEST:
            return 0, pl.ds(0, count * SPAN), (count * (count - 1)) // 2
        begin = span - (LONGEST - 1)
        rows = pl.ds(pl.multiple_of(begin * SPAN, SPAN), LONGEST * SPAN)
        return begin * SPAN, rows, LONGEST * (span - 1)

    def attend(layer, span, half, count):
        rows = half_rows(span, half)
        first_key, keys, base = keys_of(span, count)
        query_pos = (
            span * SPAN + half * part_rows + lax.broadcasted_iota(jnp.int32, (part_rows, 1), 0)
        )
        picture = jnp.full((part_rows, 1), pic_ref[span], jnp.int32) == 1
        limit = jnp.where(picture, span * SPAN + SPAN - 1, query_pos)
        key_pos = first_key + lax.broadcasted_iota(jnp.int32, (1, count * SPAN), 1)
        first = jnp.full((1, count * SPAN), doc_ref[span] * SPAN, jnp.int32)
        key_pos = jnp.where(key_pos >= first, key_pos, BEYOND)
        allowed = key_pos <= limit
        for begin, wide, heads in groups:
            cols = pl.ds(begin, wide)
            q_here = q_all[layer, rows, cols]
            k_here = k_all[layer, keys, cols]
            v_here = v_all[layer, keys, cols]
            total = jnp.zeros((part_rows, wide), F32)
            for head in heads:
                scores = dot_nt(only_head(q_here, begin, head), k_here)
                scores = jnp.where(allowed, scores, -1e30)
                raised = jnp.exp(scores - jnp.max(scores, axis=-1, keepdims=True))
                share = raised * (1.0 / jnp.sum(raised, axis=-1, keepdims=True))
                share = share.astype(BF16)
                for block in range(count):
                    prob[layer, head, base + block, pl.ds(half * part_rows, part_rows), :] = share[
                        :, block * SPAN : (block + 1) * SPAN
                    ]
                total = total + dot_nn(share, only_head(v_here, begin, head))
            att[layer, rows, cols] = total.astype(BF16)

    def attend_back(layer, span, count):
        rows = span_rows(span)
        _, keys, base = keys_of(span, count)
        for begin, wide, heads in groups:
            cols = pl.ds(begin, wide)
            q_here = q_all[layer, rows, cols]
            k_here = k_all[layer, keys, cols]
            v_here = v_all[layer, keys, cols]
            go_here = go[rows, cols]
            mixed = go_here.astype(F32) * att[layer, rows, cols].astype(F32)
            total = jnp.zeros((SPAN, wide), F32)
            key_total = gk[keys, cols]
            value_total = gv[keys, cols]
            for head in heads:
                go_head = only_head(go_here, begin, head)
                inner = jnp.sum(only_head(mixed, begin, head), axis=-1, keepdims=True)
                gp = dot_nt(go_head, v_here)
                share = jnp.concatenate(
                    [prob[layer, head, base + block] for block in range(count)], axis=1
                )
                gs = (share.astype(F32) * (gp - inner)).astype(BF16)
                total = total + dot_nn(gs, only_head(k_here, begin, head))
                key_total = key_total + dot_tn(gs, only_head(q_here, begin, head))
                value_total = value_total + dot_tn(share, go_head)
            gk[keys, cols] = key_total
            gv[keys, cols] = value_total
            gq[rows, cols] = (total * 0.125).astype(BF16)

    def member(pair, which):
        line = (1 - pair) * (1 - row) + pair * row
        return line * 2 + (1 - which) * (1 - col) + which * col

    def project(layer, owner):
        rows = span_rows(owner)
        out = dot_nt(xr[layer, rows, :], wqkv[layer])
        query_bias = vin_ref[layer, pl.ds(7, 1), pl.ds(0, heads_width)]
        value_bias = vin_ref[layer, pl.ds(7, 1), pl.ds(256, heads_width)]
        q_all[layer, rows, :] = (
            (out[:, :heads_width] + query_bias) * 0.125
        ).astype(BF16)
        k_all[layer, rows, :] = out[:, heads_width : 2 * heads_width].astype(BF16)
        v_all[layer, rows, :] = (
            out[:, 2 * heads_width :] + value_bias
        ).astype(BF16)

    def two(buf, first, second, piece):
        return jnp.concatenate(
            (buf[at_rows(first, piece), :], buf[at_rows(second, piece), :]), axis=0
        )

    def ffn_rows(layer, first, second, piece):
        pre = dot_nn(two(hr.at[layer], first, second, piece), wup[layer]) + vec(layer, 6)
        value, grad = gelu_parts(pre)
        value, grad = value.astype(BF16), grad.astype(BF16)
        for place, owner in enumerate((first, second)):
            rows = at_rows(owner, piece)
            act[layer, rows, :] = value[place * chunk : (place + 1) * chunk]
            slope[layer, rows, :] = grad[place * chunk : (place + 1) * chunk]
        out = dot_nn(value, wdown[layer])
        return out[:chunk], out[chunk:]

    def ffn_back_rows(layer, first, second, piece):
        gu = dot_nt(two(gf, first, second, piece), wdown[layer])
        gpre = (gu * two(slope.at[layer], first, second, piece).astype(F32)).astype(BF16)
        for place, owner in enumerate((first, second)):
            slope[layer, at_rows(owner, piece), :] = gpre[place * chunk : (place + 1) * chunk]
        out = dot_nt(gpre, wup[layer])
        return out[:chunk], out[chunk:]

    def ffn_phase(phase, layer, buf, rows_of):
        for piece in range(CHUNKS):
            ag_recv("s", phase, layer, piece, buf).wait_recv()
            own_part, sib_part = rows_of(layer, me, sib, piece)
            rs_sib(phase, layer, piece, sib_part)
            keep[piece] = own_part
        for piece in range(CHUNKS):
            ag_forward(phase, layer, piece, buf)
            ag_recv("f", phase, layer, piece, buf).wait_recv()
            cross_part, diag_part = rows_of(layer, cross, diag, piece)
            rs_diag(phase, layer, piece, diag_part)
            rs_cross(phase, layer, piece, cross_part)
        ag_done(phase, layer, buf)

    def weight_grad(layer, left, right, begin, wide):
        def block(place, carry):
            cols = pl.ds(pl.multiple_of(place * 256, 256), 256)
            grads_ref[layer, cols, pl.ds(begin, wide)] = dot_tn(left[:, cols], right[...]).astype(
                BF16
            )
            return carry

        lax.fori_loop(0, width // 256, block, 0)

    each = width // (NEAR * FAR_SIDE)
    blocks = (
        (0, hidden),
        (hidden, hidden),
        (2 * hidden, OUT_WIDE),
        (2 * hidden + OUT_WIDE, QKV_WIDE),
    )

    def slice_rows(owner):
        return pl.ds(pl.multiple_of(owner * each, each), each)

    def near_copy(layer, block, place):
        begin, wide = blocks[block]
        return remote(
            grads_ref.at[layer, slice_rows(place * NEAR + 1 - near), pl.ds(begin, wide)],
            y_buf.at[layer, place, :, pl.ds(begin, wide)],
            y_s.at[layer, block, place],
            y_r.at[layer, block, place],
            across,
            "dp",
        )

    def far_copy(layer, block, hop):
        begin, wide = blocks[block]
        return remote(
            grads_ref.at[layer, slice_rows(distant[hop]), pl.ds(begin, wide)],
            z_buf.at[layer, hop, :, pl.ds(begin, wide)],
            z_s.at[layer, block, hop],
            z_r.at[layer, block, hop],
            distant[hop],
            "dp",
        )

    def near_send(layer, block):
        if inside:
            for hop in NEAR_ORDER:
                near_copy(layer, block, far if hop is None else distant[hop] // NEAR).start()

    def near_part(layer, block, hop):
        begin, wide = blocks[block]
        cols = pl.ds(begin, wide)
        place = far if hop is None else distant[hop] // NEAR
        near_copy(layer, block, place).wait_recv()
        rows = slice_rows(place * NEAR + near)
        grads_ref[layer, rows, cols] = (
            grads_ref[layer, rows, cols].astype(F32) + y_buf[layer, place, :, cols].astype(F32)
        ).astype(BF16)
        if hop is not None:
            far_copy(layer, block, hop).start()

    def near_add(layer, block):
        if inside:
            for hop in NEAR_ORDER:
                near_part(layer, block, hop)

    staged = []

    def far_add(layer, block):
        begin, wide = blocks[block]
        cols = pl.ds(begin, wide)
        total = grads_ref[layer, slice_rows(share), cols].astype(F32)
        for hop in range(FAR_SIDE - 1):
            far_copy(layer, block, hop).wait_recv()
            total = total + z_buf[layer, hop, :, cols].astype(F32)
        slot = len(staged) % 2
        if len(staged) > 1:
            staged[-2].wait()
        stage[slot, :, pl.ds(0, wide)] = total
        staged.append(
            pltpu.make_async_copy(
                stage.at[slot, :, pl.ds(0, wide)], final_hbm.at[layer, :, cols], f_sem.at[slot]
            )
        )
        staged[-1].start()
        for place in range(FAR_SIDE):
            near_copy(layer, block, place).wait_send()
        for hop in range(FAR_SIDE - 1):
            far_copy(layer, block, hop).wait_send()

    def vec_copies(place, peers, axis):
        copies = []
        for order, peer in enumerate(peers):
            slot = place + order
            copies.append(
                remote(vsend.at[place], vrecv.at[slot], v_s.at[slot], v_r.at[slot], peer, axis)
            )
        return copies, place

    def vec_send(place, peers, axis):
        vsend[place] = vout_ref[...].astype(BF16)
        for copy in vec_copies(place, peers, axis)[0]:
            copy.start()

    def vec_add(pending, whole):
        copies, place = pending
        for order, copy in enumerate(copies):
            copy.wait_recv()
            term = vrecv[place + order].astype(F32)
            if not whole:
                line = lax.broadcasted_iota(jnp.int32, term.shape, 1)
                term = jnp.where(line < 6, term, 0.0)
            vout_ref[...] += term
        for copy in copies:
            copy.wait_send()

    for layer in range(layers):
        vin_ref[layer, 0:4, :] = obias_ref[layer].astype(F32)
        vin_ref[layer, 4:6, :] = gain_ref[layer].astype(F32)
        vin_ref[layer, 6:7, :] = ubias_ref[layer : layer + 1, :].astype(F32)
        for place in range(2):
            vin_ref[layer, 7:8, place * 256 : place * 256 + heads_width] = hbias_ref[
                layer, place : place + 1, :
            ].astype(F32)
    vout_ref[...] = jnp.zeros_like(vout_ref)
    for begin, wide, room in (
        (2 * hidden, heads_width, OUT_WIDE),
        (2 * hidden + OUT_WIDE, 3 * heads_width, QKV_WIDE),
    ):
        blank = (layers, width, room - wide)
        grads_ref[:, :, begin + wide : begin + room] = jnp.zeros(blank, BF16)
    loads[0].wait()
    for piece in range(CHUNKS):
        ag_send(FWD_ATTN, 0, piece, xr.at[0])
    cur[...] = xr[0, own, :].astype(F32)

    def forward(layer, carry):
        here = xr.at[layer]

        @pl.when(layer == 0)
        def _():
            loads[1].wait()

        project(layer, me)
        for piece in range(CHUNKS):
            ag_recv("s", FWD_ATTN, layer, piece, here).wait_recv()
        project(layer, sib)

        @pl.when(layer == 0)
        def _():
            for load in loads[2:]:
                load.wait()

        for piece in range(CHUNKS):
            ag_forward(FWD_ATTN, layer, piece, here)
        project(layer, cross)
        for piece in range(CHUNKS):
            ag_recv("f", FWD_ATTN, layer, piece, here).wait_recv()
        project(layer, diag)

        def heads_out(turn, inner):
            pair, half, which = turn // (2 * HALVES), (turn % (2 * HALVES)) // 2, turn % 2
            owner = member(pair, which)
            by_keys(owner, partial(attend, layer, owner, half))
            out = dot_nn(att[layer, half_rows(owner, half), :], wout[layer])
            for piece in range(CHUNKS // HALVES):
                place_part(
                    FWD_ATTN,
                    layer,
                    pair,
                    which,
                    half * (CHUNKS // HALVES) + piece,
                    out[piece * chunk : (piece + 1) * chunk],
                )
            return inner

        lax.fori_loop(0, 4 * HALVES, heads_out, 0)
        ag_done(FWD_ATTN, layer, here)
        there = hr.at[layer]
        for piece in range(CHUNKS):
            value = cur[part(piece), :] + rs_final(FWD_ATTN, layer, piece) + vec(layer, 0)
            value = norm_forward(layer, piece, value, 4, 1, n_one, r_one)
            mid[part(piece), :] = value
            hr[layer, at_rows(me, piece), :] = value.astype(BF16)
            ag_send(FWD_FFN, layer, piece, there)
        ffn_phase(FWD_FFN, layer, there, ffn_rows)
        for piece in range(CHUNKS):
            value = mid[part(piece), :] + rs_final(FWD_FFN, layer, piece) + vec(layer, 2)
            value = norm_forward(layer, piece, value, 5, 3, n_two, r_two)
            cur[part(piece), :] = value

            @pl.when(layer + 1 == layers)
            def _():
                keep[piece] = value
                result_copy(piece).start()
                begin_back(layer, piece, gf[at_rows(me, piece), :].astype(F32))

            @pl.when(layer + 1 < layers)
            def _():
                xr[layer + 1, at_rows(me, piece), :] = value.astype(BF16)
                ag_send(FWD_ATTN, layer + 1, piece, xr.at[layer + 1])

        return carry

    lax.fori_loop(0, layers, forward, 0)


    def backward(step, carry):
        layer = layers - 1 - step

        @pl.when(step == 0)
        def _():
            for piece in range(CHUNKS):
                result_copy(piece).wait()


        ffn_phase(BWD_FFN, layer, gf, ffn_back_rows)
        weight_grad(layer, gf, act.at[layer], hidden, hidden)
        near_send(layer, DOWN)

        @pl.when(step > 0)
        def _():
            near_add(layer + 1, QKV)

        for piece in range(CHUNKS):
            grad = mid[part(piece), :] + rs_final(BWD_FFN, layer, piece)
            grad = norm_backward(layer, piece, grad, 4, n_one, r_one, (4, 1, 0))
            cur[part(piece), :] = grad
            ga[at_rows(me, piece), :] = grad.astype(BF16)
            ag_send(BWD_ATTN, layer, piece, ga)
        weight_grad(layer, hr.at[layer], slope.at[layer], 0, hidden)
        near_send(layer, UP)
        vout_ref[layer, pl.ds(6, 1), :] = jnp.sum(
            slope[layer].astype(F32), axis=0, keepdims=True
        )
        gk[...] = jnp.zeros_like(gk)
        gv[...] = jnp.zeros_like(gv)

        def heads_grad(turn, inner):
            @pl.when(turn == 1)
            def _():
                for piece in range(CHUNKS):
                    ag_recv("s", BWD_ATTN, layer, piece, ga).wait_recv()

            @pl.when(turn == 2)
            def _():
                for piece in range(CHUNKS):
                    ag_forward(BWD_ATTN, layer, piece, ga)
                    if piece == 0:
                        near_add(layer, DOWN)

            @pl.when(turn == 3)
            def _():
                for piece in range(CHUNKS):
                    ag_recv("f", BWD_ATTN, layer, piece, ga).wait_recv()

            owner = member(1 - turn // 2, 1 - turn % 2)
            rows = span_rows(owner)
            go[rows, :] = dot_nt(ga[rows, :], wout[layer]).astype(BF16)
            by_keys(owner, partial(attend_back, layer, owner))
            return inner

        lax.fori_loop(0, GROUP, heads_grad, 0)

        def rows_back(turn, inner):
            @pl.when(turn == 2)
            def _():
                weight_grad(layer, ga, att.at[layer], 2 * hidden, heads_width)
                near_send(layer, OUT)

            pair, which = turn // 2, turn % 2
            rows = span_rows(member(pair, which))
            joined = jnp.concatenate(
                (gq[rows, :], gk[rows, :].astype(BF16), gv[rows, :].astype(BF16)), axis=1
            )
            gqkv[rows, :] = joined
            out = dot_nn(joined, wqkv[layer])
            for piece in range(CHUNKS):
                place_part(
                    BWD_ATTN, layer, pair, which, piece, out[piece * chunk : (piece + 1) * chunk]
                )
            return inner

        lax.fori_loop(0, GROUP, rows_back, 0)
        ag_done(BWD_ATTN, layer, ga)
        weight_grad(layer, xr.at[layer], gqkv, 2 * hidden + OUT_WIDE, 3 * heads_width)
        near_send(layer, QKV)
        sums = jnp.sum(gqkv[...].astype(F32), axis=0, keepdims=True)
        vout_ref[layer, pl.ds(7, 1), pl.ds(0, heads_width)] = sums[:, :heads_width]
        vout_ref[layer, pl.ds(7, 1), pl.ds(256, heads_width)] = sums[:, 2 * heads_width :]
        if inside:

            @pl.when(step == layers - 1)
            def _():
                vec_send(0, (sib,), "tensor")
                near_add(layer, UP)
                vec_add(vec_copies(0, (sib,), "tensor"), False)
                vec_send(1, (cross,), "tensor")
                near_add(layer, OUT)

            @pl.when(step < layers - 1)
            def _():
                near_add(layer, UP)
                near_add(layer, OUT)

        for piece in range(CHUNKS):
            grad = cur[part(piece), :] + rs_final(BWD_ATTN, layer, piece)
            cur[part(piece), :] = grad

            @pl.when(step < layers - 1)
            def _():
                begin_back(layer - 1, piece, grad)

        if inside:

            @pl.when(step == layers - 1)
            def _():
                vec_add(vec_copies(1, (cross,), "tensor"), False)
                vec_send(2, (across,), "dp")

        return carry

    lax.fori_loop(0, layers, backward, 0)
    store = pltpu.make_async_copy(cur, tgrad_hbm, w_sem.at[8])
    store.start()
    if inside:
        older = [
            (layer, block)
            for layer in range(layers - 1, 0, -1)
            for block in (DOWN, UP, OUT, QKV)
        ]
        near_part(0, QKV, NEAR_ORDER[0])
        vec_add(vec_copies(2, (across,), "dp"), True)
        vec_send(3, distant, "dp")
        for place, hop in enumerate(NEAR_ORDER[1:]):
            for layer, block in older[place :: FAR_SIDE - 1]:
                far_add(layer, block)
            near_part(0, QKV, hop)
        for block in (DOWN, UP, OUT):
            far_add(0, block)
        vec_add(vec_copies(3, distant, "dp"), True)
        far_add(0, QKV)
        for copy in staged[-2:]:
            copy.wait()
    store.wait()


def finish_kernel(hidden, heads_width, result, tgrad, vout, main, *outs):
    layers, each, _ = main.shape
    fine = each // GROUP
    head_each = heads_width // (NEAR * FAR_SIDE)
    place, mine = lax.axis_index("dp"), lax.axis_index("tensor")
    res_o, tg_o, qkv_o, head_o, out_o, up_o, ubias_o, down_o, obias_o, gain_o = outs
    res_o[...] = result[...]
    tg_o[...] = tgrad[...]

    def shifted(value, begin):
        return pltpu.roll(value, value.shape[1] - begin, 1)

    for layer in range(layers):
        up_o[layer] = main[layer, :, :hidden]
        down_o[layer] = main[layer, :, hidden : 2 * hidden]
        out_o[layer] = main[layer, :, 2 * hidden : 2 * hidden + heads_width].T
        begin = 2 * hidden + OUT_WIDE
        for third in range(3):
            qkv_o[layer, third] = main[
                layer, :, begin + third * heads_width : begin + (third + 1) * heads_width
            ]
        whole = vout[layer]
        picked = shifted(whole, place * each + mine * fine)
        obias_o[layer] = picked[0:4, :fine]
        gain_o[layer] = picked[4:6, :fine]
        ubias_o[layer : layer + 1, :] = shifted(whole, place * each)[6:7, :each]
        picked = shifted(whole, place * head_each)
        head_o[layer, 0:1, :] = picked[7:8, :head_each]
        head_o[layer, 1:2, :] = picked[7:8, 256 : 256 + head_each]


def finish(result, tokens_grad, vout, main, hidden, heads_width):
    layers, each, _ = main.shape
    fine = each // GROUP
    head_each = heads_width // (NEAR * FAR_SIDE)
    shapes = (
        result.shape,
        tokens_grad.shape,
        (layers, 3, each, heads_width),
        (layers, 2, head_each),
        (layers, heads_width, each),
        (layers, each, hidden),
        (layers, each),
        (layers, each, hidden),
        (layers, 4, fine),
        (layers, 2, fine),
    )
    outs = pl.pallas_call(
        partial(finish_kernel, hidden, heads_width),
        name="finish",
        out_shape=tuple(jax.ShapeDtypeStruct(shape, F32) for shape in shapes),
        in_specs=[pl.BlockSpec(memory_space=pltpu.VMEM)] * 4,
        out_specs=tuple(pl.BlockSpec(memory_space=pltpu.VMEM) for _ in shapes),
    )(result, tokens_grad, vout, main)
    return (
        *outs[:2],
        outs[2].transpose(0, 2, 1, 3),
        *outs[3:7],
        outs[7].transpose(0, 2, 1),
        *outs[8:],
    )


def body(
    tokens,
    qkv_weight,
    qv_bias,
    out_weight,
    up_weight,
    up_bias,
    down_weight,
    out_bias,
    norm_gain,
    doc_start,
    picture,
    cotangent,
):
    layers, width, _, heads_width = qkv_weight.shape
    shard = tokens.shape[0]
    seq = shard * GROUP
    hidden = up_weight.shape[2]
    spans = seq // SPAN
    pairs = sum(min(span + 1, LONGEST) for span in range(spans))
    heads = heads_width // HEAD_DIM
    total_width = 2 * hidden + OUT_WIDE + QKV_WIDE
    chunk = shard // CHUNKS
    wide = max(hidden, width)
    vmem = partial(pl.BlockSpec, memory_space=pltpu.VMEM)
    smem = partial(pl.BlockSpec, memory_space=pltpu.SMEM)
    anywhere = partial(pl.BlockSpec, memory_space=pl.ANY)
    sems = pltpu.SemaphoreType.DMA((4, layers, CHUNKS))
    shares = lax.axis_size("dp")
    inside = shares == NEAR * FAR_SIDE
    rows_each = width // shares
    outputs = [
        jax.ShapeDtypeStruct((shard, width), F32),
        jax.ShapeDtypeStruct((shard, width), F32),
        jax.ShapeDtypeStruct((layers, 8, wide), F32),
    ]
    dma = pltpu.SemaphoreType.DMA
    first, last = [], []
    if inside:
        outputs.append(jax.ShapeDtypeStruct((layers, rows_each, total_width), F32))
        first = [pltpu.VMEM((layers, width, total_width), BF16)]
        last = [
            pltpu.VMEM((2, rows_each, hidden), F32),
            dma((2,)),
            pltpu.VMEM((4, layers, 8, wide), BF16),
            pltpu.VMEM((2 + FAR_SIDE, layers, 8, wide), BF16),
            pltpu.VMEM((layers, FAR_SIDE, rows_each, total_width), BF16),
            pltpu.VMEM((layers, FAR_SIDE - 1, rows_each, total_width), BF16),
            dma((layers, 4, FAR_SIDE)),
            dma((layers, 4, FAR_SIDE)),
            dma((layers, 4, FAR_SIDE - 1)),
            dma((layers, 4, FAR_SIDE - 1)),
            dma((2 + FAR_SIDE,)),
            dma((2 + FAR_SIDE,)),
        ]
    else:
        outputs.append(jax.ShapeDtypeStruct((layers, width, total_width), BF16))
    result, tokens_grad, vout, grads = pl.pallas_call(
        partial(step_kernel, inside),
        name="encoder_step",
        out_shape=tuple(outputs),
        in_specs=[anywhere()] * 2 + [vmem()] * 4 + [smem()] * 2 + [anywhere()] * 4,
        out_specs=(anywhere(), anywhere(), vmem(), anywhere() if inside else vmem()),
        scratch_shapes=first
        + [
            pltpu.VMEM((layers, 3 * heads_width, width), BF16),
            pltpu.VMEM(out_weight.shape, BF16),
            pltpu.VMEM(up_weight.shape, BF16),
            pltpu.VMEM(down_weight.shape, BF16),
            pltpu.VMEM((layers, seq, width), BF16),
            pltpu.VMEM((layers, seq, heads_width), BF16),
            pltpu.VMEM((layers, seq, heads_width), BF16),
            pltpu.VMEM((layers, seq, heads_width), BF16),
            pltpu.VMEM((layers, heads, pairs, SPAN, SPAN), BF16),
            pltpu.VMEM((layers, seq, heads_width), BF16),
            pltpu.VMEM((layers, seq, width), BF16),
            pltpu.VMEM((layers, seq, hidden), BF16),
            pltpu.VMEM((layers, seq, hidden), BF16),
            pltpu.VMEM((layers, shard, width), BF16),
            pltpu.VMEM((layers, shard, 1), F32),
            pltpu.VMEM((layers, shard, width), BF16),
            pltpu.VMEM((layers, shard, 1), F32),
            pltpu.VMEM((seq, width), BF16),
            pltpu.VMEM((seq, width), BF16),
            pltpu.VMEM((seq, heads_width), BF16),
            pltpu.VMEM((seq, heads_width), BF16),
            pltpu.VMEM((seq, heads_width), F32),
            pltpu.VMEM((seq, heads_width), F32),
            pltpu.VMEM((seq, 3 * heads_width), BF16),
            pltpu.VMEM((shard, width), F32),
            pltpu.VMEM((shard, width), F32),
        ]
        + [pltpu.VMEM((CHUNKS, chunk, width), BF16)] * 6
        + [pltpu.VMEM((CHUNKS, chunk, width), F32), pltpu.SemaphoreType.DMA((9,))]
        + [sems] * 12
        + last
        + [pltpu.VMEM((layers, 8, wide), F32)],
        compiler_params=pltpu.CompilerParams(
            collective_id=0, has_side_effects=True, vmem_limit_bytes=67043328
        ),
    )(
        tokens,
        cotangent,
        out_bias,
        norm_gain,
        up_bias,
        qv_bias,
        doc_start,
        picture,
        qkv_weight.transpose(0, 2, 3, 1).reshape(layers, 3 * heads_width, width),
        out_weight,
        up_weight,
        down_weight,
    )
    head_each = heads_width // shares
    up_each = hidden // shares
    place = lax.axis_index("dp")
    if inside:
        return finish(result, tokens_grad, vout, grads, hidden, heads_width)
    else:
        main = jnp.stack(
            [
                lax.psum_scatter(grads[layer], "dp", scatter_dimension=0, tiled=True).astype(F32)
                for layer in range(layers)
            ]
        )
        vector_sum = lax.psum(vout[:, :6], ("dp", "tensor"))
        bias_sum = lax.psum(vout[:, 6:], "dp")
    begin = 2 * hidden + OUT_WIDE
    qkv_part = main[:, :, begin : begin + 3 * heads_width].reshape(
        layers, rows_each, 3, heads_width
    )
    out_part = main[:, :, 2 * hidden : 2 * hidden + heads_width].transpose(0, 2, 1)
    up_part = main[:, :, :hidden]
    down_part = main[:, :, hidden : 2 * hidden].transpose(0, 2, 1)
    fine = width // (shares * GROUP)
    vector_sum = lax.dynamic_slice_in_dim(
        vector_sum, place * rows_each + lax.axis_index("tensor") * fine, fine, 2
    )
    head_sum = jnp.stack(
        (bias_sum[:, 1, :heads_width], bias_sum[:, 1, 256 : 256 + heads_width]), axis=1
    )
    return (
        result,
        tokens_grad,
        qkv_part,
        lax.dynamic_slice_in_dim(head_sum, place * head_each, head_each, 2),
        out_part,
        up_part,
        lax.dynamic_slice_in_dim(bias_sum[:, 0, :hidden], place * up_each, up_each, 1),
        down_part,
        vector_sum[:, :4],
        vector_sum[:, 4:],
    )


def solution(mesh):
    return jax.shard_map(
        body,
        mesh=mesh,
        in_specs=(
            P(("dp", "tensor"), None),
            P(None, None, None, "tensor"),
            P(None, None, "tensor"),
            P(None, "tensor", None),
            P(None, None, "tensor"),
            P(None, "tensor"),
            P(None, "tensor", None),
            P(),
            P(),
            P("dp"),
            P("dp"),
            P(("dp", "tensor"), None),
        ),
        out_specs=(
            P(("dp", "tensor"), None),
            P(("dp", "tensor"), None),
            P(None, "dp", None, "tensor"),
            P(None, None, ("tensor", "dp")),
            P(None, "tensor", "dp"),
            P(None, "dp", "tensor"),
            P(None, ("tensor", "dp")),
            P(None, "tensor", "dp"),
            P(None, None, ("dp", "tensor")),
            P(None, None, ("dp", "tensor")),
        ),
        check_vma=False,
    )
```

```python
from functools import partial

import jax
import jax.numpy as jnp
from jax import lax
from jax.experimental import pallas as pl
from jax.experimental.pallas import tpu as pltpu
from jax.sharding import PartitionSpec as P

HEAD_DIM = 64
SPAN = 256
GROUP = 4
LONGEST = 3
CHUNKS = 2
HALVES = 2
EPSILON = 1e-05
BEYOND = 1 << 20
NEAR, FAR_SIDE = 2, 4
NEAR_ORDER = (1, 0, 2, None)
OUT_WIDE, QKV_WIDE = 256, 640
UP, DOWN, OUT, QKV = range(4)
F32 = jnp.float32
BF16 = jnp.bfloat16
MESH = pl.DeviceIdType.MESH
FWD_ATTN, FWD_FFN, BWD_FFN, BWD_ATTN = range(4)


def dot_nn(left, right):
    return lax.dot_general(left, right, (((1,), (0,)), ((), ())), preferred_element_type=F32)


def dot_nt(left, right):
    return lax.dot_general(left, right, (((1,), (1,)), ((), ())), preferred_element_type=F32)


def dot_tn(left, right):
    return lax.dot_general(left, right, (((0,), (0,)), ((), ())), preferred_element_type=F32)


def gelu_parts(value):
    cdf = 0.5 * (1.0 + lax.erf(value * 0.7071067811865476))
    density = jnp.exp(-0.5 * value * value) * 0.3989422804014327
    return value * cdf, cdf + value * density


def step_kernel(inside, *refs):
    (
        tokens_hbm,
        cot_hbm,
        obias_ref,
        gain_ref,
        ubias_ref,
        hbias_ref,
        doc_ref,
        pic_ref,
        wqkv_hbm,
        wout_hbm,
        wup_hbm,
        wdown_hbm,
        result_hbm,
        tgrad_hbm,
        vout_ref,
        *refs,
    ) = refs
    *refs, vin_ref = refs
    if inside:
        final_hbm, *refs = refs
        *refs, stage, f_sem, vsend, vrecv, y_buf, z_buf, y_s, y_r, z_s, z_r, v_s, v_r = refs
    (
        grads_ref,
        wqkv,
        wout,
        wup,
        wdown,
        xr,
        q_all,
        k_all,
        v_all,
        prob,
        att,
        hr,
        act,
        slope,
        n_one,
        r_one,
        n_two,
        r_two,
        gf,
        ga,
        go,
        gq,
        gk,
        gv,
        gqkv,
        cur,
        mid,
        d0s,
        d0r,
        d1s,
        d1r,
        xsd,
        xrv,
        keep,
        w_sem,
        agx_s,
        agx_r,
        ags_s,
        ags_r,
        agf_s,
        agf_r,
        d0_s,
        d0_r,
        d1_s,
        d1_r,
        x_s,
        x_r,
    ) = refs
    layers = obias_ref.shape[0]
    shard, width = tokens_hbm.shape
    chunk = shard // CHUNKS
    part_rows = shard // HALVES
    heads_width = att.shape[2]
    hidden = wup.shape[2]
    me = lax.axis_index("tensor")
    row, col = me // 2, me % 2
    sib = row * 2 + (1 - col)
    cross = (1 - row) * 2 + col
    diag = (1 - row) * 2 + (1 - col)

    own = pl.ds(pl.multiple_of(me * shard, shard), shard)
    loads = []
    for place, (src, dst) in enumerate(
        (
            (tokens_hbm, xr.at[0, own]),
            (wqkv_hbm, wqkv),
            (wout_hbm, wout),
            (wup_hbm, wup),
            (wdown_hbm, wdown),
            (cot_hbm, gf.at[own]),
        )
    ):
        load = pltpu.make_async_copy(src, dst, w_sem.at[place])
        load.start()
        loads.append(load)

    barrier = pltpu.get_barrier_semaphore()
    for peer in (sib, cross):
        pl.semaphore_signal(barrier, inc=1, device_id={"tensor": peer}, device_id_type=MESH)
    if inside:
        share = lax.axis_index("dp")
        far, near = share // NEAR, share % NEAR
        across = far * NEAR + (1 - near)
        distant = [((far + hop) % FAR_SIDE) * NEAR + near for hop in range(1, FAR_SIDE)]
        for peer in (across, *distant):
            pl.semaphore_signal(barrier, inc=1, device_id={"dp": peer}, device_id_type=MESH)
        pl.semaphore_wait(barrier, 3 + len(distant))
    else:
        pl.semaphore_wait(barrier, 2)

    def at_rows(owner, piece):
        return pl.ds(pl.multiple_of(owner * shard + piece * chunk, chunk), chunk)

    def half_rows(owner, half):
        return pl.ds(pl.multiple_of(owner * shard + half * part_rows, part_rows), part_rows)

    def span_rows(owner):
        return pl.ds(pl.multiple_of(owner * shard, shard), shard)

    def part(piece):
        return pl.ds(piece * chunk, chunk)

    def remote(src, dst, send, recv, peer, axis="tensor"):
        return pltpu.make_async_remote_copy(
            src_ref=src,
            dst_ref=dst,
            send_sem=send,
            recv_sem=recv,
            device_id={axis: peer},
            device_id_type=MESH,
        )

    def ag_copy(kind, phase, layer, piece, buf):
        owner, peer, send, recv = {
            "x": (me, cross, agx_s, agx_r),
            "s": (me, sib, ags_s, ags_r),
            "f": (cross, sib, agf_s, agf_r),
        }[kind]
        view = buf.at[at_rows(owner, piece)]
        return remote(view, view, send.at[phase, layer, piece], recv.at[phase, layer, piece], peer)

    def ag_recv(kind, phase, layer, piece, buf):
        owner, peer, send, recv = {
            "x": (cross, cross, agx_s, agx_r),
            "s": (sib, sib, ags_s, ags_r),
            "f": (diag, sib, agf_s, agf_r),
        }[kind]
        view = buf.at[at_rows(owner, piece)]
        return remote(view, view, send.at[phase, layer, piece], recv.at[phase, layer, piece], peer)

    def ag_send(phase, layer, piece, buf):
        ag_copy("x", phase, layer, piece, buf).start()
        ag_copy("s", phase, layer, piece, buf).start()

    def ag_forward(phase, layer, piece, buf):
        ag_recv("x", phase, layer, piece, buf).wait_recv()
        ag_copy("f", phase, layer, piece, buf).start()

    def ag_done(phase, layer, buf):
        for piece in range(CHUNKS):
            for kind in "xsf":
                ag_copy(kind, phase, layer, piece, buf).wait_send()

    def rs_copy(kind, phase, layer, piece):
        src, dst, send, recv, peer = {
            "d0": (d0s, d0r, d0_s, d0_r, sib),
            "d1": (d1s, d1r, d1_s, d1_r, sib),
            "x": (xsd, xrv, x_s, x_r, cross),
        }[kind]
        return remote(
            src.at[piece],
            dst.at[piece],
            send.at[phase, layer, piece],
            recv.at[phase, layer, piece],
            peer,
        )

    def rs_diag(phase, layer, piece, value):
        d0s[piece] = value.astype(BF16)
        rs_copy("d0", phase, layer, piece).start()

    def rs_cross(phase, layer, piece, value):
        rs_copy("d0", phase, layer, piece).wait_recv()
        xsd[piece] = (value + d0r[piece].astype(F32)).astype(BF16)
        rs_copy("x", phase, layer, piece).start()

    def rs_sib(phase, layer, piece, value):
        d1s[piece] = value.astype(BF16)
        rs_copy("d1", phase, layer, piece).start()

    def place_part(phase, layer, pair, which, piece, value):
        @pl.when((pair == 0) & (which == 0))
        def _():
            rs_diag(phase, layer, piece, value)

        @pl.when((pair == 0) & (which == 1))
        def _():
            rs_cross(phase, layer, piece, value)

        @pl.when((pair == 1) & (which == 0))
        def _():
            rs_sib(phase, layer, piece, value)

        @pl.when((pair == 1) & (which == 1))
        def _():
            keep[piece] = value

    def rs_final(phase, layer, piece):
        rs_copy("d1", phase, layer, piece).wait_recv()
        rs_copy("x", phase, layer, piece).wait_recv()
        total = keep[piece] + d1r[piece].astype(F32) + xrv[piece].astype(F32)
        for kind in ("d0", "d1", "x"):
            rs_copy(kind, phase, layer, piece).wait_send()
        return total

    def vec(layer, place):
        return vin_ref[layer, pl.ds(place, 1), :]

    def norm_forward(layer, piece, value, gain, shift, normed, inverse):
        centered = value - jnp.mean(value, axis=-1, keepdims=True)
        scale = lax.rsqrt(jnp.mean(centered * centered, axis=-1, keepdims=True) + EPSILON)
        unit = centered * scale
        normed[layer, part(piece), :] = unit.astype(BF16)
        inverse[layer, part(piece), :] = scale
        return unit * vec(layer, gain) + vec(layer, shift)

    def norm_backward(layer, piece, grad, gain, normed, inverse, rows):
        unit = normed[layer, part(piece), :].astype(F32)
        scale = inverse[layer, part(piece), :]
        scaled = grad * vec(layer, gain)
        out = scale * (
            scaled
            - jnp.mean(scaled, axis=-1, keepdims=True)
            - unit * jnp.mean(scaled * unit, axis=-1, keepdims=True)
        )
        gain_row, shift_row, bias_row = rows
        for place, term in ((gain_row, grad * unit), (shift_row, grad), (bias_row, out)):
            vout_ref[layer, pl.ds(place, 1), :] += jnp.sum(term, axis=0, keepdims=True)
        return out

    def begin_back(layer, piece, grad):
        grad = norm_backward(layer, piece, grad, 5, n_two, r_two, (5, 3, 2))
        mid[part(piece), :] = grad
        gf[at_rows(me, piece), :] = grad.astype(BF16)
        ag_send(BWD_FFN, layer, piece, gf)

    def result_copy(piece):
        return pltpu.make_async_copy(
            keep.at[piece], result_hbm.at[part(piece)], w_sem.at[6 + piece]
        )

    groups = []
    for begin in range(0, heads_width, 128):
        wide = min(128, heads_width - begin)
        groups.append((begin, wide, range(begin // HEAD_DIM, (begin + wide) // HEAD_DIM)))

    def only_head(value, begin, head):
        if value.shape[1] == HEAD_DIM:
            return value
        lane = lax.broadcasted_iota(jnp.int32, value.shape, 1)
        low = head * HEAD_DIM - begin
        return jnp.where((lane >= low) & (lane < low + HEAD_DIM), value, jnp.zeros_like(value))

    def by_keys(span, run):
        for count in range(1, LONGEST + 1):

            @pl.when((span == count - 1) if count < LONGEST else (span >= count - 1))
            def _():
                run(count)

    def keys_of(span, count):
        if count < LONGEST:
            return 0, pl.ds(0, count * SPAN), (count * (count - 1)) // 2
        begin = span - (LONGEST - 1)
        rows = pl.ds(pl.multiple_of(begin * SPAN, SPAN), LONGEST * SPAN)
        return begin * SPAN, rows, LONGEST * (span - 1)

    def attend(layer, span, half, count):
        rows = half_rows(span, half)
        first_key, keys, base = keys_of(span, count)
        query_pos = (
            span * SPAN + half * part_rows + lax.broadcasted_iota(jnp.int32, (part_rows, 1), 0)
        )
        picture = jnp.full((part_rows, 1), pic_ref[span], jnp.int32) == 1
        limit = jnp.where(picture, span * SPAN + SPAN - 1, query_pos)
        key_pos = first_key + lax.broadcasted_iota(jnp.int32, (1, count * SPAN), 1)
        first = jnp.full((1, count * SPAN), doc_ref[span] * SPAN, jnp.int32)
        key_pos = jnp.where(key_pos >= first, key_pos, BEYOND)
        allowed = key_pos <= limit
        for begin, wide, heads in groups:
            cols = pl.ds(begin, wide)
            q_here = q_all[layer, rows, cols]
            k_here = k_all[layer, keys, cols]
            v_here = v_all[layer, keys, cols]
            total = jnp.zeros((part_rows, wide), F32)
            for head in heads:
                scores = dot_nt(only_head(q_here, begin, head), k_here)
                scores = jnp.where(allowed, scores, -1e30)
                raised = jnp.exp(scores - jnp.max(scores, axis=-1, keepdims=True))
                share = raised * (1.0 / jnp.sum(raised, axis=-1, keepdims=True))
                share = share.astype(BF16)
                for block in range(count):
                    prob[layer, head, base + block, pl.ds(half * part_rows, part_rows), :] = share[
                        :, block * SPAN : (block + 1) * SPAN
                    ]
                total = total + dot_nn(share, only_head(v_here, begin, head))
            att[layer, rows, cols] = total.astype(BF16)

    def attend_back(layer, span, count):
        rows = span_rows(span)
        _, keys, base = keys_of(span, count)
        for begin, wide, heads in groups:
            cols = pl.ds(begin, wide)
            q_here = q_all[layer, rows, cols]
            k_here = k_all[layer, keys, cols]
            v_here = v_all[layer, keys, cols]
            go_here = go[rows, cols]
            mixed = go_here.astype(F32) * att[layer, rows, cols].astype(F32)
            total = jnp.zeros((SPAN, wide), F32)
            key_total = gk[keys, cols]
            value_total = gv[keys, cols]
            for head in heads:
                go_head = only_head(go_here, begin, head)
                inner = jnp.sum(only_head(mixed, begin, head), axis=-1, keepdims=True)
                gp = dot_nt(go_head, v_here)
                share = jnp.concatenate(
                    [prob[layer, head, base + block] for block in range(count)], axis=1
                )
                gs = (share.astype(F32) * (gp - inner)).astype(BF16)
                total = total + dot_nn(gs, only_head(k_here, begin, head))
                key_total = key_total + dot_tn(gs, only_head(q_here, begin, head))
                value_total = value_total + dot_tn(share, go_head)
            gk[keys, cols] = key_total
            gv[keys, cols] = value_total
            gq[rows, cols] = (total * 0.125).astype(BF16)

    def member(pair, which):
        line = (1 - pair) * (1 - row) + pair * row
        return line * 2 + (1 - which) * (1 - col) + which * col

    def project(layer, owner):
        rows = span_rows(owner)
        out = dot_nt(xr[layer, rows, :], wqkv[layer])
        query_bias = vin_ref[layer, pl.ds(7, 1), pl.ds(0, heads_width)]
        value_bias = vin_ref[layer, pl.ds(7, 1), pl.ds(256, heads_width)]
        q_all[layer, rows, :] = (
            (out[:, :heads_width] + query_bias) * 0.125
        ).astype(BF16)
        k_all[layer, rows, :] = out[:, heads_width : 2 * heads_width].astype(BF16)
        v_all[layer, rows, :] = (
            out[:, 2 * heads_width :] + value_bias
        ).astype(BF16)

    def two(buf, first, second, piece):
        return jnp.concatenate(
            (buf[at_rows(first, piece), :], buf[at_rows(second, piece), :]), axis=0
        )

    def ffn_rows(layer, first, second, piece):
        pre = dot_nn(two(hr.at[layer], first, second, piece), wup[layer]) + vec(layer, 6)
        value, grad = gelu_parts(pre)
        value, grad = value.astype(BF16), grad.astype(BF16)
        for place, owner in enumerate((first, second)):
            rows = at_rows(owner, piece)
            act[layer, rows, :] = value[place * chunk : (place + 1) * chunk]
            slope[layer, rows, :] = grad[place * chunk : (place + 1) * chunk]
        out = dot_nn(value, wdown[layer])
        return out[:chunk], out[chunk:]

    def ffn_back_rows(layer, first, second, piece):
        gu = dot_nt(two(gf, first, second, piece), wdown[layer])
        gpre = (gu * two(slope.at[layer], first, second, piece).astype(F32)).astype(BF16)
        for place, owner in enumerate((first, second)):
            slope[layer, at_rows(owner, piece), :] = gpre[place * chunk : (place + 1) * chunk]
        out = dot_nt(gpre, wup[layer])
        return out[:chunk], out[chunk:]

    def ffn_phase(phase, layer, buf, rows_of):
        for piece in range(CHUNKS):
            ag_recv("s", phase, layer, piece, buf).wait_recv()
            own_part, sib_part = rows_of(layer, me, sib, piece)
            rs_sib(phase, layer, piece, sib_part)
            keep[piece] = own_part
        for piece in range(CHUNKS):
            ag_forward(phase, layer, piece, buf)
            ag_recv("f", phase, layer, piece, buf).wait_recv()
            cross_part, diag_part = rows_of(layer, cross, diag, piece)
            rs_diag(phase, layer, piece, diag_part)
            rs_cross(phase, layer, piece, cross_part)
        ag_done(phase, layer, buf)

    def weight_grad(layer, left, right, begin, wide):
        def block(place, carry):
            cols = pl.ds(pl.multiple_of(place * 256, 256), 256)
            grads_ref[layer, cols, pl.ds(begin, wide)] = dot_tn(left[:, cols], right[...]).astype(
                BF16
            )
            return carry

        lax.fori_loop(0, width // 256, block, 0)

    each = width // (NEAR * FAR_SIDE)
    blocks = (
        (0, hidden),
        (hidden, hidden),
        (2 * hidden, OUT_WIDE),
        (2 * hidden + OUT_WIDE, QKV_WIDE),
    )

    def slice_rows(owner):
        return pl.ds(pl.multiple_of(owner * each, each), each)

    def near_copy(layer, block, place):
        begin, wide = blocks[block]
        return remote(
            grads_ref.at[layer, slice_rows(place * NEAR + 1 - near), pl.ds(begin, wide)],
            y_buf.at[layer, place, :, pl.ds(begin, wide)],
            y_s.at[layer, block, place],
            y_r.at[layer, block, place],
            across,
            "dp",
        )

    def far_copy(layer, block, hop):
        begin, wide = blocks[block]
        return remote(
            grads_ref.at[layer, slice_rows(distant[hop]), pl.ds(begin, wide)],
            z_buf.at[layer, hop, :, pl.ds(begin, wide)],
            z_s.at[layer, block, hop],
            z_r.at[layer, block, hop],
            distant[hop],
            "dp",
        )

    def near_send(layer, block):
        if inside:
            for hop in NEAR_ORDER:
                near_copy(layer, block, far if hop is None else distant[hop] // NEAR).start()

    def near_part(layer, block, hop):
        begin, wide = blocks[block]
        cols = pl.ds(begin, wide)
        place = far if hop is None else distant[hop] // NEAR
        near_copy(layer, block, place).wait_recv()
        rows = slice_rows(place * NEAR + near)
        grads_ref[layer, rows, cols] = (
            grads_ref[layer, rows, cols].astype(F32) + y_buf[layer, place, :, cols].astype(F32)
        ).astype(BF16)
        if hop is not None:
            far_copy(layer, block, hop).start()

    def near_add(layer, block):
        if inside:
            for hop in NEAR_ORDER:
                near_part(layer, block, hop)

    staged = []

    def far_add(layer, block):
        begin, wide = blocks[block]
        cols = pl.ds(begin, wide)
        total = grads_ref[layer, slice_rows(share), cols].astype(F32)
        for hop in range(FAR_SIDE - 1):
            far_copy(layer, block, hop).wait_recv()
            total = total + z_buf[layer, hop, :, cols].astype(F32)
        slot = len(staged) % 2
        if len(staged) > 1:
            staged[-2].wait()
        stage[slot, :, pl.ds(0, wide)] = total
        staged.append(
            pltpu.make_async_copy(
                stage.at[slot, :, pl.ds(0, wide)], final_hbm.at[layer, :, cols], f_sem.at[slot]
            )
        )
        staged[-1].start()
        for place in range(FAR_SIDE):
            near_copy(layer, block, place).wait_send()
        for hop in range(FAR_SIDE - 1):
            far_copy(layer, block, hop).wait_send()

    def vec_copies(place, peers, axis):
        copies = []
        for order, peer in enumerate(peers):
            slot = place + order
            copies.append(
                remote(vsend.at[place], vrecv.at[slot], v_s.at[slot], v_r.at[slot], peer, axis)
            )
        return copies, place

    def vec_send(place, peers, axis):
        vsend[place] = vout_ref[...].astype(BF16)
        for copy in vec_copies(place, peers, axis)[0]:
            copy.start()

    def vec_add(pending, whole):
        copies, place = pending
        for order, copy in enumerate(copies):
            copy.wait_recv()
            term = vrecv[place + order].astype(F32)
            if not whole:
                line = lax.broadcasted_iota(jnp.int32, term.shape, 1)
                term = jnp.where(line < 6, term, 0.0)
            vout_ref[...] += term
        for copy in copies:
            copy.wait_send()

    for layer in range(layers):
        vin_ref[layer, 0:4, :] = obias_ref[layer].astype(F32)
        vin_ref[layer, 4:6, :] = gain_ref[layer].astype(F32)
        vin_ref[layer, 6:7, :] = ubias_ref[layer : layer + 1, :].astype(F32)
        for place in range(2):
            vin_ref[layer, 7:8, place * 256 : place * 256 + heads_width] = hbias_ref[
                layer, place : place + 1, :
            ].astype(F32)
    vout_ref[...] = jnp.zeros_like(vout_ref)
    for begin, wide, room in (
        (2 * hidden, heads_width, OUT_WIDE),
        (2 * hidden + OUT_WIDE, 3 * heads_width, QKV_WIDE),
    ):
        blank = (layers, width, room - wide)
        grads_ref[:, :, begin + wide : begin + room] = jnp.zeros(blank, BF16)
    loads[0].wait()
    for piece in range(CHUNKS):
        ag_send(FWD_ATTN, 0, piece, xr.at[0])
    cur[...] = xr[0, own, :].astype(F32)

    def forward(layer, carry):
        here = xr.at[layer]

        @pl.when(layer == 0)
        def _():
            loads[1].wait()

        project(layer, me)
        for piece in range(CHUNKS):
            ag_recv("s", FWD_ATTN, layer, piece, here).wait_recv()
        project(layer, sib)

        @pl.when(layer == 0)
        def _():
            for load in loads[2:]:
                load.wait()

        for piece in range(CHUNKS):
            ag_forward(FWD_ATTN, layer, piece, here)
        project(layer, cross)
        for piece in range(CHUNKS):
            ag_recv("f", FWD_ATTN, layer, piece, here).wait_recv()
        project(layer, diag)

        def heads_out(turn, inner):
            pair, half, which = turn // (2 * HALVES), (turn % (2 * HALVES)) // 2, turn % 2
            owner = member(pair, which)
            by_keys(owner, partial(attend, layer, owner, half))
            out = dot_nn(att[layer, half_rows(owner, half), :], wout[layer])
            for piece in range(CHUNKS // HALVES):
                place_part(
                    FWD_ATTN,
                    layer,
                    pair,
                    which,
                    half * (CHUNKS // HALVES) + piece,
                    out[piece * chunk : (piece + 1) * chunk],
                )
            return inner

        lax.fori_loop(0, 4 * HALVES, heads_out, 0)
        ag_done(FWD_ATTN, layer, here)
        there = hr.at[layer]
        for piece in range(CHUNKS):
            value = cur[part(piece), :] + rs_final(FWD_ATTN, layer, piece) + vec(layer, 0)
            value = norm_forward(layer, piece, value, 4, 1, n_one, r_one)
            mid[part(piece), :] = value
            hr[layer, at_rows(me, piece), :] = value.astype(BF16)
            ag_send(FWD_FFN, layer, piece, there)
        ffn_phase(FWD_FFN, layer, there, ffn_rows)
        for piece in range(CHUNKS):
            value = mid[part(piece), :] + rs_final(FWD_FFN, layer, piece) + vec(layer, 2)
            value = norm_forward(layer, piece, value, 5, 3, n_two, r_two)
            cur[part(piece), :] = value

            @pl.when(layer + 1 == layers)
            def _():
                keep[piece] = value
                result_copy(piece).start()
                begin_back(layer, piece, gf[at_rows(me, piece), :].astype(F32))

            @pl.when(layer + 1 < layers)
            def _():
                xr[layer + 1, at_rows(me, piece), :] = value.astype(BF16)
                ag_send(FWD_ATTN, layer + 1, piece, xr.at[layer + 1])

        return carry

    lax.fori_loop(0, layers, forward, 0)


    def backward(step, carry):
        layer = layers - 1 - step

        @pl.when(step == 0)
        def _():
            for piece in range(CHUNKS):
                result_copy(piece).wait()


        ffn_phase(BWD_FFN, layer, gf, ffn_back_rows)
        weight_grad(layer, gf, act.at[layer], hidden, hidden)
        near_send(layer, DOWN)

        @pl.when(step > 0)
        def _():
            near_add(layer + 1, QKV)

        for piece in range(CHUNKS):
            grad = mid[part(piece), :] + rs_final(BWD_FFN, layer, piece)
            grad = norm_backward(layer, piece, grad, 4, n_one, r_one, (4, 1, 0))
            cur[part(piece), :] = grad
            ga[at_rows(me, piece), :] = grad.astype(BF16)
            ag_send(BWD_ATTN, layer, piece, ga)
        weight_grad(layer, hr.at[layer], slope.at[layer], 0, hidden)
        near_send(layer, UP)
        vout_ref[layer, pl.ds(6, 1), :] = jnp.sum(
            slope[layer].astype(F32), axis=0, keepdims=True
        )
        gk[...] = jnp.zeros_like(gk)
        gv[...] = jnp.zeros_like(gv)

        def heads_grad(turn, inner):
            @pl.when(turn == 1)
            def _():
                for piece in range(CHUNKS):
                    ag_recv("s", BWD_ATTN, layer, piece, ga).wait_recv()

            @pl.when(turn == 2)
            def _():
                for piece in range(CHUNKS):
                    ag_forward(BWD_ATTN, layer, piece, ga)
                    if piece == 0:
                        near_add(layer, DOWN)

            @pl.when(turn == 3)
            def _():
                for piece in range(CHUNKS):
                    ag_recv("f", BWD_ATTN, layer, piece, ga).wait_recv()

            owner = member(1 - turn // 2, 1 - turn % 2)
            rows = span_rows(owner)
            go[rows, :] = dot_nt(ga[rows, :], wout[layer]).astype(BF16)
            by_keys(owner, partial(attend_back, layer, owner))
            return inner

        lax.fori_loop(0, GROUP, heads_grad, 0)

        def rows_back(turn, inner):
            @pl.when(turn == 2)
            def _():
                weight_grad(layer, ga, att.at[layer], 2 * hidden, heads_width)
                near_send(layer, OUT)

            pair, which = turn // 2, turn % 2
            rows = span_rows(member(pair, which))
            joined = jnp.concatenate(
                (gq[rows, :], gk[rows, :].astype(BF16), gv[rows, :].astype(BF16)), axis=1
            )
            gqkv[rows, :] = joined
            out = dot_nn(joined, wqkv[layer])
            for piece in range(CHUNKS):
                place_part(
                    BWD_ATTN, layer, pair, which, piece, out[piece * chunk : (piece + 1) * chunk]
                )
            return inner

        lax.fori_loop(0, GROUP, rows_back, 0)
        ag_done(BWD_ATTN, layer, ga)
        weight_grad(layer, xr.at[layer], gqkv, 2 * hidden + OUT_WIDE, 3 * heads_width)
        near_send(layer, QKV)
        sums = jnp.sum(gqkv[...].astype(F32), axis=0, keepdims=True)
        vout_ref[layer, pl.ds(7, 1), pl.ds(0, heads_width)] = sums[:, :heads_width]
        vout_ref[layer, pl.ds(7, 1), pl.ds(256, heads_width)] = sums[:, 2 * heads_width :]
        if inside:

            @pl.when(step == layers - 1)
            def _():
                vec_send(0, (sib,), "tensor")
                near_add(layer, UP)
                vec_add(vec_copies(0, (sib,), "tensor"), False)
                vec_send(1, (cross,), "tensor")
                near_add(layer, OUT)

            @pl.when(step < layers - 1)
            def _():
                near_add(layer, UP)

        for piece in range(CHUNKS):
            grad = cur[part(piece), :] + rs_final(BWD_ATTN, layer, piece)
            cur[part(piece), :] = grad

            @pl.when(step < layers - 1)
            def _():
                begin_back(layer - 1, piece, grad)
                if piece == 0:
                    near_add(layer, OUT)

        if inside:

            @pl.when(step == layers - 1)
            def _():
                vec_add(vec_copies(1, (cross,), "tensor"), False)
                vec_send(2, (across,), "dp")

        return carry

    lax.fori_loop(0, layers, backward, 0)
    store = pltpu.make_async_copy(cur, tgrad_hbm, w_sem.at[8])
    store.start()
    if inside:
        older = [
            (layer, block)
            for layer in range(layers - 1, 0, -1)
            for block in (DOWN, UP, OUT, QKV)
        ]
        near_part(0, QKV, NEAR_ORDER[0])
        vec_add(vec_copies(2, (across,), "dp"), True)
        vec_send(3, distant, "dp")
        for place, hop in enumerate(NEAR_ORDER[1:]):
            for layer, block in older[place :: FAR_SIDE - 1]:
                far_add(layer, block)
            near_part(0, QKV, hop)
        for block in (DOWN, UP, OUT):
            far_add(0, block)
        vec_add(vec_copies(3, distant, "dp"), True)
        far_add(0, QKV)
        for copy in staged[-2:]:
            copy.wait()
    store.wait()


def finish_kernel(hidden, heads_width, result, tgrad, vout, main, *outs):
    layers, each, _ = main.shape
    fine = each // GROUP
    head_each = heads_width // (NEAR * FAR_SIDE)
    place, mine = lax.axis_index("dp"), lax.axis_index("tensor")
    res_o, tg_o, qkv_o, head_o, out_o, up_o, ubias_o, down_o, obias_o, gain_o = outs
    res_o[...] = result[...]
    tg_o[...] = tgrad[...]

    def shifted(value, begin):
        return pltpu.roll(value, value.shape[1] - begin, 1)

    for layer in range(layers):
        up_o[layer] = main[layer, :, :hidden]
        down_o[layer] = main[layer, :, hidden : 2 * hidden]
        out_o[layer] = main[layer, :, 2 * hidden : 2 * hidden + heads_width].T
        begin = 2 * hidden + OUT_WIDE
        for third in range(3):
            qkv_o[layer, third] = main[
                layer, :, begin + third * heads_width : begin + (third + 1) * heads_width
            ]
        whole = vout[layer]
        picked = shifted(whole, place * each + mine * fine)
        obias_o[layer] = picked[0:4, :fine]
        gain_o[layer] = picked[4:6, :fine]
        ubias_o[layer : layer + 1, :] = shifted(whole, place * each)[6:7, :each]
        picked = shifted(whole, place * head_each)
        head_o[layer, 0:1, :] = picked[7:8, :head_each]
        head_o[layer, 1:2, :] = picked[7:8, 256 : 256 + head_each]


def finish(result, tokens_grad, vout, main, hidden, heads_width):
    layers, each, _ = main.shape
    fine = each // GROUP
    head_each = heads_width // (NEAR * FAR_SIDE)
    shapes = (
        result.shape,
        tokens_grad.shape,
        (layers, 3, each, heads_width),
        (layers, 2, head_each),
        (layers, heads_width, each),
        (layers, each, hidden),
        (layers, each),
        (layers, each, hidden),
        (layers, 4, fine),
        (layers, 2, fine),
    )
    outs = pl.pallas_call(
        partial(finish_kernel, hidden, heads_width),
        name="finish",
        out_shape=tuple(jax.ShapeDtypeStruct(shape, F32) for shape in shapes),
        in_specs=[pl.BlockSpec(memory_space=pltpu.VMEM)] * 4,
        out_specs=tuple(pl.BlockSpec(memory_space=pltpu.VMEM) for _ in shapes),
    )(result, tokens_grad, vout, main)
    return (
        *outs[:2],
        outs[2].transpose(0, 2, 1, 3),
        *outs[3:7],
        outs[7].transpose(0, 2, 1),
        *outs[8:],
    )


def body(
    tokens,
    qkv_weight,
    qv_bias,
    out_weight,
    up_weight,
    up_bias,
    down_weight,
    out_bias,
    norm_gain,
    doc_start,
    picture,
    cotangent,
):
    layers, width, _, heads_width = qkv_weight.shape
    shard = tokens.shape[0]
    seq = shard * GROUP
    hidden = up_weight.shape[2]
    spans = seq // SPAN
    pairs = sum(min(span + 1, LONGEST) for span in range(spans))
    heads = heads_width // HEAD_DIM
    total_width = 2 * hidden + OUT_WIDE + QKV_WIDE
    chunk = shard // CHUNKS
    wide = max(hidden, width)
    vmem = partial(pl.BlockSpec, memory_space=pltpu.VMEM)
    smem = partial(pl.BlockSpec, memory_space=pltpu.SMEM)
    anywhere = partial(pl.BlockSpec, memory_space=pl.ANY)
    sems = pltpu.SemaphoreType.DMA((4, layers, CHUNKS))
    shares = lax.axis_size("dp")
    inside = shares == NEAR * FAR_SIDE
    rows_each = width // shares
    outputs = [
        jax.ShapeDtypeStruct((shard, width), F32),
        jax.ShapeDtypeStruct((shard, width), F32),
        jax.ShapeDtypeStruct((layers, 8, wide), F32),
    ]
    dma = pltpu.SemaphoreType.DMA
    first, last = [], []
    if inside:
        outputs.append(jax.ShapeDtypeStruct((layers, rows_each, total_width), F32))
        first = [pltpu.VMEM((layers, width, total_width), BF16)]
        last = [
            pltpu.VMEM((2, rows_each, hidden), F32),
            dma((2,)),
            pltpu.VMEM((4, layers, 8, wide), BF16),
            pltpu.VMEM((2 + FAR_SIDE, layers, 8, wide), BF16),
            pltpu.VMEM((layers, FAR_SIDE, rows_each, total_width), BF16),
            pltpu.VMEM((layers, FAR_SIDE - 1, rows_each, total_width), BF16),
            dma((layers, 4, FAR_SIDE)),
            dma((layers, 4, FAR_SIDE)),
            dma((layers, 4, FAR_SIDE - 1)),
            dma((layers, 4, FAR_SIDE - 1)),
            dma((2 + FAR_SIDE,)),
            dma((2 + FAR_SIDE,)),
        ]
    else:
        outputs.append(jax.ShapeDtypeStruct((layers, width, total_width), BF16))
    result, tokens_grad, vout, grads = pl.pallas_call(
        partial(step_kernel, inside),
        name="encoder_step",
        out_shape=tuple(outputs),
        in_specs=[anywhere()] * 2 + [vmem()] * 4 + [smem()] * 2 + [anywhere()] * 4,
        out_specs=(anywhere(), anywhere(), vmem(), anywhere() if inside else vmem()),
        scratch_shapes=first
        + [
            pltpu.VMEM((layers, 3 * heads_width, width), BF16),
            pltpu.VMEM(out_weight.shape, BF16),
            pltpu.VMEM(up_weight.shape, BF16),
            pltpu.VMEM(down_weight.shape, BF16),
            pltpu.VMEM((layers, seq, width), BF16),
            pltpu.VMEM((layers, seq, heads_width), BF16),
            pltpu.VMEM((layers, seq, heads_width), BF16),
            pltpu.VMEM((layers, seq, heads_width), BF16),
            pltpu.VMEM((layers, heads, pairs, SPAN, SPAN), BF16),
            pltpu.VMEM((layers, seq, heads_width), BF16),
            pltpu.VMEM((layers, seq, width), BF16),
            pltpu.VMEM((layers, seq, hidden), BF16),
            pltpu.VMEM((layers, seq, hidden), BF16),
            pltpu.VMEM((layers, shard, width), BF16),
            pltpu.VMEM((layers, shard, 1), F32),
            pltpu.VMEM((layers, shard, width), BF16),
            pltpu.VMEM((layers, shard, 1), F32),
            pltpu.VMEM((seq, width), BF16),
            pltpu.VMEM((seq, width), BF16),
            pltpu.VMEM((seq, heads_width), BF16),
            pltpu.VMEM((seq, heads_width), BF16),
            pltpu.VMEM((seq, heads_width), F32),
            pltpu.VMEM((seq, heads_width), F32),
            pltpu.VMEM((seq, 3 * heads_width), BF16),
            pltpu.VMEM((shard, width), F32),
            pltpu.VMEM((shard, width), F32),
        ]
        + [pltpu.VMEM((CHUNKS, chunk, width), BF16)] * 6
        + [pltpu.VMEM((CHUNKS, chunk, width), F32), pltpu.SemaphoreType.DMA((9,))]
        + [sems] * 12
        + last
        + [pltpu.VMEM((layers, 8, wide), F32)],
        compiler_params=pltpu.CompilerParams(
            collective_id=0, has_side_effects=True, vmem_limit_bytes=67043328
        ),
    )(
        tokens,
        cotangent,
        out_bias,
        norm_gain,
        up_bias,
        qv_bias,
        doc_start,
        picture,
        qkv_weight.transpose(0, 2, 3, 1).reshape(layers, 3 * heads_width, width),
        out_weight,
        up_weight,
        down_weight,
    )
    head_each = heads_width // shares
    up_each = hidden // shares
    place = lax.axis_index("dp")
    if inside:
        return finish(result, tokens_grad, vout, grads, hidden, heads_width)
    else:
        main = jnp.stack(
            [
                lax.psum_scatter(grads[layer], "dp", scatter_dimension=0, tiled=True).astype(F32)
                for layer in range(layers)
            ]
        )
        vector_sum = lax.psum(vout[:, :6], ("dp", "tensor"))
        bias_sum = lax.psum(vout[:, 6:], "dp")
    begin = 2 * hidden + OUT_WIDE
    qkv_part = main[:, :, begin : begin + 3 * heads_width].reshape(
        layers, rows_each, 3, heads_width
    )
    out_part = main[:, :, 2 * hidden : 2 * hidden + heads_width].transpose(0, 2, 1)
    up_part = main[:, :, :hidden]
    down_part = main[:, :, hidden : 2 * hidden].transpose(0, 2, 1)
    fine = width // (shares * GROUP)
    vector_sum = lax.dynamic_slice_in_dim(
        vector_sum, place * rows_each + lax.axis_index("tensor") * fine, fine, 2
    )
    head_sum = jnp.stack(
        (bias_sum[:, 1, :heads_width], bias_sum[:, 1, 256 : 256 + heads_width]), axis=1
    )
    return (
        result,
        tokens_grad,
        qkv_part,
        lax.dynamic_slice_in_dim(head_sum, place * head_each, head_each, 2),
        out_part,
        up_part,
        lax.dynamic_slice_in_dim(bias_sum[:, 0, :hidden], place * up_each, up_each, 1),
        down_part,
        vector_sum[:, :4],
        vector_sum[:, 4:],
    )


def solution(mesh):
    return jax.shard_map(
        body,
        mesh=mesh,
        in_specs=(
            P(("dp", "tensor"), None),
            P(None, None, None, "tensor"),
            P(None, None, "tensor"),
            P(None, "tensor", None),
            P(None, None, "tensor"),
            P(None, "tensor"),
            P(None, "tensor", None),
            P(),
            P(),
            P("dp"),
            P("dp"),
            P(("dp", "tensor"), None),
        ),
        out_specs=(
            P(("dp", "tensor"), None),
            P(("dp", "tensor"), None),
            P(None, "dp", None, "tensor"),
            P(None, None, ("tensor", "dp")),
            P(None, "tensor", "dp"),
            P(None, "dp", "tensor"),
            P(None, ("tensor", "dp")),
            P(None, "tensor", "dp"),
            P(None, None, ("dp", "tensor")),
            P(None, None, ("dp", "tensor")),
        ),
        check_vma=False,
    )
```
